32 devices in a mesh: gx: 4 (over y, x), gy: 8 (over z, core).
Axes of the slice: x: 2, y: 2, z: 4, core: 2. Of those that a mesh axis runs over, the one named last changes fastest.
Arguments:
- source: float32 [8, 8, 8, 32, 256], P(None, None, 'gx', 'gy'), may hold values from -6 to 6
- geometry: float32 [3, 8, 32, 32], P(None, 'gx', 'gy'), may hold values from 0.5 to 2
- disc_mask: int32 [8, 32, 32], P('gx', 'gy'), may hold values 0 or 1
- thrust: float32 [8, 32, 32], P('gx', 'gy'), may hold values from 0.5 to 4
- xxt_factor: float32 [6, 32, 65536], P(None, None, ('gx', 'gy')), as said below
- col_count: int32 [6, 32], P(None, ('gx', 'gy')), may hold values from 8 to 32, as said below
Outputs:
- pressure: float32 [8, 8, 8, 32, 256], P(None, None, 'gx', 'gy')
The draws below stay inside these ranges and needn't reach their ends.
Inputs may be any that keep to these rules, and one draw needn't show every extreme that they name: `col_count`: equal on all devices of a level-l group (flat device index along gx+gy agreeing after the lowest l bits are dropped); at every level some group has exactly 32. `xxt_factor`: Real-valued entries of order one or below.
All inputs are finite; a program needn't handle non-finite values. No bound on the sum of `disc_mask` on one device may be relied on, other than what follows from the above.
Results may differ from the reference program's by a relative error of at most 0.00018.
Values sent between devices are 32-bit elements; how exact they have to be, the bound alone decides.
No kernel may reach another device: no remote copies, remote signals or barrier semaphores. Data moves between devices by JAX's collectives and lax.ppermute only.
A program may use at most 128 MiB of HBM per device.

```python
import math
import jax
import jax.numpy as jnp
import numpy as np
from jax import lax

NODES = 8
EX = 2
EY = 4
EZ = 32
CYCLES = 2
CHEB_DEGREE = 2
XCOLS = 32
NEX = 8
NEY = 32
ZN = 256
RANKS = 32
SEP_LEVELS = 6
NC = 2048
COARSE = 65536
N_GX = 4
N_GY = 8


def draw_xxt_factor(key, part):
    full_shape = (SEP_LEVELS, XCOLS, COARSE)
    level_index = jnp.arange(SEP_LEVELS, dtype=jnp.float32)[:, None, None]
    level_scale = 1.4 * (XCOLS * NC * 2.0 ** level_index) ** (-0.25)
    noise_draw = jax.random.normal(key, full_shape, jnp.float32)
    return noise_draw * level_scale


def draw_col_count(key, part):
    level_index = jnp.arange(SEP_LEVELS, dtype=jnp.int32)[:, None]
    device = jnp.arange(RANKS, dtype=jnp.int32)[None, :]
    base_counts = jax.random.randint(key, (SEP_LEVELS, RANKS), XCOLS // 4, XCOLS + 1, dtype=jnp.int32)
    group_index = jnp.right_shift(device, level_index)
    counts = jnp.take_along_axis(base_counts, group_index, axis=1)
    chosen = jax.random.randint(jax.random.fold_in(key, 7), (SEP_LEVELS, 1), 0, RANKS, dtype=jnp.int32)
    counts = jnp.where(group_index == jnp.right_shift(chosen, level_index), XCOLS, counts)
    return counts.astype(jnp.int32)


def plant(entries, stream_key, low, largest):
    shape = entries.shape
    spot = [jax.random.randint(jax.random.fold_in(stream_key, axis), (), 0, shape[axis]) for axis in range(len(shape))]
    entries = entries.at[tuple(spot)].set(low)
    longest = shape.index(max(shape))
    spot[longest] = (spot[longest] + 1) % shape[longest]
    return entries.at[tuple(spot)].set(largest)


def block_scale(key, shape, cuts, low, high):
    level, own = 1.0, jax.random.fold_in(key, 6)
    for dim, parts in cuts:
        heights = jnp.exp(jax.random.uniform(jax.random.fold_in(own, dim), (parts,), jnp.float32, low / len(cuts), high / len(cuts)))
        level = level * jnp.repeat(heights, shape[dim] // parts).reshape([-1 if axis == dim else 1 for axis in range(len(shape))])
    return level


def centred(rng, shape, width, limit, split=(), held_as=jnp.bfloat16):
    entries = width * jax.random.normal(rng, shape, jnp.float32)
    if split:
        entries = entries * block_scale(rng, shape, split, -0.22, 0.18)
    return jnp.clip(entries, -limit, limit).astype(held_as)


def setup_inputs(seed: int = 0) -> dict:
    streams_of = jax.random.split(jax.random.key(seed), 7)
    source = centred(streams_of[0], (NODES, NODES, NEX, NEY, ZN), 1.0, 6.0, ((2, 4), (3, 8)), jnp.float32)
    geometry = jnp.clip(jnp.exp(math.log(2.0) - 1.3862944 * jax.random.uniform(streams_of[1], (3, NEX, NEY, EZ), jnp.float32) ** block_scale(streams_of[1], (3, NEX, NEY, EZ), ((1, 4), (2, 8)), -0.2, 0.2)), 0.5, 2.0)
    disc_mask = plant((jax.random.randint(streams_of[2], (NEX, NEY, EZ), 0, 8) < 1).astype(jnp.int32), jax.random.fold_in(streams_of[2], 1), 0, 1)
    thrust = jnp.clip(jnp.exp(math.log(4.0) - 2.0794415 * jax.random.uniform(streams_of[3], (NEX, NEY, EZ), jnp.float32) ** block_scale(streams_of[3], (NEX, NEY, EZ), ((0, 4), (1, 8)), -0.2, 0.2)), 0.5, 4.0)
    xxt_factor = draw_xxt_factor(jax.random.fold_in(streams_of[6], 71), 0)
    col_count = draw_col_count(jax.random.fold_in(streams_of[6], 71), 0)
    return dict(source=source, geometry=geometry, disc_mask=disc_mask, thrust=thrust, xxt_factor=xxt_factor, col_count=col_count)


highest = lax.Precision.HIGHEST
bound_low = 0.3
bound_high = 3.0
shift_ratio = 0.25

def legendre_table(points, poly_order):
    table = [points * 0.0 + 1.0, points]
    for degree in range(2, poly_order + 1):
        table.append(((2.0 * degree - 1.0) * points * table[-1] - (degree - 1.0) * table[-2]) / degree)
    return table

def jacobi_eigen(matrix):
    size_n = matrix.shape[0]
    current = matrix.copy()
    vectors = np.eye(size_n)
    for sweep_index in range(30):
        for first in range(size_n - 1):
            for second in range(first + 1, size_n):
                angle = 0.5 * math.atan2(2.0 * float(current[first, second]), float(current[second, second] - current[first, first]))
                rotation = np.eye(size_n)
                rotation[first, first] = math.cos(angle)
                rotation[second, second] = math.cos(angle)
                rotation[first, second] = math.sin(angle)
                rotation[second, first] = -math.sin(angle)
                current = rotation.T @ current @ rotation
                vectors = vectors @ rotation
    values = np.array([current[index, index] for index in range(size_n)])
    order = np.argsort(values)
    return (values[order], vectors[:, order])

def gll_tables(node_count):
    poly_order = node_count - 1
    points = np.cos(np.pi * np.arange(node_count) / poly_order)
    for newton_index in range(200):
        table = legendre_table(points, poly_order)
        points = points - (points * table[poly_order] - table[poly_order - 1]) / (node_count * table[poly_order])
    points = points[::-1].copy()
    legendre = legendre_table(points, poly_order)[poly_order]
    weights = 2.0 / (poly_order * (poly_order + 1) * legendre ** 2)
    identity = np.eye(node_count)
    gap_matrix = points[:, None] - points[None, :] + identity
    off_diagonal = legendre[:, None] / (legendre[None, :] * gap_matrix) * (1.0 - identity)
    end_value = poly_order * (poly_order + 1) / 4.0
    end_terms = np.concatenate([[-end_value], np.zeros(node_count - 2), [end_value]])
    derivative = off_diagonal + identity * end_terms[None, :]
    stiffness = derivative.T @ (weights[:, None] * derivative)
    root_inverse = 1.0 / np.sqrt(weights)
    symmetric = root_inverse[:, None] * stiffness * root_inverse[None, :]
    symmetric = 0.5 * (symmetric + symmetric.T)
    eigen_values, eigen_vectors = jacobi_eigen(symmetric)
    eigen_modes = root_inverse[:, None] * eigen_vectors
    vertex_interp = np.stack([(1.0 - points) / 2.0, (1.0 + points) / 2.0], axis=1)
    return (weights.astype(np.float32), stiffness.astype(np.float32), eigen_modes.astype(np.float32), eigen_values.astype(np.float32), vertex_interp.astype(np.float32))

def build_setup(geometry):
    weights, stiffness, eigen_modes, eigen_values, vertex_interp = gll_tables(NODES)
    elem_z = geometry.shape[3]
    z_count = elem_z * NODES
    lengths = jnp.repeat(geometry, NODES, axis=3)
    len_x = lengths[0][None, None]
    len_y = lengths[1][None, None]
    len_z = lengths[2][None, None]
    metric_x = len_y * len_z / (2.0 * len_x)
    metric_y = len_x * len_z / (2.0 * len_y)
    metric_z = len_x * len_y / (2.0 * len_z)
    node_weight = jnp.asarray(weights)
    weight_a = node_weight[:, None, None, None, None]
    weight_b = node_weight[None, :, None, None, None]
    weight_c = jnp.tile(node_weight, elem_z)
    coef_x = metric_x * weight_b * weight_c
    coef_y = metric_y * weight_a * weight_c
    coef_z = metric_z * weight_a * weight_b
    mass_diag = len_x * len_y * len_z / 8.0 * weight_a * weight_b * weight_c
    spectrum = jnp.asarray(eigen_values)
    denominator = metric_x * spectrum[:, None, None, None, None] + metric_y * spectrum[None, :, None, None, None] + metric_z * jnp.tile(spectrum, elem_z) + shift_ratio * (metric_x + metric_y + metric_z)
    inv_denom = 1.0 / denominator
    z_index = jnp.arange(z_count)
    z_node = z_index % NODES
    dirichlet = (z_index < z_count - 1).astype(jnp.float32)
    node_index = jnp.arange(NODES)
    edge_node = ((node_index == 0) | (node_index == NODES - 1)).astype(jnp.float32) + 1.0
    z_shared = 1.0 + ((z_node == 0) & (z_index > 0)).astype(jnp.float32) + ((z_node == NODES - 1) & (z_index < z_count - 1)).astype(jnp.float32)
    inv_mult = 1.0 / (edge_node[:, None, None, None, None] * edge_node[None, :, None, None, None] * z_shared)
    eye_z = jnp.eye(elem_z, dtype=jnp.float32)
    stiff_matrix = jnp.asarray(stiffness)
    mode_matrix = jnp.asarray(eigen_modes)
    interp = jnp.asarray(vertex_interp)
    z_stiff = jnp.kron(eye_z, stiff_matrix.T)
    z_modes = jnp.kron(eye_z, mode_matrix)
    z_modes_t = jnp.kron(eye_z, mode_matrix.T)
    z_restrict = jnp.kron(eye_z, interp)
    z_prolong = jnp.kron(eye_z, interp.T)
    link_up = (z_index[None, :] == z_index[:, None] + 1) & (z_node[:, None] == NODES - 1)
    link_down = (z_index[None, :] == z_index[:, None] - 1) & (z_node[:, None] == 0)
    z_sum = ((z_index[:, None] == z_index[None, :]) | link_up | link_down).astype(jnp.float32)
    return (coef_x, coef_y, coef_z, mass_diag, inv_denom, dirichlet, inv_mult, stiff_matrix, mode_matrix, z_stiff, z_modes, z_modes_t, z_restrict, z_prolong, z_sum, interp)

def pair_sum_x(data_field, prev_high, next_low):
    low_face = data_field[0]
    high_face = data_field[-1]
    before_faces = jnp.concatenate([prev_high[:, None], high_face[:, :-1]], axis=1)
    after_faces = jnp.concatenate([low_face[:, 1:], next_low[:, None]], axis=1)
    return jnp.concatenate([(low_face + before_faces)[None], data_field[1:-1], (high_face + after_faces)[None]], axis=0)

def pair_sum_y(data_field, prev_high, next_low):
    low_face = data_field[:, 0]
    high_face = data_field[:, -1]
    before_faces = jnp.concatenate([prev_high[:, :, None], high_face[:, :, :-1]], axis=2)
    after_faces = jnp.concatenate([low_face[:, :, 1:], next_low[:, :, None]], axis=2)
    return jnp.concatenate([(low_face + before_faces)[:, None], data_field[:, 1:-1], (high_face + after_faces)[:, None]], axis=1)

def assemble_wrap(data_field, z_sum):
    data_field = pair_sum_x(data_field, data_field[-1][:, -1], data_field[0][:, 0])
    data_field = pair_sum_y(data_field, data_field[:, -1][:, :, -1], data_field[:, 0][:, :, 0])
    return jnp.matmul(data_field, z_sum, precision=highest)

def chebyshev(solution, resid, apply_op, precond, keep_resid):
    center = 0.5 * (bound_high + bound_low)
    radius = 0.5 * (bound_high - bound_low)
    center_ratio = center / radius
    rho_old = 1.0 / center_ratio
    direction = precond(resid) / center
    for step_index in range(CHEB_DEGREE):
        solution = solution + direction
        if step_index < CHEB_DEGREE - 1 or keep_resid:
            resid = resid - apply_op(direction)
        if step_index < CHEB_DEGREE - 1:
            rho_new = 1.0 / (2.0 * center_ratio - rho_old)
            direction = rho_new * rho_old * direction + 2.0 * rho_new / radius * precond(resid)
            rho_old = rho_new
    return (solution, resid)

def pressure_solve(source, disc_mask, thrust, setup_tables, assembler, coarse_solve):
    coef_x, coef_y, coef_z, mass_diag, inv_denom, dirichlet, inv_mult, stiff_matrix, mode_matrix, z_stiff, z_modes, z_modes_t, z_restrict, z_prolong, z_sum, interp = setup_tables

    def apply_op(data_field):
        along_x = jnp.einsum('ac,cbxyz->abxyz', stiff_matrix, data_field, precision=highest)
        along_y = jnp.einsum('bc,acxyz->abxyz', stiff_matrix, data_field, precision=highest)
        along_z = jnp.matmul(data_field, z_stiff, precision=highest)
        return dirichlet * assembler(coef_x * along_x + coef_y * along_y + coef_z * along_z, z_sum)

    def precond(resid):
        spectral = jnp.einsum('ai,abxyz->ibxyz', mode_matrix, resid, precision=highest)
        spectral = jnp.einsum('bj,abxyz->ajxyz', mode_matrix, spectral, precision=highest)
        spectral = jnp.matmul(spectral, z_modes, precision=highest) * inv_denom
        spectral = jnp.einsum('ai,ibxyz->abxyz', mode_matrix, spectral, precision=highest)
        spectral = jnp.einsum('bj,ajxyz->abxyz', mode_matrix, spectral, precision=highest)
        return dirichlet * inv_mult * assembler(jnp.matmul(spectral, z_modes_t, precision=highest), z_sum)

    def restrict(resid):
        coarse = jnp.einsum('av,abxyz->vbxyz', interp, inv_mult * resid, precision=highest)
        coarse = jnp.einsum('bu,vbxyz->vuxyz', interp, coarse, precision=highest)
        return jnp.matmul(coarse, z_restrict, precision=highest)

    def prolong(coarse):
        fine_field = jnp.einsum('av,vuxyz->auxyz', interp, coarse, precision=highest)
        fine_field = jnp.einsum('bu,auxyz->abxyz', interp, fine_field, precision=highest)
        return jnp.matmul(fine_field, z_prolong, precision=highest)
    forcing = source + jnp.repeat(disc_mask.astype(jnp.float32) * thrust, NODES, axis=2)[None, None]
    rhs_field = dirichlet * assembler(mass_diag * forcing, z_sum)
    solution = jnp.zeros_like(rhs_field)
    for sweep_index in range(CYCLES):
        if sweep_index == 0:
            resid = rhs_field
        else:
            resid = rhs_field - apply_op(solution)
        solution, resid = chebyshev(solution, resid, apply_op, precond, True)
        correction = coarse_solve(restrict(resid))
        solution = solution + dirichlet * inv_mult * assembler(prolong(correction), z_sum)
        resid = rhs_field - apply_op(solution)
        solution, resid = chebyshev(solution, resid, apply_op, precond, False)
    return solution

def coarse_reference(coarse, xxt_factor, col_count):
    z_pairs = coarse.shape[4]
    split_rows = coarse.reshape(2, 2, N_GX, EX, N_GY, EY, z_pairs)
    by_rank = split_rows.transpose(2, 4, 0, 1, 3, 5, 6).reshape(RANKS, NC)
    blocks = xxt_factor.reshape(SEP_LEVELS, XCOLS, RANKS, NC)
    partial_value = jnp.einsum('lkdn,dn->ldk', blocks, by_rank, precision=highest)
    level_sums = []
    for level_index in range(SEP_LEVELS):
        width_group = 2 ** level_index
        summed = partial_value[level_index].reshape(RANKS // width_group, width_group, XCOLS).sum(axis=1)
        level_sums.append(jnp.repeat(summed, width_group, axis=0))
    totals = jnp.stack(level_sums)
    live_mask = (jnp.arange(XCOLS)[None, None, :] < col_count[:, :, None]).astype(jnp.float32)
    totals = totals * live_mask
    rank_rows = jnp.einsum('lkdn,ldk->dn', blocks, totals, precision=highest)
    return rank_rows.reshape(N_GX, N_GY, 2, 2, EX, EY, z_pairs).transpose(2, 3, 0, 4, 1, 5, 6).reshape(coarse.shape)

def reference(source, geometry, disc_mask, thrust, xxt_factor, col_count):
    setup_tables = build_setup(geometry)

    def coarse_solve(coarse):
        return coarse_reference(coarse, xxt_factor, col_count)
    return pressure_solve(source, disc_mask, thrust, setup_tables, assemble_wrap, coarse_solve)
```

```python
import functools
import math

import jax
import jax.numpy as jnp
import numpy as np
from jax import lax
from jax.experimental import pallas as pl
from jax.experimental.pallas import tpu as pltpu
from jax.sharding import PartitionSpec as P

NODES = 8
CYCLES = 2
CHEB_DEGREE = 2


highest = lax.Precision.HIGHEST
bound_low = 0.3
bound_high = 3.0
shift_ratio = 0.25


def padded(block, sides, width):
    for axis, dim in sides:
        count = lax.axis_size(axis)
        forward = [(i, i + 1) for i in range(count - 1)]
        forward.append((count - 1, 0))
        backward = [(target, source) for source, target in forward]
        low = lax.ppermute(
            lax.slice_in_dim(block, block.shape[dim] - width, None, axis=dim), axis, forward
        )
        high = lax.ppermute(lax.slice_in_dim(block, 0, width, axis=dim), axis, backward)
        block = jnp.concatenate([low, block, high], axis=dim)
    return block


def swapped(x, axis, bit):
    return lax.ppermute(x, axis, [(i, i ^ 1 << bit) for i in range(lax.axis_size(axis))])


def legendre_table(points, poly_order):
    table = [points * 0.0 + 1.0, points]
    for degree in range(2, poly_order + 1):
        table.append(
            ((2.0 * degree - 1.0) * points * table[-1] - (degree - 1.0) * table[-2]) / degree
        )
    return table


def jacobi_eigen(matrix):
    size_n = matrix.shape[0]
    current = matrix.copy()
    vectors = np.eye(size_n)
    for sweep_index in range(30):
        for first in range(size_n - 1):
            for second in range(first + 1, size_n):
                angle = 0.5 * math.atan2(
                    2.0 * float(current[first, second]),
                    float(current[second, second] - current[first, first]),
                )
                rotation = np.eye(size_n)
                rotation[first, first] = math.cos(angle)
                rotation[second, second] = math.cos(angle)
                rotation[first, second] = math.sin(angle)
                rotation[second, first] = -math.sin(angle)
                current = rotation.T @ current @ rotation
                vectors = vectors @ rotation
    values = np.array([current[index, index] for index in range(size_n)])
    order = np.argsort(values)
    return (values[order], vectors[:, order])


def gll_tables(node_count):
    poly_order = node_count - 1
    points = np.cos(np.pi * np.arange(node_count) / poly_order)
    for newton_index in range(200):
        table = legendre_table(points, poly_order)
        points = points - (points * table[poly_order] - table[poly_order - 1]) / (
            node_count * table[poly_order]
        )
    points = points[::-1].copy()
    legendre = legendre_table(points, poly_order)[poly_order]
    weights = 2.0 / (poly_order * (poly_order + 1) * legendre**2)
    identity = np.eye(node_count)
    gap_matrix = points[:, None] - points[None, :] + identity
    off_diagonal = legendre[:, None] / (legendre[None, :] * gap_matrix) * (1.0 - identity)
    end_value = poly_order * (poly_order + 1) / 4.0
    end_terms = np.concatenate([[-end_value], np.zeros(node_count - 2), [end_value]])
    derivative = off_diagonal + identity * end_terms[None, :]
    stiffness = derivative.T @ (weights[:, None] * derivative)
    root_inverse = 1.0 / np.sqrt(weights)
    symmetric = root_inverse[:, None] * stiffness * root_inverse[None, :]
    symmetric = 0.5 * (symmetric + symmetric.T)
    eigen_values, eigen_vectors = jacobi_eigen(symmetric)
    eigen_modes = root_inverse[:, None] * eigen_vectors
    vertex_interp = np.stack([(1.0 - points) / 2.0, (1.0 + points) / 2.0], axis=1)
    return (
        weights.astype(np.float32),
        stiffness.astype(np.float32),
        eigen_modes.astype(np.float32),
        eigen_values.astype(np.float32),
        vertex_interp.astype(np.float32),
    )


def build_setup(geometry):
    weights, stiffness, eigen_modes, eigen_values, vertex_interp = gll_tables(NODES)
    elem_z = geometry.shape[3]
    z_count = elem_z * NODES
    lengths = jnp.repeat(geometry, NODES, axis=3)
    len_x = lengths[0][None, None]
    len_y = lengths[1][None, None]
    len_z = lengths[2][None, None]
    metric_x = len_y * len_z / (2.0 * len_x)
    metric_y = len_x * len_z / (2.0 * len_y)
    metric_z = len_x * len_y / (2.0 * len_z)
    node_weight = jnp.asarray(weights)
    weight_a = node_weight[:, None, None, None, None]
    weight_b = node_weight[None, :, None, None, None]
    weight_c = jnp.tile(node_weight, elem_z)
    coef_x = metric_x * weight_b * weight_c
    coef_y = metric_y * weight_a * weight_c
    coef_z = metric_z * weight_a * weight_b
    mass_diag = len_x * len_y * len_z / 8.0 * weight_a * weight_b * weight_c
    spectrum = jnp.asarray(eigen_values)
    denominator = (
        metric_x * spectrum[:, None, None, None, None]
        + metric_y * spectrum[None, :, None, None, None]
        + metric_z * jnp.tile(spectrum, elem_z)
        + shift_ratio * (metric_x + metric_y + metric_z)
    )
    inv_denom = 1.0 / denominator
    z_index = jnp.arange(z_count)
    z_node = z_index % NODES
    dirichlet = (z_index < z_count - 1).astype(jnp.float32)
    node_index = jnp.arange(NODES)
    edge_node = ((node_index == 0) | (node_index == NODES - 1)).astype(jnp.float32) + 1.0
    z_shared = (
        1.0
        + ((z_node == 0) & (z_index > 0)).astype(jnp.float32)
        + ((z_node == NODES - 1) & (z_index < z_count - 1)).astype(jnp.float32)
    )
    inv_mult = 1.0 / (
        edge_node[:, None, None, None, None] * edge_node[None, :, None, None, None] * z_shared
    )
    eye_z = jnp.eye(elem_z, dtype=jnp.float32)
    stiff_matrix = jnp.asarray(stiffness)
    mode_matrix = jnp.asarray(eigen_modes)
    interp = jnp.asarray(vertex_interp)
    z_stiff = jnp.kron(eye_z, stiff_matrix.T)
    z_modes = jnp.kron(eye_z, mode_matrix)
    z_modes_t = jnp.kron(eye_z, mode_matrix.T)
    z_restrict = jnp.kron(eye_z, interp)
    z_prolong = jnp.kron(eye_z, interp.T)
    link_up = (z_index[None, :] == z_index[:, None] + 1) & (z_node[:, None] == NODES - 1)
    link_down = (z_index[None, :] == z_index[:, None] - 1) & (z_node[:, None] == 0)
    z_sum = ((z_index[:, None] == z_index[None, :]) | link_up | link_down).astype(jnp.float32)
    return (
        coef_x,
        coef_y,
        coef_z,
        mass_diag,
        inv_denom,
        dirichlet,
        inv_mult,
        stiff_matrix,
        mode_matrix,
        z_stiff,
        z_modes,
        z_modes_t,
        z_restrict,
        z_prolong,
        z_sum,
        interp,
    )


def pair_sum_x(data_field, prev_high, next_low):
    low_face = data_field[0]
    high_face = data_field[-1]
    before_faces = jnp.concatenate([prev_high[:, None], high_face[:, :-1]], axis=1)
    after_faces = jnp.concatenate([low_face[:, 1:], next_low[:, None]], axis=1)
    return jnp.concatenate(
        [(low_face + before_faces)[None], data_field[1:-1], (high_face + after_faces)[None]], axis=0
    )


def pair_sum_y(data_field, prev_high, next_low):
    low_face = data_field[:, 0]
    high_face = data_field[:, -1]
    before_faces = jnp.concatenate([prev_high[:, :, None], high_face[:, :, :-1]], axis=2)
    after_faces = jnp.concatenate([low_face[:, :, 1:], next_low[:, :, None]], axis=2)
    return jnp.concatenate(
        [
            (low_face + before_faces)[:, None],
            data_field[:, 1:-1],
            (high_face + after_faces)[:, None],
        ],
        axis=1,
    )


def corner_slot(line_values, node_count):
    padding = jnp.zeros((node_count - 1, line_values.shape[0]), jnp.float32)
    return jnp.concatenate([line_values[None], padding], axis=0)


def summed_neighbour_face(raw_face, prev_line, next_line):
    node_count, elem_x, z_count = raw_face.shape
    shaped = raw_face.reshape(node_count, 1, elem_x, 1, z_count)
    summed = pair_sum_x(shaped, prev_line[None, None], next_line[None, None])
    return summed.reshape(node_count, elem_x, z_count)


def assemble(data_field, z_sum):
    node_count = data_field.shape[0]
    elem_x = data_field.shape[2]
    elem_y = data_field.shape[3]
    z_count = data_field.shape[4]
    frame = jnp.zeros((elem_x + 2, elem_y + 2, node_count, z_count), jnp.float32)
    frame = frame.at[0, 1 : elem_y + 1].set(jnp.transpose(data_field[0][:, 0], (1, 0, 2)))
    frame = frame.at[elem_x + 1, 1 : elem_y + 1].set(
        jnp.transpose(data_field[-1][:, -1], (1, 0, 2))
    )
    frame = frame.at[1 : elem_x + 1, 0].set(jnp.transpose(data_field[:, 0][:, :, 0], (1, 0, 2)))
    frame = frame.at[1 : elem_x + 1, elem_y + 1].set(
        jnp.transpose(data_field[:, -1][:, :, -1], (1, 0, 2))
    )
    frame = frame.at[0, 0].set(corner_slot(data_field[0, 0, 0, 0], node_count))
    frame = frame.at[0, elem_y + 1].set(corner_slot(data_field[0, -1, 0, -1], node_count))
    frame = frame.at[elem_x + 1, 0].set(corner_slot(data_field[-1, 0, -1, 0], node_count))
    frame = frame.at[elem_x + 1, elem_y + 1].set(
        corner_slot(data_field[-1, -1, -1, -1], node_count)
    )
    bordered = padded(frame, (("gx", 0), ("gy", 1)), 1)
    last_x = elem_x + 3
    last_y = elem_y + 3
    left_high = jnp.transpose(bordered[0, 2 : elem_y + 2], (1, 0, 2))
    right_low = jnp.transpose(bordered[last_x, 2 : elem_y + 2], (1, 0, 2))
    down_raw = jnp.transpose(bordered[2 : elem_x + 2, 0], (1, 0, 2))
    up_raw = jnp.transpose(bordered[2 : elem_x + 2, last_y], (1, 0, 2))
    down_high = summed_neighbour_face(down_raw, bordered[0, 0][0], bordered[last_x, 0][0])
    up_low = summed_neighbour_face(up_raw, bordered[0, last_y][0], bordered[last_x, last_y][0])
    data_field = pair_sum_x(data_field, left_high, right_low)
    data_field = pair_sum_y(data_field, down_high, up_low)
    return jnp.matmul(data_field, z_sum, precision=highest)


def chebyshev(solution, resid, apply_op, precond, keep_resid):
    center = 0.5 * (bound_high + bound_low)
    radius = 0.5 * (bound_high - bound_low)
    center_ratio = center / radius
    rho_old = 1.0 / center_ratio
    direction = precond(resid) / center
    for step_index in range(CHEB_DEGREE):
        solution = solution + direction
        if step_index < CHEB_DEGREE - 1 or keep_resid:
            resid = resid - apply_op(direction)
        if step_index < CHEB_DEGREE - 1:
            rho_new = 1.0 / (2.0 * center_ratio - rho_old)
            direction = rho_new * rho_old * direction + 2.0 * rho_new / radius * precond(resid)
            rho_old = rho_new
    return (solution, resid)


def pressure_solve(source, disc_mask, thrust, setup_tables, assembler, coarse_solve):
    (
        coef_x,
        coef_y,
        coef_z,
        mass_diag,
        inv_denom,
        dirichlet,
        inv_mult,
        stiff_matrix,
        mode_matrix,
        z_stiff,
        z_modes,
        z_modes_t,
        z_restrict,
        z_prolong,
        z_sum,
        interp,
    ) = setup_tables

    def apply_op(data_field):
        along_x = jnp.einsum("ac,cbxyz->abxyz", stiff_matrix, data_field, precision=highest)
        along_y = jnp.einsum("bc,acxyz->abxyz", stiff_matrix, data_field, precision=highest)
        along_z = jnp.matmul(data_field, z_stiff, precision=highest)
        return dirichlet * assembler(coef_x * along_x + coef_y * along_y + coef_z * along_z, z_sum)

    def precond(resid):
        spectral = jnp.einsum("ai,abxyz->ibxyz", mode_matrix, resid, precision=highest)
        spectral = jnp.einsum("bj,abxyz->ajxyz", mode_matrix, spectral, precision=highest)
        spectral = jnp.matmul(spectral, z_modes, precision=highest) * inv_denom
        spectral = jnp.einsum("ai,ibxyz->abxyz", mode_matrix, spectral, precision=highest)
        spectral = jnp.einsum("bj,ajxyz->abxyz", mode_matrix, spectral, precision=highest)
        return (
            dirichlet
            * inv_mult
            * assembler(jnp.matmul(spectral, z_modes_t, precision=highest), z_sum)
        )

    forcing = source + jnp.repeat(disc_mask.astype(jnp.float32) * thrust, NODES, axis=2)[None, None]
    rhs_field = dirichlet * assembler(mass_diag * forcing, z_sum)
    solution = jnp.zeros_like(rhs_field)
    for sweep_index in range(CYCLES):
        if sweep_index == 0:
            resid = rhs_field
        else:
            resid = rhs_field - apply_op(solution)
        solution, resid = chebyshev(solution, resid, apply_op, precond, True)
        restrict_coarse = jnp.einsum("av,abxyz->vbxyz", interp, inv_mult * resid, precision=highest)
        restrict_coarse = jnp.einsum("bu,vbxyz->vuxyz", interp, restrict_coarse, precision=highest)
        correction = coarse_solve(jnp.matmul(restrict_coarse, z_restrict, precision=highest))
        fine_field = jnp.einsum("av,vuxyz->auxyz", interp, correction, precision=highest)
        fine_field = jnp.einsum("bu,auxyz->abxyz", interp, fine_field, precision=highest)
        solution = solution + dirichlet * inv_mult * assembler(
            jnp.matmul(fine_field, z_prolong, precision=highest), z_sum
        )
        resid = rhs_field - apply_op(solution)
        solution, resid = chebyshev(solution, resid, apply_op, precond, False)
    return solution


def per_device(source, geometry, disc_mask, thrust, xxt_factor, col_count):
    setup_tables = build_setup(geometry)

    def coarse_solve(coarse):
        flattened = coarse.reshape(-1)
        partial_value = jnp.einsum("lkn,n->lk", xxt_factor, flattened, precision=highest)
        live_mask = (jnp.arange(xxt_factor.shape[1])[None, :] < col_count).astype(jnp.float32)
        partial_value = partial_value * live_mask
        bit_count = (lax.axis_size("gx") * lax.axis_size("gy")).bit_length() - 1
        for bit_index in range(bit_count):
            upper_levels = partial_value[bit_index + 1 :]
            partner = swapped(upper_levels, ("gx", "gy"), bit_index)
            partial_value = jnp.concatenate(
                [partial_value[: bit_index + 1], upper_levels + partner], axis=0
            )
        return jnp.einsum("lkn,lk->n", xxt_factor, partial_value, precision=highest).reshape(
            coarse.shape
        )

    return pressure_solve(source, disc_mask, thrust, setup_tables, assemble, coarse_solve)


VMEM = pltpu.VMEM
SMEM = pltpu.SMEM
f32 = jnp.float32
bf16 = jnp.bfloat16


def device_ring(gx_count, gy_count):
    layers = gy_count // 2
    chips = []
    for z in range(layers):
        pair = [(0, 0), (0, 1)]
        chips += [(y, x, z) for y, x in (pair if z % 2 == 0 else pair[::-1])]
    for k, z in enumerate(reversed(range(layers))):
        pair = [(1, 0), (1, 1)] if layers % 2 == 0 else [(1, 1), (1, 0)]
        chips += [(y, x, z) for y, x in (pair if k % 2 == 0 else pair[::-1])]
    return [(y * 2 + x) * gy_count + z * 2 + core for y, x, z in chips for core in (0, 1)]


def split_bf16(values):
    high = values.astype(np.float32).astype(bf16)
    low = (values - high.astype(np.float64)).astype(np.float32).astype(bf16)
    return high, low


def wide(matrix):
    high, low = split_bf16(matrix)
    return np.concatenate([high, high, low], axis=1)


@functools.lru_cache(maxsize=None)
def constant_tables(ez_count, lanes):
    weights, _, modes, values, interp = [
        np.asarray(t, np.float64) for t in gll_tables(NODES)
    ]
    half = NODES // 2
    root = np.sqrt(weights)
    basis = root[:, None] * modes
    parity = np.sign(np.sum(basis * basis[::-1], axis=0))
    basis = 0.5 * (basis + parity * basis[::-1])
    even = [i for i in range(NODES) if parity[i] > 0]
    odd = [i for i in range(NODES) if parity[i] < 0]
    blocks = []
    for picked in (even, odd):
        blocks.append(np.kron(basis[:half, picked].T, np.kron(basis.T, basis.T)))
    forward = np.stack([wide(m) for m in blocks])
    backward = np.stack([wide(m.T) for m in blocks])
    order_b = even + odd
    one = np.ones(NODES)
    lam_a = np.kron(one, np.kron(values, one))
    lam_b = np.kron(values[order_b], np.kron(one, one))
    lam_c = np.kron(one, np.kron(one, values))
    spectrum = np.stack([lam_a, lam_b, lam_c] + [0 * lam_a] * 5, axis=1)
    root3 = np.kron(root, np.kron(root, root))
    edge = np.where((np.arange(NODES) == 0) | (np.arange(NODES) == NODES - 1), 0.5, 1.0)
    jw = interp * root[:, None] * edge[:, None]
    first = np.zeros_like(jw)
    first[0] = jw[0]
    def rows_of(jc):
        return np.stack(
            [
                np.kron(jw[:, u], np.kron(jw[:, v], jc[:, t]))
                for t in (0, 1) for v in (0, 1) for u in (0, 1)
            ]
        )
    restrict = np.concatenate([rows_of(jw), rows_of(first)], axis=0)
    jp = interp * root[:, None]
    prolong = np.stack(
        [
            np.kron(jp[:, u], np.kron(jp[:, v], jp[:, t]))
            for t in (0, 1) for v in (0, 1) for u in (0, 1)
        ],
        axis=1,
    )
    swap = np.zeros((4 * ez_count, 4 * ez_count))
    for t in range(2):
        for ex in range(2):
            for ez in range(ez_count):
                swap[(t * 2 + ex) * ez_count + ez, ex * 2 * ez_count + 2 * ez + t] = 1.0
    as32 = lambda t: np.asarray(t, np.float32)
    return dict(
        forward=forward,
        backward=backward,
        spectrum=as32(spectrum),
        root3=as32(root3[:, None]),
        inv_root3=as32(1.0 / root3[:, None]),
        restrict=as32(restrict),
        prolong=as32(prolong),
        swap=as32(swap),
        unswap=as32(swap.T),
    )


def hp_dot(a, b):
    return jnp.dot(a, b, precision=highest, preferred_element_type=f32)


def wide_dot(table, field):
    high = field.astype(bf16)
    low = (field - high.astype(f32)).astype(bf16)
    stacked = jnp.concatenate([high, low, high], axis=0)
    return jnp.dot(table, stacked, preferred_element_type=f32)


def spectral_apply(field, forward_ref, backward_ref, scale_ref):
    face = field.shape[0] // NODES
    half = field.shape[0] // 2
    top = field[:half]
    bottom = jnp.concatenate(
        [field[(NODES - 1 - b) * face : (NODES - b) * face] for b in range(NODES // 2)], axis=0
    )
    even = wide_dot(forward_ref[0], top + bottom) * scale_ref[:half]
    odd = wide_dot(forward_ref[1], top - bottom) * scale_ref[half:]
    even = wide_dot(backward_ref[0], even)
    odd = wide_dot(backward_ref[1], odd)
    low_half = even + odd
    diff = even - odd
    parts = [low_half] + [diff[b * face : (b + 1) * face] for b in reversed(range(NODES // 2))]
    return jnp.concatenate(parts, axis=0)


def lane_layer(shape, ez_count):
    return lax.rem(lax.broadcasted_iota(jnp.int32, shape, 1), ez_count)


def lane_halves(ref):
    rows = ref.shape[0] // 2
    return jnp.concatenate([ref[:rows], ref[rows:]], axis=1)


def store_halves(ref, field):
    rows = field.shape[0]
    ref[:rows] = field[:, :128]
    ref[rows:] = field[:, 128:]


def assemble_local(field, out_ref, low_ref, high_ref, ez_count, average):
    rows, lanes = field.shape
    face = rows // NODES
    tile = NODES
    f4 = field.reshape(NODES, NODES, tile, lanes)
    a_low = f4[:, 0].reshape(face, lanes)
    a_high = f4[:, NODES - 1].reshape(face, lanes)
    new_low = a_low + pltpu.roll(a_high, ez_count, 1)
    new_high = a_high + pltpu.roll(a_low, lanes - ez_count, 1)
    if average:
        new_low = 0.5 * new_low
        new_high = 0.5 * new_high
    store_halves(out_ref, field)
    layer = lane_layer((face, 128), ez_count)
    for side in range(2):
        base = side * rows
        span = slice(side * 128, (side + 1) * 128)
        for b in range(NODES):
            at = base + b * face
            out_ref[at : at + tile] = new_low[b * tile : (b + 1) * tile, span]
            out_ref[at + face - tile : at + face] = new_high[b * tile : (b + 1) * tile, span]
        c_low = out_ref[pl.ds(base, face, stride=NODES), :]
        c_high = out_ref[pl.ds(base + NODES - 1, face, stride=NODES), :]
        above = c_low + pltpu.roll(c_high, 1, 1)
        below = c_high + pltpu.roll(c_low, 127, 1)
        if average:
            above = 0.5 * above
            below = 0.5 * below
        out_ref[pl.ds(base, face, stride=NODES), :] = jnp.where(layer > 0, above, c_low)
        out_ref[pl.ds(base + NODES - 1, face, stride=NODES), :] = jnp.where(
            layer < ez_count - 1, below, 0.0
        )
        low_ref[:, span] = out_ref[base : base + face]
        high_ref[:, span] = out_ref[base + rows - face : base + rows]


def joined(w_ref, from_prev_ref, from_next_ref, scale):
    face = from_prev_ref.shape[0]
    rows = w_ref.shape[0] // 2
    field = lane_halves(w_ref)
    low = field[:face] + from_prev_ref[...]
    high = field[rows - face :] + from_next_ref[...]
    if scale != 1.0:
        low = low * scale
        high = high * scale
    return jnp.concatenate([low, field[face : rows - face], high], axis=0)


def entry_kernel(ez_count, *refs):
    (shift_ref, q0, q1, q2, q3, spectrum_ref, root_ref,
     w_ref, low_ref, high_ref, inv_ref, den_ref, live_ref, held) = refs
    rows = w_ref.shape[0] // 2
    face = rows // NODES
    lanes = 2 * w_ref.shape[1]
    parts = 4
    width = lanes // parts
    for q, ref in enumerate((q0, q1, q2, q3)):
        held[lax.rem(shift_ref[0] - q + parts, parts)] = ref[...]
    sizes = jnp.concatenate([held[i, face : face + 8, :width] for i in range(parts)], axis=1)
    len_x, len_y, len_z = sizes[0:1], sizes[1:2], sizes[2:3]
    metric_x = len_y * len_z / (2.0 * len_x)
    metric_y = len_x * len_z / (2.0 * len_y)
    metric_z = len_x * len_y / (2.0 * len_z)
    volume = len_x * len_y * len_z / 8.0
    metrics = jnp.concatenate(
        [metric_x, metric_y, metric_z, jnp.zeros((5, lanes), f32)], axis=0
    )
    stiff = hp_dot(spectrum_ref[...], metrics)
    den_ref[...] = stiff
    inv_ref[...] = 1.0 / (stiff + shift_ratio * (metric_x + metric_y + metric_z))
    for i in range(parts):
        live = held[i, face + 3 : face + 4, : 2 * 128]
        live_ref[2 * i : 2 * i + 1] = live[:, :128]
        live_ref[2 * i + 1 : 2 * i + 2] = live[:, 128:]
    for c in range(NODES):
        for side in range(2):
            w_ref[pl.ds(side * rows + c, face, stride=NODES), :] = jnp.concatenate(
                [held[i, :face, c * width : (c + 1) * width] for i in (2 * side, 2 * side + 1)],
                axis=1,
            )
    forcing = lane_halves(w_ref) * (root_ref[...] * volume)
    assemble_local(forcing, w_ref, low_ref, high_ref, ez_count, False)


def precond_kernel(ez_count, first, *refs):
    if first:
        (w_ref, prev_ref, next_ref, fwd_ref, bwd_ref, inv_ref,
         r_ref, u_ref, low_ref, high_ref) = refs
        resid = joined(w_ref, prev_ref, next_ref, 1.0)
    else:
        (w_ref, prev_ref, next_ref, r_in_ref, fwd_ref, bwd_ref, inv_ref,
         r_ref, u_ref, low_ref, high_ref) = refs
        resid = r_in_ref[...] - joined(w_ref, prev_ref, next_ref, 1.0)
    r_ref[...] = resid
    field = spectral_apply(resid, fwd_ref, bwd_ref, inv_ref)
    assemble_local(field, u_ref, low_ref, high_ref, ez_count, True)


def apply_kernel(ez_count, keep, gain, start, keep_d, *refs):
    refs = list(refs)
    w_ref, prev_ref, next_ref = refs[:3]
    refs = refs[3:]
    step = joined(w_ref, prev_ref, next_ref, 0.5)
    if gain != 1.0:
        step = step * gain
    if keep != 0.0:
        step = step + keep * refs.pop(0)[...]
    total = step if start else refs.pop(0)[...] + step
    fwd_ref, bwd_ref, den_ref = refs[:3]
    refs = refs[3:]
    x_ref, k_ref, low_ref, high_ref = refs[:4]
    x_ref[...] = total
    if keep_d:
        refs[4][...] = step
    field = spectral_apply(step, fwd_ref, bwd_ref, den_ref)
    assemble_local(field, k_ref, low_ref, high_ref, ez_count, False)


def restrict_kernel(ez_count, *refs):
    (shift_ref, w_ref, prev_ref, next_ref, r_in_ref, restrict_ref, swap_ref, x0, x1, x2, x3,
     r_ref, part_ref, coarse, sums) = refs
    lanes = 2 * w_ref.shape[1]
    parts = 4
    width = lanes // parts
    resid = r_in_ref[...] - joined(w_ref, prev_ref, next_ref, 1.0)
    r_ref[...] = resid
    rows = hp_dot(restrict_ref[...], resid)
    b = rows[:8] + jnp.where(lane_layer((8, lanes), ez_count) == 0, rows[8:], 0.0)
    for i in range(parts):
        pair = jnp.concatenate(
            [b[:4, i * width : (i + 1) * width], b[4:, i * width : (i + 1) * width]], axis=1
        )
        coarse[i] = hp_dot(jnp.concatenate([pair, pair], axis=0), swap_ref[...])
    sums[...] = jnp.zeros_like(sums)
    count = x0.shape[0]
    block = 2 * width
    for q, ref in enumerate((x0, x1, x2, x3)):
        i = lax.rem(shift_ref[0] - q + parts, parts)
        mine = coarse[i]
        acc = ref[:, :block] * mine[0:1]
        for vu in range(1, 4):
            acc = acc + ref[:, vu * block : (vu + 1) * block] * mine[vu : vu + 1]
        sums[i, :count] = acc
    flat = sums[...].reshape(parts * sums.shape[1], block)
    ones = jnp.ones((8, block), f32)
    row = lax.dot_general(
        ones, flat, (((1,), (1,)), ((), ())), precision=highest, preferred_element_type=f32
    )
    for i in range(2 * parts):
        part_ref[i : i + 1] = row[0:1, i * 128 : (i + 1) * 128]


def prolong_kernel(ez_count, inner_levels, cols, *refs):
    (shift_ref, all_ref, member_ref, live_ref, unswap_ref, prolong_ref, x0, x1, x2, x3,
     w_ref, low_ref, high_ref, table, coarse) = refs
    lanes = 2 * w_ref.shape[1]
    parts = 4
    width = lanes // parts
    block = 2 * width
    count = x0.shape[0]
    base = all_ref[0] * member_ref[0]
    for source in range(1, all_ref.shape[0]):
        base = base + all_ref[source] * member_ref[source]
    row_id = lax.broadcasted_iota(jnp.int32, base.shape, 0)
    lane_id = lax.broadcasted_iota(jnp.int32, base.shape, 1)
    level = (lax.rem(row_id, 2) * 128 + lane_id) // cols
    total = base
    step = 2
    for bit in range(2):
        flip = jnp.where(
            lax.rem(row_id // step, 2) == 0,
            pltpu.roll(total, 8 - step, 0),
            pltpu.roll(total, step, 0),
        )
        total = jnp.where(level > inner_levels + bit, total + flip, total)
        step *= 2
    total = total * live_ref[...]
    turned = jnp.transpose(total)
    for i in range(parts):
        table[i, :128] = jnp.broadcast_to(turned[:, 2 * i : 2 * i + 1], (128, block))
        table[i, 128:] = jnp.broadcast_to(turned[:, 2 * i + 1 : 2 * i + 2], (128, block))
    for q, ref in enumerate((x0, x1, x2, x3)):
        i = lax.rem(shift_ref[0] - q + parts, parts)
        y = table[i, :count]
        for vu in range(4):
            coarse[i, vu : vu + 1] = jnp.sum(
                ref[:, vu * block : (vu + 1) * block] * y, axis=0, keepdims=True
            )
    lows, highs = [], []
    for i in range(parts):
        pair = hp_dot(coarse[i], unswap_ref[...])
        lows.append(pair[:4, :width])
        highs.append(pair[:4, width:])
    e = jnp.concatenate([jnp.concatenate(lows, axis=1), jnp.concatenate(highs, axis=1)], axis=0)
    field = hp_dot(prolong_ref[...], e)
    assemble_local(field, w_ref, low_ref, high_ref, ez_count, True)


def exit_kernel(keep, gain, *refs):
    (shift_ref, w_ref, prev_ref, next_ref, d_ref, x_ref, inv_root_ref,
     q0, q1, q2, q3, field, held) = refs
    lanes = 2 * w_ref.shape[1]
    parts = 4
    width = lanes // parts
    face = prev_ref.shape[0]
    step = joined(w_ref, prev_ref, next_ref, 0.5) * gain + keep * d_ref[...]
    rows = x_ref.shape[0]
    store_halves(field, (x_ref[...] + step) * inv_root_ref[...])
    for c in range(NODES):
        for side in range(2):
            layer = field[pl.ds(side * rows + c, face, stride=NODES), :]
            for i in range(2):
                held[2 * side + i, :, c * width : (c + 1) * width] = layer[
                    :, i * width : (i + 1) * width
                ]
    for q, ref in enumerate((q0, q1, q2, q3)):
        ref[...] = held[lax.rem(shift_ref[0] - q + parts, parts)]


def call(kernel, name, out_shapes, args, scratch=(), smem_args=0):
    specs = [pl.BlockSpec(memory_space=SMEM)] * smem_args
    specs += [pl.BlockSpec(memory_space=VMEM)] * (len(args) - smem_args)
    return pl.pallas_call(
        kernel,
        name=name,
        out_shape=[jax.ShapeDtypeStruct(s, f32) for s in out_shapes],
        in_specs=specs,
        out_specs=[pl.BlockSpec(memory_space=VMEM)] * len(out_shapes),
        scratch_shapes=list(scratch),
        compiler_params=pltpu.CompilerParams(vmem_limit_bytes=24 * 1024 * 1024),
    )(*args)


def fast_device(source, geometry, disc_mask, thrust, xxt_factor, col_count):
    gx_count, gy_count = lax.axis_size("gx"), lax.axis_size("gy")
    axes = ("gx", "gy")
    nodes, _, elem_x, elem_y, z_count = source.shape
    ez_count = geometry.shape[3]
    levels, cols, _ = xxt_factor.shape
    parts = gx_count
    lanes = parts * elem_x * ez_count
    width = elem_x * ez_count
    rows = nodes**3
    face = nodes * nodes
    devices = gx_count * gy_count
    tables = {k: jnp.asarray(v) for k, v in constant_tables(ez_count, lanes).items()}
    ring = device_ring(gx_count, gy_count)
    place = np.zeros(devices, np.int32)
    for position, device in enumerate(ring):
        place[device] = position
    gx_index, gy_index = lax.axis_index("gx"), lax.axis_index("gy")
    position = jnp.asarray(place)[gx_index * gy_count + gy_index]
    shift = lax.rem(position, parts)
    shift_arr = shift[None].astype(jnp.int32)
    up = [(ring[i], ring[(i + 1) % devices]) for i in range(devices)]
    down = [(target, origin) for origin, target in up]

    def spread(q):
        return [
            (i * gy_count + j, ring[parts * j + (q + i) % parts])
            for i in range(gx_count)
            for j in range(gy_count)
        ]

    def halo(low, high):
        return lax.ppermute(high, axes, up), lax.ppermute(low, axes, down)

    def chunk(stack, q):
        return lax.dynamic_index_in_dim(stack, lax.rem(q + gx_index, parts), 0, keepdims=False)

    force = source + jnp.repeat(disc_mask.astype(f32) * thrust, nodes, axis=2)[None, None]
    force = force.reshape(nodes, nodes, elem_x, elem_y, ez_count, nodes)
    force = force.transpose(3, 1, 0, 5, 2, 4).reshape(elem_y, face, nodes * width)
    sizes = geometry.transpose(2, 0, 1, 3).reshape(elem_y, 3, width)
    sizes = jnp.pad(sizes, ((0, 0), (0, 0), (0, nodes * width - width)))
    live = (jnp.arange(cols)[None, :] < col_count).astype(f32).reshape(1, 1, levels * cols)
    live = jnp.pad(live, ((0, 0), (0, 0), (0, nodes * width - levels * cols)))
    live = jnp.broadcast_to(live, (elem_y, 1, nodes * width))
    packed = jnp.concatenate(
        [force, sizes, live, jnp.zeros((elem_y, 4, nodes * width), f32)], axis=1
    )
    received = [lax.ppermute(chunk(packed, q), axes, spread(q)) for q in range(parts)]

    factor = xxt_factor.reshape(levels * cols, 4 * elem_x, elem_y, 2 * ez_count)
    factor = factor.transpose(2, 0, 1, 3).reshape(elem_y, levels * cols, 8 * width)
    factors = [lax.ppermute(chunk(factor, q), axes, spread(q)) for q in range(parts)]

    inner_levels = gy_count.bit_length() - 1
    level_of = np.minimum(np.arange(256) // cols, 31)
    group_of = place // parts
    member = (
        jnp.right_shift(jnp.asarray(group_of)[:, None], jnp.asarray(level_of)[None])
        == jnp.right_shift(position // parts, jnp.asarray(level_of))[None]
    ) & (np.arange(256) < levels * cols)[None]
    member = jnp.tile(member.astype(f32), (1, parts)).reshape(devices, 2 * parts, 128)

    fshape = (rows, lanes)
    sshape = (2 * rows, lanes // 2)
    hshape = (face, lanes)
    w, low, high, inv, den, live_tile = call(
        functools.partial(entry_kernel, ez_count), "entry",
        [sshape, hshape, hshape, fshape, fshape, (2 * parts, 128)],
        [shift_arr, *received, tables["spectrum"], tables["root3"]],
        [VMEM((parts, face + 8, nodes * width), f32)], 1,
    )
    fwd, bwd = tables["forward"], tables["backward"]

    def precond(w, low, high, resid):
        prev, nxt = halo(low, high)
        args = [w, prev, nxt] + ([] if resid is None else [resid]) + [fwd, bwd, inv]
        return call(
            functools.partial(precond_kernel, ez_count, resid is None), "precond",
            [fshape, sshape, hshape, hshape], args,
        )

    def advance(w, low, high, d, x, keep, gain, keep_d):
        prev, nxt = halo(low, high)
        args = [w, prev, nxt] + ([] if keep == 0.0 else [d]) + ([] if x is None else [x])
        out = call(
            functools.partial(apply_kernel, ez_count, keep, gain, x is None, keep_d), "apply",
            [fshape, sshape, hshape, hshape] + ([fshape] if keep_d else []),
            args + [fwd, bwd, den],
        )
        return out[0], out[1], out[2], out[3], (out[4] if keep_d else None)

    center = 0.5 * (bound_high + bound_low)
    radius = 0.5 * (bound_high - bound_low)
    ratio = center / radius
    rho_old = 1.0 / ratio
    rho_new = 1.0 / (2.0 * ratio - rho_old)
    first_gain = 1.0 / center
    keep = rho_new * rho_old
    gain = 2.0 * rho_new / radius

    x = None
    resid = None
    for cycle in range(CYCLES):
        resid, u, low, high = precond(w, low, high, resid)
        x, k, low, high, d = advance(u, low, high, None, x, 0.0, first_gain, True)
        resid, u, low, high = precond(k, low, high, resid)
        x, k, low, high, _ = advance(u, low, high, d, x, keep, gain, False)
        prev, nxt = halo(low, high)
        resid, partial = call(
            functools.partial(restrict_kernel, ez_count), "restrict",
            [fshape, (2 * parts, 128)],
            [shift_arr, k, prev, nxt, resid, tables["restrict"], tables["swap"], *factors],
            [VMEM((parts, 8, 2 * width), f32), VMEM((parts, 256, 2 * width), f32)], 1,
        )
        everyone = lax.all_to_all(
            jnp.broadcast_to(partial[None], (devices,) + partial.shape), axes, 0, 0
        )
        f, low, high = call(
            functools.partial(prolong_kernel, ez_count, inner_levels, cols), "prolong",
            [sshape, hshape, hshape],
            [shift_arr, everyone, member, live_tile, tables["unswap"], tables["prolong"], *factors],
            [VMEM((parts, 256, 2 * width), f32), VMEM((parts, 8, 2 * width), f32)], 1,
        )
        x, k, low, high, _ = advance(f, low, high, None, x, 0.0, 1.0, False)
        resid, u, low, high = precond(k, low, high, resid)
        x, k, low, high, d = advance(u, low, high, None, x, 0.0, first_gain, True)
        resid, u, low, high = precond(k, low, high, resid)
        if cycle < CYCLES - 1:
            x, w, low, high, _ = advance(u, low, high, d, x, keep, gain, False)
    prev, nxt = halo(low, high)
    chunks = call(
        functools.partial(exit_kernel, keep, gain), "exit",
        [(face, nodes * width)] * parts,
        [shift_arr, u, prev, nxt, d, x, tables["inv_root3"]],
        [VMEM(sshape, f32), VMEM((parts, face, nodes * width), f32)], 1,
    )
    back = [
        lax.ppermute(chunks[q], axes, [(t, s) for s, t in spread(q)]) for q in range(parts)
    ]
    stacked = jnp.stack(back + back)
    start = lax.rem(parts - gx_index, parts)
    by_ey = lax.dynamic_slice_in_dim(stacked, start, parts, 0)
    by_ey = by_ey.reshape(elem_y, nodes, nodes, nodes, elem_x, ez_count)
    return by_ey.transpose(2, 1, 4, 0, 5, 3).reshape(source.shape)


def is_fast(mesh, source, geometry, xxt_factor):
    gx_count, gy_count = mesh.shape["gx"], mesh.shape["gy"]
    nodes, _, elem_x, elem_y, z_count = source.shape
    ez_count = geometry.shape[3]
    levels, cols, _ = xxt_factor.shape
    return (
        gx_count == 4 and elem_y == gx_count and gy_count % 2 == 0 and gy_count >= 4
        and gy_count & (gy_count - 1) == 0 and elem_x == 2 and nodes == NODES
        and 2 * elem_x * ez_count == 128 and levels * cols <= 256
        and 4 * elem_x * ez_count == 256 and levels == (gx_count * gy_count).bit_length() and (levels * cols) % 8 == 0
    )


def solution(mesh):
    def body(source, geometry, disc_mask, thrust, xxt_factor, col_count):
        run = fast_device if is_fast(mesh, source, geometry, xxt_factor) else per_device
        return run(source, geometry, disc_mask, thrust, xxt_factor, col_count)

    return jax.shard_map(
        body,
        mesh=mesh,
        in_specs=(
            P(None, None, "gx", "gy", None),
            P(None, "gx", "gy", None),
            P("gx", "gy", None),
            P("gx", "gy", None),
            P(None, None, ("gx", "gy")),
            P(None, ("gx", "gy")),
        ),
        out_specs=P(None, None, "gx", "gy", None),
        check_vma=False,
    )
```

```python
import functools
import itertools
import math

import jax
import jax.numpy as jnp
import numpy as np
from jax import lax
from jax.experimental import pallas as pl
from jax.experimental.pallas import tpu as pltpu
from jax.sharding import PartitionSpec as P

NODES = 8
CYCLES = 2
CHEB_DEGREE = 2


highest = lax.Precision.HIGHEST
bound_low = 0.3
bound_high = 3.0
shift_ratio = 0.25


def padded(block, sides, width):
    for axis, dim in sides:
        count = lax.axis_size(axis)
        forward = [(i, i + 1) for i in range(count - 1)]
        forward.append((count - 1, 0))
        backward = [(target, source) for source, target in forward]
        low = lax.ppermute(
            lax.slice_in_dim(block, block.shape[dim] - width, None, axis=dim), axis, forward
        )
        high = lax.ppermute(lax.slice_in_dim(block, 0, width, axis=dim), axis, backward)
        block = jnp.concatenate([low, block, high], axis=dim)
    return block


def swapped(x, axis, bit):
    return lax.ppermute(x, axis, [(i, i ^ 1 << bit) for i in range(lax.axis_size(axis))])


def legendre_table(points, poly_order):
    table = [points * 0.0 + 1.0, points]
    for degree in range(2, poly_order + 1):
        table.append(
            ((2.0 * degree - 1.0) * points * table[-1] - (degree - 1.0) * table[-2]) / degree
        )
    return table


def jacobi_eigen(matrix):
    size_n = matrix.shape[0]
    current = matrix.copy()
    vectors = np.eye(size_n)
    for sweep_index in range(30):
        for first in range(size_n - 1):
            for second in range(first + 1, size_n):
                angle = 0.5 * math.atan2(
                    2.0 * float(current[first, second]),
                    float(current[second, second] - current[first, first]),
                )
                rotation = np.eye(size_n)
                rotation[first, first] = math.cos(angle)
                rotation[second, second] = math.cos(angle)
                rotation[first, second] = math.sin(angle)
                rotation[second, first] = -math.sin(angle)
                current = rotation.T @ current @ rotation
                vectors = vectors @ rotation
    values = np.array([current[index, index] for index in range(size_n)])
    order = np.argsort(values)
    return (values[order], vectors[:, order])


def gll_tables(node_count):
    poly_order = node_count - 1
    points = np.cos(np.pi * np.arange(node_count) / poly_order)
    for newton_index in range(200):
        table = legendre_table(points, poly_order)
        points = points - (points * table[poly_order] - table[poly_order - 1]) / (
            node_count * table[poly_order]
        )
    points = points[::-1].copy()
    legendre = legendre_table(points, poly_order)[poly_order]
    weights = 2.0 / (poly_order * (poly_order + 1) * legendre**2)
    identity = np.eye(node_count)
    gap_matrix = points[:, None] - points[None, :] + identity
    off_diagonal = legendre[:, None] / (legendre[None, :] * gap_matrix) * (1.0 - identity)
    end_value = poly_order * (poly_order + 1) / 4.0
    end_terms = np.concatenate([[-end_value], np.zeros(node_count - 2), [end_value]])
    derivative = off_diagonal + identity * end_terms[None, :]
    stiffness = derivative.T @ (weights[:, None] * derivative)
    root_inverse = 1.0 / np.sqrt(weights)
    symmetric = root_inverse[:, None] * stiffness * root_inverse[None, :]
    symmetric = 0.5 * (symmetric + symmetric.T)
    eigen_values, eigen_vectors = jacobi_eigen(symmetric)
    eigen_modes = root_inverse[:, None] * eigen_vectors
    vertex_interp = np.stack([(1.0 - points) / 2.0, (1.0 + points) / 2.0], axis=1)
    return (
        weights.astype(np.float32),
        stiffness.astype(np.float32),
        eigen_modes.astype(np.float32),
        eigen_values.astype(np.float32),
        vertex_interp.astype(np.float32),
    )


def build_setup(geometry):
    weights, stiffness, eigen_modes, eigen_values, vertex_interp = gll_tables(NODES)
    elem_z = geometry.shape[3]
    z_count = elem_z * NODES
    lengths = jnp.repeat(geometry, NODES, axis=3)
    len_x = lengths[0][None, None]
    len_y = lengths[1][None, None]
    len_z = lengths[2][None, None]
    metric_x = len_y * len_z / (2.0 * len_x)
    metric_y = len_x * len_z / (2.0 * len_y)
    metric_z = len_x * len_y / (2.0 * len_z)
    node_weight = jnp.asarray(weights)
    weight_a = node_weight[:, None, None, None, None]
    weight_b = node_weight[None, :, None, None, None]
    weight_c = jnp.tile(node_weight, elem_z)
    coef_x = metric_x * weight_b * weight_c
    coef_y = metric_y * weight_a * weight_c
    coef_z = metric_z * weight_a * weight_b
    mass_diag = len_x * len_y * len_z / 8.0 * weight_a * weight_b * weight_c
    spectrum = jnp.asarray(eigen_values)
    denominator = (
        metric_x * spectrum[:, None, None, None, None]
        + metric_y * spectrum[None, :, None, None, None]
        + metric_z * jnp.tile(spectrum, elem_z)
        + shift_ratio * (metric_x + metric_y + metric_z)
    )
    inv_denom = 1.0 / denominator
    z_index = jnp.arange(z_count)
    z_node = z_index % NODES
    dirichlet = (z_index < z_count - 1).astype(jnp.float32)
    node_index = jnp.arange(NODES)
    edge_node = ((node_index == 0) | (node_index == NODES - 1)).astype(jnp.float32) + 1.0
    z_shared = (
        1.0
        + ((z_node == 0) & (z_index > 0)).astype(jnp.float32)
        + ((z_node == NODES - 1) & (z_index < z_count - 1)).astype(jnp.float32)
    )
    inv_mult = 1.0 / (
        edge_node[:, None, None, None, None] * edge_node[None, :, None, None, None] * z_shared
    )
    eye_z = jnp.eye(elem_z, dtype=jnp.float32)
    stiff_matrix = jnp.asarray(stiffness)
    mode_matrix = jnp.asarray(eigen_modes)
    interp = jnp.asarray(vertex_interp)
    z_stiff = jnp.kron(eye_z, stiff_matrix.T)
    z_modes = jnp.kron(eye_z, mode_matrix)
    z_modes_t = jnp.kron(eye_z, mode_matrix.T)
    z_restrict = jnp.kron(eye_z, interp)
    z_prolong = jnp.kron(eye_z, interp.T)
    link_up = (z_index[None, :] == z_index[:, None] + 1) & (z_node[:, None] == NODES - 1)
    link_down = (z_index[None, :] == z_index[:, None] - 1) & (z_node[:, None] == 0)
    z_sum = ((z_index[:, None] == z_index[None, :]) | link_up | link_down).astype(jnp.float32)
    return (
        coef_x,
        coef_y,
        coef_z,
        mass_diag,
        inv_denom,
        dirichlet,
        inv_mult,
        stiff_matrix,
        mode_matrix,
        z_stiff,
        z_modes,
        z_modes_t,
        z_restrict,
        z_prolong,
        z_sum,
        interp,
    )


def pair_sum_x(data_field, prev_high, next_low):
    low_face = data_field[0]
    high_face = data_field[-1]
    before_faces = jnp.concatenate([prev_high[:, None], high_face[:, :-1]], axis=1)
    after_faces = jnp.concatenate([low_face[:, 1:], next_low[:, None]], axis=1)
    return jnp.concatenate(
        [(low_face + before_faces)[None], data_field[1:-1], (high_face + after_faces)[None]], axis=0
    )


def pair_sum_y(data_field, prev_high, next_low):
    low_face = data_field[:, 0]
    high_face = data_field[:, -1]
    before_faces = jnp.concatenate([prev_high[:, :, None], high_face[:, :, :-1]], axis=2)
    after_faces = jnp.concatenate([low_face[:, :, 1:], next_low[:, :, None]], axis=2)
    return jnp.concatenate(
        [
            (low_face + before_faces)[:, None],
            data_field[:, 1:-1],
            (high_face + after_faces)[:, None],
        ],
        axis=1,
    )


def corner_slot(line_values, node_count):
    padding = jnp.zeros((node_count - 1, line_values.shape[0]), jnp.float32)
    return jnp.concatenate([line_values[None], padding], axis=0)


def summed_neighbour_face(raw_face, prev_line, next_line):
    node_count, elem_x, z_count = raw_face.shape
    shaped = raw_face.reshape(node_count, 1, elem_x, 1, z_count)
    summed = pair_sum_x(shaped, prev_line[None, None], next_line[None, None])
    return summed.reshape(node_count, elem_x, z_count)


def assemble(data_field, z_sum):
    node_count = data_field.shape[0]
    elem_x = data_field.shape[2]
    elem_y = data_field.shape[3]
    z_count = data_field.shape[4]
    frame = jnp.zeros((elem_x + 2, elem_y + 2, node_count, z_count), jnp.float32)
    frame = frame.at[0, 1 : elem_y + 1].set(jnp.transpose(data_field[0][:, 0], (1, 0, 2)))
    frame = frame.at[elem_x + 1, 1 : elem_y + 1].set(
        jnp.transpose(data_field[-1][:, -1], (1, 0, 2))
    )
    frame = frame.at[1 : elem_x + 1, 0].set(jnp.transpose(data_field[:, 0][:, :, 0], (1, 0, 2)))
    frame = frame.at[1 : elem_x + 1, elem_y + 1].set(
        jnp.transpose(data_field[:, -1][:, :, -1], (1, 0, 2))
    )
    frame = frame.at[0, 0].set(corner_slot(data_field[0, 0, 0, 0], node_count))
    frame = frame.at[0, elem_y + 1].set(corner_slot(data_field[0, -1, 0, -1], node_count))
    frame = frame.at[elem_x + 1, 0].set(corner_slot(data_field[-1, 0, -1, 0], node_count))
    frame = frame.at[elem_x + 1, elem_y + 1].set(
        corner_slot(data_field[-1, -1, -1, -1], node_count)
    )
    bordered = padded(frame, (("gx", 0), ("gy", 1)), 1)
    last_x = elem_x + 3
    last_y = elem_y + 3
    left_high = jnp.transpose(bordered[0, 2 : elem_y + 2], (1, 0, 2))
    right_low = jnp.transpose(bordered[last_x, 2 : elem_y + 2], (1, 0, 2))
    down_raw = jnp.transpose(bordered[2 : elem_x + 2, 0], (1, 0, 2))
    up_raw = jnp.transpose(bordered[2 : elem_x + 2, last_y], (1, 0, 2))
    down_high = summed_neighbour_face(down_raw, bordered[0, 0][0], bordered[last_x, 0][0])
    up_low = summed_neighbour_face(up_raw, bordered[0, last_y][0], bordered[last_x, last_y][0])
    data_field = pair_sum_x(data_field, left_high, right_low)
    data_field = pair_sum_y(data_field, down_high, up_low)
    return jnp.matmul(data_field, z_sum, precision=highest)


def chebyshev(solution, resid, apply_op, precond, keep_resid):
    center = 0.5 * (bound_high + bound_low)
    radius = 0.5 * (bound_high - bound_low)
    center_ratio = center / radius
    rho_old = 1.0 / center_ratio
    direction = precond(resid) / center
    for step_index in range(CHEB_DEGREE):
        solution = solution + direction
        if step_index < CHEB_DEGREE - 1 or keep_resid:
            resid = resid - apply_op(direction)
        if step_index < CHEB_DEGREE - 1:
            rho_new = 1.0 / (2.0 * center_ratio - rho_old)
            direction = rho_new * rho_old * direction + 2.0 * rho_new / radius * precond(resid)
            rho_old = rho_new
    return (solution, resid)


def pressure_solve(source, disc_mask, thrust, setup_tables, assembler, coarse_solve):
    (
        coef_x,
        coef_y,
        coef_z,
        mass_diag,
        inv_denom,
        dirichlet,
        inv_mult,
        stiff_matrix,
        mode_matrix,
        z_stiff,
        z_modes,
        z_modes_t,
        z_restrict,
        z_prolong,
        z_sum,
        interp,
    ) = setup_tables

    def apply_op(data_field):
        along_x = jnp.einsum("ac,cbxyz->abxyz", stiff_matrix, data_field, precision=highest)
        along_y = jnp.einsum("bc,acxyz->abxyz", stiff_matrix, data_field, precision=highest)
        along_z = jnp.matmul(data_field, z_stiff, precision=highest)
        return dirichlet * assembler(coef_x * along_x + coef_y * along_y + coef_z * along_z, z_sum)

    def precond(resid):
        spectral = jnp.einsum("ai,abxyz->ibxyz", mode_matrix, resid, precision=highest)
        spectral = jnp.einsum("bj,abxyz->ajxyz", mode_matrix, spectral, precision=highest)
        spectral = jnp.matmul(spectral, z_modes, precision=highest) * inv_denom
        spectral = jnp.einsum("ai,ibxyz->abxyz", mode_matrix, spectral, precision=highest)
        spectral = jnp.einsum("bj,ajxyz->abxyz", mode_matrix, spectral, precision=highest)
        return (
            dirichlet
            * inv_mult
            * assembler(jnp.matmul(spectral, z_modes_t, precision=highest), z_sum)
        )

    forcing = source + jnp.repeat(disc_mask.astype(jnp.float32) * thrust, NODES, axis=2)[None, None]
    rhs_field = dirichlet * assembler(mass_diag * forcing, z_sum)
    solution = jnp.zeros_like(rhs_field)
    for sweep_index in range(CYCLES):
        if sweep_index == 0:
            resid = rhs_field
        else:
            resid = rhs_field - apply_op(solution)
        solution, resid = chebyshev(solution, resid, apply_op, precond, True)
        restrict_coarse = jnp.einsum("av,abxyz->vbxyz", interp, inv_mult * resid, precision=highest)
        restrict_coarse = jnp.einsum("bu,vbxyz->vuxyz", interp, restrict_coarse, precision=highest)
        correction = coarse_solve(jnp.matmul(restrict_coarse, z_restrict, precision=highest))
        fine_field = jnp.einsum("av,vuxyz->auxyz", interp, correction, precision=highest)
        fine_field = jnp.einsum("bu,auxyz->abxyz", interp, fine_field, precision=highest)
        solution = solution + dirichlet * inv_mult * assembler(
            jnp.matmul(fine_field, z_prolong, precision=highest), z_sum
        )
        resid = rhs_field - apply_op(solution)
        solution, resid = chebyshev(solution, resid, apply_op, precond, False)
    return solution


def per_device(source, geometry, disc_mask, thrust, xxt_factor, col_count):
    setup_tables = build_setup(geometry)

    def coarse_solve(coarse):
        flattened = coarse.reshape(-1)
        partial_value = jnp.einsum("lkn,n->lk", xxt_factor, flattened, precision=highest)
        live_mask = (jnp.arange(xxt_factor.shape[1])[None, :] < col_count).astype(jnp.float32)
        partial_value = partial_value * live_mask
        bit_count = (lax.axis_size("gx") * lax.axis_size("gy")).bit_length() - 1
        for bit_index in range(bit_count):
            upper_levels = partial_value[bit_index + 1 :]
            partner = swapped(upper_levels, ("gx", "gy"), bit_index)
            partial_value = jnp.concatenate(
                [partial_value[: bit_index + 1], upper_levels + partner], axis=0
            )
        return jnp.einsum("lkn,lk->n", xxt_factor, partial_value, precision=highest).reshape(
            coarse.shape
        )

    return pressure_solve(source, disc_mask, thrust, setup_tables, assemble, coarse_solve)


VMEM = pltpu.VMEM
SMEM = pltpu.SMEM
f32 = jnp.float32
bf16 = jnp.bfloat16


@functools.lru_cache(maxsize=None)
def placement(gx_count, gy_count):
    layers = gy_count // 2
    a, b, c, d = (0, 0), (0, 1), (1, 1), (1, 0)
    chips = [(d, 0), (a, 0), (b, 0), (c, 0)]
    for z in range(1, layers - 1):
        chips += [(column, z) for column in ((c, b, a) if z % 2 else (a, b, c))]
    chips += [(column, layers - 1) for column in (c, b, a, d)]
    chips += [(d, z) for z in range(layers - 2, 0, -1)]
    count = len(chips)

    def moved(turn):
        return sum(abs(chips[(i + turn) % count][1] - i // gx_count) for i in range(count))

    turn = min(range(count), key=moved)
    chips = chips[turn:] + chips[:turn]
    spots = [(column, z, core) for column, z in chips for core in (0, 1)]
    ring = [(y * 2 + x) * gy_count + 2 * z + core for (y, x), z, core in spots]

    def hops(i, j, place):
        (y, x), z, _ = spots[place]
        return abs(i // 2 - y) + abs(i % 2 - x) + abs(j // 2 - z)

    orders = list(itertools.permutations(range(gx_count)))
    squares = [
        rows
        for rows in itertools.product(orders, repeat=gx_count)
        if all(len(set(column)) == gx_count for column in zip(*rows))
    ]
    send = np.zeros((gx_count * gy_count, gx_count), np.int32)
    part = np.zeros((gx_count * gy_count, gx_count), np.int32)
    group = np.zeros(gx_count * gy_count, np.int32)
    for j in range(gy_count):
        far = [[hops(i, j, gx_count * j + s) for s in range(gx_count)] for i in range(gx_count)]
        cost = lambda rows: [max(far[i][row[i]] for i in range(gx_count)) for row in rows]
        best = min(squares, key=lambda rows: (sum(cost(rows)), cost(rows)))
        for q, row in enumerate(best):
            for i in range(gx_count):
                send[i * gy_count + j, q] = row[i]
                part[ring[gx_count * j + row[i]], q] = i
        for s in range(gx_count):
            group[ring[gx_count * j + s]] = j
    return ring, send, part, group


def split_bf16(values):
    high = values.astype(np.float32).astype(bf16)
    low = (values - high.astype(np.float64)).astype(np.float32).astype(bf16)
    return high, low


def wide(matrix):
    high, low = split_bf16(matrix)
    return np.concatenate([high, high, low], axis=1)


@functools.lru_cache(maxsize=None)
def constant_tables(ez_count, lanes):
    weights, _, modes, values, interp = [
        np.asarray(t, np.float64) for t in gll_tables(NODES)
    ]
    half = NODES // 2
    root = np.sqrt(weights)
    basis = root[:, None] * modes
    parity = np.sign(np.sum(basis * basis[::-1], axis=0))
    basis = 0.5 * (basis + parity * basis[::-1])
    even = [i for i in range(NODES) if parity[i] > 0]
    odd = [i for i in range(NODES) if parity[i] < 0]
    blocks = []
    for picked in (even, odd):
        blocks.append(np.kron(basis[:half, picked].T, np.kron(basis.T, basis.T)))
    forward = np.stack([wide(m) for m in blocks])
    backward = np.stack([wide(m.T) for m in blocks])
    order_b = even + odd
    one = np.ones(NODES)
    lam_a = np.kron(one, np.kron(values, one))
    lam_b = np.kron(values[order_b], np.kron(one, one))
    lam_c = np.kron(one, np.kron(one, values))
    root3 = np.kron(root, np.kron(root, root))
    spectrum = np.stack([lam_a, lam_b, lam_c, root3, 1.0 / root3] + [0 * lam_a] * 3, axis=1)
    edge = np.where((np.arange(NODES) == 0) | (np.arange(NODES) == NODES - 1), 0.5, 1.0)
    jw = interp * root[:, None] * edge[:, None]
    first = np.zeros_like(jw)
    first[0] = jw[0]
    def rows_of(jc):
        return np.stack(
            [
                np.kron(jw[:, u], np.kron(jw[:, v], jc[:, t]))
                for t in (0, 1) for v in (0, 1) for u in (0, 1)
            ]
        )
    restrict = np.concatenate([rows_of(jw), rows_of(first)], axis=0)
    jp = interp * root[:, None]
    prolong = np.stack(
        [
            np.kron(jp[:, u], np.kron(jp[:, v], jp[:, t]))
            for t in (0, 1) for v in (0, 1) for u in (0, 1)
        ],
        axis=1,
    )
    swap = np.zeros((4 * ez_count, 4 * ez_count))
    for t in range(2):
        for ex in range(2):
            for ez in range(ez_count):
                swap[(t * 2 + ex) * ez_count + ez, ex * 2 * ez_count + 2 * ez + t] = 1.0
    span = 2 * ez_count * NODES
    deal = np.zeros((span, span))
    for ex in range(2):
        for ez in range(ez_count):
            for c in range(NODES):
                deal[(ex * ez_count + ez) * NODES + c, (c * 2 + ex) * ez_count + ez] = 1.0
    as32 = lambda t: np.asarray(t, np.float32)
    return dict(
        forward=forward,
        backward=backward,
        columns=as32(np.concatenate([spectrum, prolong], axis=1)),
        restrict=as32(restrict),
        swaps=as32(np.concatenate([swap, swap.T], axis=0)),
        deal=deal.astype(bf16),
        gather=deal.T.astype(bf16),
    )


def hp_dot(a, b):
    return jnp.dot(a, b, precision=highest, preferred_element_type=f32)


def move_lanes(field, table):
    rows = field.shape[0]
    high = field.astype(bf16)
    rest = field - high.astype(f32)
    middle = rest.astype(bf16)
    low = (rest - middle.astype(f32)).astype(bf16)
    moved = jnp.dot(
        jnp.concatenate([high, middle, low], axis=0), table, preferred_element_type=f32
    )
    return moved[:rows] + moved[rows : 2 * rows] + moved[2 * rows :]


def wide_dot(table, field):
    high = field.astype(bf16)
    low = (field - high.astype(f32)).astype(bf16)
    stacked = jnp.concatenate([high, low, high], axis=0)
    return jnp.dot(table, stacked, preferred_element_type=f32)


def spectral_apply(field, forward_ref, backward_ref, scale_ref):
    face = field.shape[0] // NODES
    half = field.shape[0] // 2
    top = field[:half]
    bottom = jnp.concatenate(
        [field[(NODES - 1 - b) * face : (NODES - b) * face] for b in range(NODES // 2)], axis=0
    )
    even = wide_dot(forward_ref[0], top + bottom) * scale_ref[:half]
    odd = wide_dot(forward_ref[1], top - bottom) * scale_ref[half:]
    even = wide_dot(backward_ref[0], even)
    odd = wide_dot(backward_ref[1], odd)
    low_half = even + odd
    diff = even - odd
    parts = [low_half] + [diff[b * face : (b + 1) * face] for b in reversed(range(NODES // 2))]
    return jnp.concatenate(parts, axis=0)


def lane_layer(shape, ez_count):
    return lax.rem(lax.broadcasted_iota(jnp.int32, shape, 1), ez_count)


def lane_halves(ref):
    rows = ref.shape[0] // 2
    return jnp.concatenate([ref[:rows], ref[rows:]], axis=1)


def store_halves(ref, field):
    rows = field.shape[0]
    ref[:rows] = field[:, :128]
    ref[rows:] = field[:, 128:]


def assemble_local(field, out_ref, low_ref, high_ref, ez_count, average):
    rows, lanes = field.shape
    face = rows // NODES
    tile = NODES
    f4 = field.reshape(NODES, NODES, tile, lanes)
    a_low = f4[:, 0].reshape(face, lanes)
    a_high = f4[:, NODES - 1].reshape(face, lanes)
    new_low = a_low + pltpu.roll(a_high, ez_count, 1)
    new_high = a_high + pltpu.roll(a_low, lanes - ez_count, 1)
    if average:
        new_low = 0.5 * new_low
        new_high = 0.5 * new_high
    store_halves(out_ref, field)
    layer = lane_layer((face, 128), ez_count)
    for side in range(2):
        base = side * rows
        span = slice(side * 128, (side + 1) * 128)
        for b in range(NODES):
            at = base + b * face
            out_ref[at : at + tile] = new_low[b * tile : (b + 1) * tile, span]
            out_ref[at + face - tile : at + face] = new_high[b * tile : (b + 1) * tile, span]
        c_low = out_ref[pl.ds(base, face, stride=NODES), :]
        c_high = out_ref[pl.ds(base + NODES - 1, face, stride=NODES), :]
        above = c_low + pltpu.roll(c_high, 1, 1)
        below = c_high + pltpu.roll(c_low, 127, 1)
        if average:
            above = 0.5 * above
            below = 0.5 * below
        out_ref[pl.ds(base, face, stride=NODES), :] = jnp.where(layer > 0, above, c_low)
        out_ref[pl.ds(base + NODES - 1, face, stride=NODES), :] = jnp.where(
            layer < ez_count - 1, below, 0.0
        )
        low_ref[:, span] = out_ref[base : base + face]
        high_ref[:, span] = out_ref[base + rows - face : base + rows]


def joined(w_ref, from_prev_ref, from_next_ref, scale):
    face = from_prev_ref.shape[0]
    rows = w_ref.shape[0] // 2
    field = lane_halves(w_ref)
    low = field[:face] + from_prev_ref[...]
    high = field[rows - face :] + from_next_ref[...]
    if scale != 1.0:
        low = low * scale
        high = high * scale
    return jnp.concatenate([low, field[face : rows - face], high], axis=0)


def pack_kernel(*refs):
    (place_ref, count_ref, source_ref, geometry_ref, disc_ref, thrust_ref, factor_ref,
     q0, q1, q2, q3) = refs
    parts, nodes_rows, lanes = source_ref.shape
    levels = count_ref.shape[0]
    count = factor_ref.shape[0]
    cols = count // levels
    span = factor_ref.shape[1] // (8 * parts)
    lane = lax.broadcasted_iota(jnp.int32, (1, lanes), 1)
    limit = jnp.zeros((1, lanes), jnp.int32)
    for l in range(levels):
        limit = jnp.where(lane // cols == l, count_ref[l, 0], limit)
    live = jnp.where(lax.rem(lane, cols) < limit, 1.0, 0.0).astype(f32)
    push = disc_ref[...].astype(f32) * thrust_ref[...]
    ez_count = push.shape[2]
    blank = jnp.zeros((1, lanes - 2 * ez_count), f32)

    def fill(ref, ey):
        ref[:nodes_rows] = source_ref[ey]
        for c in range(3):
            ref[nodes_rows + c : nodes_rows + c + 1] = jnp.concatenate(
                [geometry_ref[c, ex, ey : ey + 1] for ex in range(2)] + [blank], axis=1
            )
        ref[nodes_rows + 3 : nodes_rows + 4] = jnp.concatenate(
            [push[ex, ey : ey + 1] for ex in range(2)] + [blank], axis=1
        )
        ref[nodes_rows + 4 : nodes_rows + 5] = live
        ref[nodes_rows + 5 : nodes_rows + 8] = jnp.zeros((3, lanes), f32)
        for pair in range(4):
            at = [(2 * pair + k) * parts * span + ey * span for k in range(2)]
            base = nodes_rows + 8 + (pair // 2) * count
            column = (pair % 2) * 2 * span
            ref[base : base + count, column : column + 2 * span] = jnp.concatenate(
                [factor_ref[:, start : start + span] for start in at], axis=1
            )

    for q, ref in enumerate((q0, q1, q2, q3)):
        for ey in range(parts):
            pl.when(place_ref[q] == ey)(functools.partial(fill, ref, ey))


def message_part(base_ref, q):
    return base_ref[4 + q]


def factor_block(ref, count, vu):
    base = ref.shape[0] - 2 * count + (vu // 2) * count
    return ref[base : base + count, (vu % 2) * 128 : (vu % 2) * 128 + 128]


def entry_kernel(ez_count, *refs):
    (place_ref, q0, q1, q2, q3, columns_ref, deal_ref,
     w_ref, low_ref, high_ref, inv_ref, den_ref, live_ref, held) = refs
    rows = w_ref.shape[0] // 2
    face = rows // NODES
    lanes = 2 * w_ref.shape[1]
    parts = 4
    width = lanes // parts
    for q, ref in enumerate((q0, q1, q2, q3)):
        held[message_part(place_ref, q)] = ref[: 2 * face + 8]
    sizes = jnp.concatenate(
        [held[i, 2 * face : 2 * face + 8, :width] for i in range(parts)], axis=1
    )
    len_x, len_y, len_z, push = sizes[0:1], sizes[1:2], sizes[2:3], sizes[3:4]
    metric_x = len_y * len_z / (2.0 * len_x)
    metric_y = len_x * len_z / (2.0 * len_y)
    metric_z = len_x * len_y / (2.0 * len_z)
    volume = len_x * len_y * len_z / 8.0
    metrics = jnp.concatenate(
        [metric_x, metric_y, metric_z, jnp.zeros((5, lanes), f32)], axis=0
    )
    stiff = hp_dot(columns_ref[:, :8], metrics)
    den_ref[...] = stiff
    inv_ref[...] = 1.0 / (stiff + shift_ratio * (metric_x + metric_y + metric_z))
    for i in range(parts):
        live_ref[2 * i : 2 * i + 1] = held[i, 2 * face + 4 : 2 * face + 5, :128]
        live_ref[2 * i + 1 : 2 * i + 2] = held[i, 2 * face + 4 : 2 * face + 5, 128:256]
    raw = jnp.concatenate(
        [
            jnp.concatenate([held[i, :face], held[i, face : 2 * face]], axis=1)
            for i in range(parts)
        ],
        axis=0,
    )
    dealt = move_lanes(raw, deal_ref[...])
    for c in range(NODES):
        for side in range(2):
            w_ref[pl.ds(side * rows + c, face, stride=NODES), :] = jnp.concatenate(
                [
                    dealt[i * face : (i + 1) * face, c * width : (c + 1) * width]
                    for i in (2 * side, 2 * side + 1)
                ],
                axis=1,
            )
    forcing = (lane_halves(w_ref) + push) * (columns_ref[:, 3:4] * volume)
    assemble_local(forcing, w_ref, low_ref, high_ref, ez_count, False)


def precond_kernel(ez_count, first, *refs):
    if first:
        (w_ref, prev_ref, next_ref, fwd_ref, bwd_ref, inv_ref,
         r_ref, u_ref, low_ref, high_ref) = refs
        resid = joined(w_ref, prev_ref, next_ref, 1.0)
    else:
        (w_ref, prev_ref, next_ref, r_in_ref, fwd_ref, bwd_ref, inv_ref,
         r_ref, u_ref, low_ref, high_ref) = refs
        resid = r_in_ref[...] - joined(w_ref, prev_ref, next_ref, 1.0)
    r_ref[...] = resid
    field = spectral_apply(resid, fwd_ref, bwd_ref, inv_ref)
    assemble_local(field, u_ref, low_ref, high_ref, ez_count, True)


def apply_kernel(ez_count, keep, gain, start, keep_d, *refs):
    refs = list(refs)
    w_ref, prev_ref, next_ref = refs[:3]
    refs = refs[3:]
    step = joined(w_ref, prev_ref, next_ref, 0.5)
    if gain != 1.0:
        step = step * gain
    if keep != 0.0:
        step = step + keep * refs.pop(0)[...]
    total = step if start else refs.pop(0)[...] + step
    fwd_ref, bwd_ref, den_ref = refs[:3]
    refs = refs[3:]
    x_ref, k_ref, low_ref, high_ref = refs[:4]
    x_ref[...] = total
    if keep_d:
        refs[4][...] = step
    field = spectral_apply(step, fwd_ref, bwd_ref, den_ref)
    assemble_local(field, k_ref, low_ref, high_ref, ez_count, False)


def restrict_kernel(ez_count, count, *refs):
    (place_ref, w_ref, prev_ref, next_ref, r_in_ref, restrict_ref, swaps_ref, x0, x1, x2, x3,
     r_ref, part_ref, coarse, sums) = refs
    lanes = 2 * w_ref.shape[1]
    parts = 4
    width = lanes // parts
    resid = r_in_ref[...] - joined(w_ref, prev_ref, next_ref, 1.0)
    r_ref[...] = resid
    rows = hp_dot(restrict_ref[...], resid)
    b = rows[:8] + jnp.where(lane_layer((8, lanes), ez_count) == 0, rows[8:], 0.0)
    for i in range(parts):
        pair = jnp.concatenate(
            [b[:4, i * width : (i + 1) * width], b[4:, i * width : (i + 1) * width]], axis=1
        )
        coarse[i] = hp_dot(jnp.concatenate([pair, pair], axis=0), swaps_ref[: 2 * width])
    sums[...] = jnp.zeros_like(sums)
    block = 2 * width
    for q, ref in enumerate((x0, x1, x2, x3)):
        i = message_part(place_ref, q)
        mine = coarse[i]
        acc = factor_block(ref, count, 0) * mine[0:1]
        for vu in range(1, 4):
            acc = acc + factor_block(ref, count, vu) * mine[vu : vu + 1]
        sums[i, :count] = acc
    flat = sums[...].reshape(parts * sums.shape[1], block)
    ones = jnp.ones((8, block), f32)
    row = lax.dot_general(
        ones, flat, (((1,), (1,)), ((), ())), precision=highest, preferred_element_type=f32
    )
    tile = jnp.concatenate(
        [row[0:1, i * 128 : (i + 1) * 128] for i in range(2 * parts)], axis=0
    )
    part_ref[...] = jnp.broadcast_to(tile[None], part_ref.shape)


def prolong_kernel(ez_count, count, inner_levels, cols, groups, *refs):
    (place_ref, all_ref, live_ref, swaps_ref, columns_ref, x0, x1, x2, x3,
     w_ref, low_ref, high_ref, table, coarse) = refs
    lanes = 2 * w_ref.shape[1]
    parts = 4
    width = lanes // parts
    block = 2 * width
    row_id = lax.broadcasted_iota(jnp.int32, all_ref.shape[1:], 0)
    lane_id = lax.broadcasted_iota(jnp.int32, all_ref.shape[1:], 1)
    level = (lax.rem(row_id, 2) * 128 + lane_id) // cols
    mine = lax.shift_right_logical(jnp.full_like(level, place_ref[8]), level)
    base = jnp.zeros(all_ref.shape[1:], f32)
    for source in range(all_ref.shape[0]):
        theirs = lax.shift_right_logical(jnp.full_like(level, groups[source]), level)
        base = base + jnp.where(theirs == mine, all_ref[source], 0.0)
    total = base
    step = 2
    for bit in range(2):
        flip = jnp.where(
            lax.rem(row_id // step, 2) == 0,
            pltpu.roll(total, 8 - step, 0),
            pltpu.roll(total, step, 0),
        )
        total = jnp.where(level > inner_levels + bit, total + flip, total)
        step *= 2
    total = total * live_ref[...]
    turned = jnp.transpose(total)
    for i in range(parts):
        table[i, :128] = jnp.broadcast_to(turned[:, 2 * i : 2 * i + 1], (128, block))
        table[i, 128:] = jnp.broadcast_to(turned[:, 2 * i + 1 : 2 * i + 2], (128, block))
    for q, ref in enumerate((x0, x1, x2, x3)):
        i = message_part(place_ref, q)
        y = table[i, :count]
        for vu in range(4):
            coarse[i, vu : vu + 1] = jnp.sum(
                factor_block(ref, count, vu) * y, axis=0, keepdims=True
            )
    lows, highs = [], []
    for i in range(parts):
        pair = hp_dot(coarse[i], swaps_ref[2 * width :])
        lows.append(pair[:4, :width])
        highs.append(pair[:4, width:])
    e = jnp.concatenate([jnp.concatenate(lows, axis=1), jnp.concatenate(highs, axis=1)], axis=0)
    field = hp_dot(columns_ref[...], jnp.concatenate([jnp.zeros_like(e), e], axis=0))
    assemble_local(field, w_ref, low_ref, high_ref, ez_count, True)


def exit_kernel(keep, gain, *refs):
    (place_ref, w_ref, prev_ref, next_ref, d_ref, x_ref, columns_ref, gather_ref,
     q0, q1, q2, q3, field, held) = refs
    lanes = 2 * w_ref.shape[1]
    parts = 4
    width = lanes // parts
    face = prev_ref.shape[0]
    rows = x_ref.shape[0]
    step = joined(w_ref, prev_ref, next_ref, 0.5) * gain + keep * d_ref[...]
    store_halves(field, (x_ref[...] + step) * columns_ref[:, 4:5])
    blocks = []
    for side in range(2):
        layers = [field[pl.ds(side * rows + c, face, stride=NODES), :] for c in range(NODES)]
        for i in range(2):
            blocks.append(
                jnp.concatenate([t[:, i * width : (i + 1) * width] for t in layers], axis=1)
            )
    dealt = move_lanes(jnp.concatenate(blocks, axis=0), gather_ref[...])
    half = dealt.shape[1] // 2
    for i in range(parts):
        held[i, 0] = dealt[i * face : (i + 1) * face, :half]
        held[i, 1] = dealt[i * face : (i + 1) * face, half:]
    for q, ref in enumerate((q0, q1, q2, q3)):
        ref[...] = held[message_part(place_ref, q)]


def call(kernel, name, out_shapes, args, scratch=(), smem_args=0):
    specs = [pl.BlockSpec(memory_space=SMEM)] * smem_args
    specs += [pl.BlockSpec(memory_space=VMEM)] * (len(args) - smem_args)
    return pl.pallas_call(
        kernel,
        name=name,
        out_shape=[jax.ShapeDtypeStruct(s, f32) for s in out_shapes],
        in_specs=specs,
        out_specs=[pl.BlockSpec(memory_space=VMEM)] * len(out_shapes),
        scratch_shapes=list(scratch),
        compiler_params=pltpu.CompilerParams(vmem_limit_bytes=12 * 1024 * 1024),
    )(*args)


def fast_device(source, geometry, disc_mask, thrust, xxt_factor, col_count):
    gx_count, gy_count = lax.axis_size("gx"), lax.axis_size("gy")
    axes = ("gx", "gy")
    nodes, _, elem_x, elem_y, z_count = source.shape
    ez_count = geometry.shape[3]
    levels, cols, _ = xxt_factor.shape
    parts = gx_count
    lanes = parts * elem_x * ez_count
    width = elem_x * ez_count
    rows = nodes**3
    face = nodes * nodes
    devices = gx_count * gy_count
    tables = {k: jnp.asarray(v) for k, v in constant_tables(ez_count, lanes).items()}
    ring, send, part, group = placement(gx_count, gy_count)
    groups = [int(g) for g in group]
    facts = np.concatenate([send, part, group[:, None], np.argsort(send, axis=1)], axis=1)
    device = lax.axis_index("gx") * gy_count + lax.axis_index("gy")
    place = lax.dynamic_index_in_dim(
        jnp.asarray(facts.astype(np.int32)), device, 0, keepdims=False
    )
    up = [(ring[i], ring[(i + 1) % devices]) for i in range(devices)]
    down = [(target, origin) for origin, target in up]

    def spread(q):
        return [
            (i * gy_count + j, ring[parts * j + int(send[i * gy_count + j, q])])
            for i in range(gx_count)
            for j in range(gy_count)
        ]

    def halo(low, high):
        return lax.ppermute(high, axes, up), lax.ppermute(low, axes, down)

    count = levels * cols
    moved = source.transpose(3, 2, 1, 0, 4).reshape(elem_y, elem_x * face, z_count)
    message = (elem_x * face + 8 + 2 * count, z_count)
    packed = call(
        pack_kernel, "pack", [message] * parts,
        [place, col_count, moved, geometry, disc_mask, thrust,
         xxt_factor.reshape(count, -1)],
        (), 2,
    )
    received = [lax.ppermute(packed[q], axes, spread(q)) for q in range(parts)]
    inner_levels = gy_count.bit_length() - 1

    fshape = (rows, lanes)
    sshape = (2 * rows, lanes // 2)
    hshape = (face, lanes)
    w, low, high, inv, den, live_tile = call(
        functools.partial(entry_kernel, ez_count), "entry",
        [sshape, hshape, hshape, fshape, fshape, (2 * parts, 128)],
        [place, *received, tables["columns"], tables["deal"]],
        [VMEM((parts, 2 * face + 8, z_count), f32)], 1,
    )
    fwd, bwd = tables["forward"], tables["backward"]

    def precond(w, low, high, resid):
        prev, nxt = halo(low, high)
        args = [w, prev, nxt] + ([] if resid is None else [resid]) + [fwd, bwd, inv]
        return call(
            functools.partial(precond_kernel, ez_count, resid is None), "precond",
            [fshape, sshape, hshape, hshape], args,
        )

    def advance(w, low, high, d, x, keep, gain, keep_d):
        prev, nxt = halo(low, high)
        args = [w, prev, nxt] + ([] if keep == 0.0 else [d]) + ([] if x is None else [x])
        out = call(
            functools.partial(apply_kernel, ez_count, keep, gain, x is None, keep_d), "apply",
            [fshape, sshape, hshape, hshape] + ([fshape] if keep_d else []),
            args + [fwd, bwd, den],
        )
        return out[0], out[1], out[2], out[3], (out[4] if keep_d else None)

    center = 0.5 * (bound_high + bound_low)
    radius = 0.5 * (bound_high - bound_low)
    ratio = center / radius
    rho_old = 1.0 / ratio
    rho_new = 1.0 / (2.0 * ratio - rho_old)
    first_gain = 1.0 / center
    keep = rho_new * rho_old
    gain = 2.0 * rho_new / radius

    x = None
    resid = None
    for cycle in range(CYCLES):
        resid, u, low, high = precond(w, low, high, resid)
        x, k, low, high, d = advance(u, low, high, None, x, 0.0, first_gain, True)
        resid, u, low, high = precond(k, low, high, resid)
        x, k, low, high, _ = advance(u, low, high, d, x, keep, gain, False)
        prev, nxt = halo(low, high)
        resid, partial = call(
            functools.partial(restrict_kernel, ez_count, count), "restrict",
            [fshape, (devices, 2 * parts, 128)],
            [place, k, prev, nxt, resid, tables["restrict"], tables["swaps"], *received],
            [VMEM((parts, 8, 2 * width), f32), VMEM((parts, 256, 2 * width), f32)], 1,
        )
        everyone = lax.all_to_all(partial, axes, 0, 0)
        f, low, high = call(
            functools.partial(prolong_kernel, ez_count, count, inner_levels, cols, groups), "prolong",
            [sshape, hshape, hshape],
            [place, everyone, live_tile, tables["swaps"], tables["columns"],
             *received],
            [VMEM((parts, 256, 2 * width), f32), VMEM((parts, 8, 2 * width), f32)], 1,
        )
        x, k, low, high, _ = advance(f, low, high, None, x, 0.0, 1.0, False)
        resid, u, low, high = precond(k, low, high, resid)
        x, k, low, high, d = advance(u, low, high, None, x, 0.0, first_gain, True)
        resid, u, low, high = precond(k, low, high, resid)
        if cycle < CYCLES - 1:
            x, w, low, high, _ = advance(u, low, high, d, x, keep, gain, False)
    prev, nxt = halo(low, high)
    chunks = call(
        functools.partial(exit_kernel, keep, gain), "exit",
        [(2, face, z_count)] * parts,
        [place, u, prev, nxt, d, x, tables["columns"], tables["gather"]],
        [VMEM(sshape, f32), VMEM((parts, 2, face, z_count), f32)], 1,
    )
    back = [
        lax.ppermute(chunks[q], axes, [(t, s) for s, t in spread(q)]) for q in range(parts)
    ]
    stacked = jnp.stack(back)
    by_ey = jnp.stack(
        [
            lax.dynamic_index_in_dim(stacked, place[9 + ey], 0, keepdims=False)
            for ey in range(parts)
        ]
    )
    by_ey = by_ey.reshape(elem_y, elem_x, nodes, nodes, z_count)
    return by_ey.transpose(3, 2, 1, 0, 4)


def is_fast(mesh, source, geometry, xxt_factor):
    gx_count, gy_count = mesh.shape["gx"], mesh.shape["gy"]
    nodes, _, elem_x, elem_y, z_count = source.shape
    ez_count = geometry.shape[3]
    levels, cols, _ = xxt_factor.shape
    return (
        gx_count == 4 and elem_y == gx_count and gy_count % 4 == 0 and gy_count >= 8
        and gy_count & (gy_count - 1) == 0 and elem_x == 2 and nodes == NODES and z_count == 256
        and 2 * elem_x * ez_count == 128 and levels * cols <= 256
        and 4 * elem_x * ez_count == 256 and levels == (gx_count * gy_count).bit_length() and (levels * cols) % 8 == 0
    )


def solution(mesh):
    def body(source, geometry, disc_mask, thrust, xxt_factor, col_count):
        run = fast_device if is_fast(mesh, source, geometry, xxt_factor) else per_device
        return run(source, geometry, disc_mask, thrust, xxt_factor, col_count)

    return jax.shard_map(
        body,
        mesh=mesh,
        in_specs=(
            P(None, None, "gx", "gy", None),
            P(None, "gx", "gy", None),
            P("gx", "gy", None),
            P("gx", "gy", None),
            P(None, None, ("gx", "gy")),
            P(None, ("gx", "gy")),
        ),
        out_specs=P(None, None, "gx", "gy", None),
        check_vma=False,
    )
```

```python
import functools
import itertools
import math

import jax
import jax.numpy as jnp
import numpy as np
from jax import lax
from jax.experimental import pallas as pl
from jax.experimental.pallas import tpu as pltpu
from jax.sharding import PartitionSpec as P

NODES = 8
CYCLES = 2
CHEB_DEGREE = 2


highest = lax.Precision.HIGHEST
bound_low = 0.3
bound_high = 3.0
shift_ratio = 0.25


def padded(block, sides, width):
    for axis, dim in sides:
        count = lax.axis_size(axis)
        forward = [(i, i + 1) for i in range(count - 1)]
        forward.append((count - 1, 0))
        backward = [(target, source) for source, target in forward]
        low = lax.ppermute(
            lax.slice_in_dim(block, block.shape[dim] - width, None, axis=dim), axis, forward
        )
        high = lax.ppermute(lax.slice_in_dim(block, 0, width, axis=dim), axis, backward)
        block = jnp.concatenate([low, block, high], axis=dim)
    return block


def swapped(x, axis, bit):
    return lax.ppermute(x, axis, [(i, i ^ 1 << bit) for i in range(lax.axis_size(axis))])


def legendre_table(points, poly_order):
    table = [points * 0.0 + 1.0, points]
    for degree in range(2, poly_order + 1):
        table.append(
            ((2.0 * degree - 1.0) * points * table[-1] - (degree - 1.0) * table[-2]) / degree
        )
    return table


def jacobi_eigen(matrix):
    size_n = matrix.shape[0]
    current = matrix.copy()
    vectors = np.eye(size_n)
    for sweep_index in range(30):
        for first in range(size_n - 1):
            for second in range(first + 1, size_n):
                angle = 0.5 * math.atan2(
                    2.0 * float(current[first, second]),
                    float(current[second, second] - current[first, first]),
                )
                rotation = np.eye(size_n)
                rotation[first, first] = math.cos(angle)
                rotation[second, second] = math.cos(angle)
                rotation[first, second] = math.sin(angle)
                rotation[second, first] = -math.sin(angle)
                current = rotation.T @ current @ rotation
                vectors = vectors @ rotation
    values = np.array([current[index, index] for index in range(size_n)])
    order = np.argsort(values)
    return (values[order], vectors[:, order])


def gll_tables(node_count):
    poly_order = node_count - 1
    points = np.cos(np.pi * np.arange(node_count) / poly_order)
    for newton_index in range(200):
        table = legendre_table(points, poly_order)
        points = points - (points * table[poly_order] - table[poly_order - 1]) / (
            node_count * table[poly_order]
        )
    points = points[::-1].copy()
    legendre = legendre_table(points, poly_order)[poly_order]
    weights = 2.0 / (poly_order * (poly_order + 1) * legendre**2)
    identity = np.eye(node_count)
    gap_matrix = points[:, None] - points[None, :] + identity
    off_diagonal = legendre[:, None] / (legendre[None, :] * gap_matrix) * (1.0 - identity)
    end_value = poly_order * (poly_order + 1) / 4.0
    end_terms = np.concatenate([[-end_value], np.zeros(node_count - 2), [end_value]])
    derivative = off_diagonal + identity * end_terms[None, :]
    stiffness = derivative.T @ (weights[:, None] * derivative)
    root_inverse = 1.0 / np.sqrt(weights)
    symmetric = root_inverse[:, None] * stiffness * root_inverse[None, :]
    symmetric = 0.5 * (symmetric + symmetric.T)
    eigen_values, eigen_vectors = jacobi_eigen(symmetric)
    eigen_modes = root_inverse[:, None] * eigen_vectors
    vertex_interp = np.stack([(1.0 - points) / 2.0, (1.0 + points) / 2.0], axis=1)
    return (
        weights.astype(np.float32),
        stiffness.astype(np.float32),
        eigen_modes.astype(np.float32),
        eigen_values.astype(np.float32),
        vertex_interp.astype(np.float32),
    )


def build_setup(geometry):
    weights, stiffness, eigen_modes, eigen_values, vertex_interp = gll_tables(NODES)
    elem_z = geometry.shape[3]
    z_count = elem_z * NODES
    lengths = jnp.repeat(geometry, NODES, axis=3)
    len_x = lengths[0][None, None]
    len_y = lengths[1][None, None]
    len_z = lengths[2][None, None]
    metric_x = len_y * len_z / (2.0 * len_x)
    metric_y = len_x * len_z / (2.0 * len_y)
    metric_z = len_x * len_y / (2.0 * len_z)
    node_weight = jnp.asarray(weights)
    weight_a = node_weight[:, None, None, None, None]
    weight_b = node_weight[None, :, None, None, None]
    weight_c = jnp.tile(node_weight, elem_z)
    coef_x = metric_x * weight_b * weight_c
    coef_y = metric_y * weight_a * weight_c
    coef_z = metric_z * weight_a * weight_b
    mass_diag = len_x * len_y * len_z / 8.0 * weight_a * weight_b * weight_c
    spectrum = jnp.asarray(eigen_values)
    denominator = (
        metric_x * spectrum[:, None, None, None, None]
        + metric_y * spectrum[None, :, None, None, None]
        + metric_z * jnp.tile(spectrum, elem_z)
        + shift_ratio * (metric_x + metric_y + metric_z)
    )
    inv_denom = 1.0 / denominator
    z_index = jnp.arange(z_count)
    z_node = z_index % NODES
    dirichlet = (z_index < z_count - 1).astype(jnp.float32)
    node_index = jnp.arange(NODES)
    edge_node = ((node_index == 0) | (node_index == NODES - 1)).astype(jnp.float32) + 1.0
    z_shared = (
        1.0
        + ((z_node == 0) & (z_index > 0)).astype(jnp.float32)
        + ((z_node == NODES - 1) & (z_index < z_count - 1)).astype(jnp.float32)
    )
    inv_mult = 1.0 / (
        edge_node[:, None, None, None, None] * edge_node[None, :, None, None, None] * z_shared
    )
    eye_z = jnp.eye(elem_z, dtype=jnp.float32)
    stiff_matrix = jnp.asarray(stiffness)
    mode_matrix = jnp.asarray(eigen_modes)
    interp = jnp.asarray(vertex_interp)
    z_stiff = jnp.kron(eye_z, stiff_matrix.T)
    z_modes = jnp.kron(eye_z, mode_matrix)
    z_modes_t = jnp.kron(eye_z, mode_matrix.T)
    z_restrict = jnp.kron(eye_z, interp)
    z_prolong = jnp.kron(eye_z, interp.T)
    link_up = (z_index[None, :] == z_index[:, None] + 1) & (z_node[:, None] == NODES - 1)
    link_down = (z_index[None, :] == z_index[:, None] - 1) & (z_node[:, None] == 0)
    z_sum = ((z_index[:, None] == z_index[None, :]) | link_up | link_down).astype(jnp.float32)
    return (
        coef_x,
        coef_y,
        coef_z,
        mass_diag,
        inv_denom,
        dirichlet,
        inv_mult,
        stiff_matrix,
        mode_matrix,
        z_stiff,
        z_modes,
        z_modes_t,
        z_restrict,
        z_prolong,
        z_sum,
        interp,
    )


def pair_sum_x(data_field, prev_high, next_low):
    low_face = data_field[0]
    high_face = data_field[-1]
    before_faces = jnp.concatenate([prev_high[:, None], high_face[:, :-1]], axis=1)
    after_faces = jnp.concatenate([low_face[:, 1:], next_low[:, None]], axis=1)
    return jnp.concatenate(
        [(low_face + before_faces)[None], data_field[1:-1], (high_face + after_faces)[None]], axis=0
    )


def pair_sum_y(data_field, prev_high, next_low):
    low_face = data_field[:, 0]
    high_face = data_field[:, -1]
    before_faces = jnp.concatenate([prev_high[:, :, None], high_face[:, :, :-1]], axis=2)
    after_faces = jnp.concatenate([low_face[:, :, 1:], next_low[:, :, None]], axis=2)
    return jnp.concatenate(
        [
            (low_face + before_faces)[:, None],
            data_field[:, 1:-1],
            (high_face + after_faces)[:, None],
        ],
        axis=1,
    )


def corner_slot(line_values, node_count):
    padding = jnp.zeros((node_count - 1, line_values.shape[0]), jnp.float32)
    return jnp.concatenate([line_values[None], padding], axis=0)


def summed_neighbour_face(raw_face, prev_line, next_line):
    node_count, elem_x, z_count = raw_face.shape
    shaped = raw_face.reshape(node_count, 1, elem_x, 1, z_count)
    summed = pair_sum_x(shaped, prev_line[None, None], next_line[None, None])
    return summed.reshape(node_count, elem_x, z_count)


def assemble(data_field, z_sum):
    node_count = data_field.shape[0]
    elem_x = data_field.shape[2]
    elem_y = data_field.shape[3]
    z_count = data_field.shape[4]
    frame = jnp.zeros((elem_x + 2, elem_y + 2, node_count, z_count), jnp.float32)
    frame = frame.at[0, 1 : elem_y + 1].set(jnp.transpose(data_field[0][:, 0], (1, 0, 2)))
    frame = frame.at[elem_x + 1, 1 : elem_y + 1].set(
        jnp.transpose(data_field[-1][:, -1], (1, 0, 2))
    )
    frame = frame.at[1 : elem_x + 1, 0].set(jnp.transpose(data_field[:, 0][:, :, 0], (1, 0, 2)))
    frame = frame.at[1 : elem_x + 1, elem_y + 1].set(
        jnp.transpose(data_field[:, -1][:, :, -1], (1, 0, 2))
    )
    frame = frame.at[0, 0].set(corner_slot(data_field[0, 0, 0, 0], node_count))
    frame = frame.at[0, elem_y + 1].set(corner_slot(data_field[0, -1, 0, -1], node_count))
    frame = frame.at[elem_x + 1, 0].set(corner_slot(data_field[-1, 0, -1, 0], node_count))
    frame = frame.at[elem_x + 1, elem_y + 1].set(
        corner_slot(data_field[-1, -1, -1, -1], node_count)
    )
    bordered = padded(frame, (("gx", 0), ("gy", 1)), 1)
    last_x = elem_x + 3
    last_y = elem_y + 3
    left_high = jnp.transpose(bordered[0, 2 : elem_y + 2], (1, 0, 2))
    right_low = jnp.transpose(bordered[last_x, 2 : elem_y + 2], (1, 0, 2))
    down_raw = jnp.transpose(bordered[2 : elem_x + 2, 0], (1, 0, 2))
    up_raw = jnp.transpose(bordered[2 : elem_x + 2, last_y], (1, 0, 2))
    down_high = summed_neighbour_face(down_raw, bordered[0, 0][0], bordered[last_x, 0][0])
    up_low = summed_neighbour_face(up_raw, bordered[0, last_y][0], bordered[last_x, last_y][0])
    data_field = pair_sum_x(data_field, left_high, right_low)
    data_field = pair_sum_y(data_field, down_high, up_low)
    return jnp.matmul(data_field, z_sum, precision=highest)


def chebyshev(solution, resid, apply_op, precond, keep_resid):
    center = 0.5 * (bound_high + bound_low)
    radius = 0.5 * (bound_high - bound_low)
    center_ratio = center / radius
    rho_old = 1.0 / center_ratio
    direction = precond(resid) / center
    for step_index in range(CHEB_DEGREE):
        solution = solution + direction
        if step_index < CHEB_DEGREE - 1 or keep_resid:
            resid = resid - apply_op(direction)
        if step_index < CHEB_DEGREE - 1:
            rho_new = 1.0 / (2.0 * center_ratio - rho_old)
            direction = rho_new * rho_old * direction + 2.0 * rho_new / radius * precond(resid)
            rho_old = rho_new
    return (solution, resid)


def pressure_solve(source, disc_mask, thrust, setup_tables, assembler, coarse_solve):
    (
        coef_x,
        coef_y,
        coef_z,
        mass_diag,
        inv_denom,
        dirichlet,
        inv_mult,
        stiff_matrix,
        mode_matrix,
        z_stiff,
        z_modes,
        z_modes_t,
        z_restrict,
        z_prolong,
        z_sum,
        interp,
    ) = setup_tables

    def apply_op(data_field):
        along_x = jnp.einsum("ac,cbxyz->abxyz", stiff_matrix, data_field, precision=highest)
        along_y = jnp.einsum("bc,acxyz->abxyz", stiff_matrix, data_field, precision=highest)
        along_z = jnp.matmul(data_field, z_stiff, precision=highest)
        return dirichlet * assembler(coef_x * along_x + coef_y * along_y + coef_z * along_z, z_sum)

    def precond(resid):
        spectral = jnp.einsum("ai,abxyz->ibxyz", mode_matrix, resid, precision=highest)
        spectral = jnp.einsum("bj,abxyz->ajxyz", mode_matrix, spectral, precision=highest)
        spectral = jnp.matmul(spectral, z_modes, precision=highest) * inv_denom
        spectral = jnp.einsum("ai,ibxyz->abxyz", mode_matrix, spectral, precision=highest)
        spectral = jnp.einsum("bj,ajxyz->abxyz", mode_matrix, spectral, precision=highest)
        return (
            dirichlet
            * inv_mult
            * assembler(jnp.matmul(spectral, z_modes_t, precision=highest), z_sum)
        )

    forcing = source + jnp.repeat(disc_mask.astype(jnp.float32) * thrust, NODES, axis=2)[None, None]
    rhs_field = dirichlet * assembler(mass_diag * forcing, z_sum)
    solution = jnp.zeros_like(rhs_field)
    for sweep_index in range(CYCLES):
        if sweep_index == 0:
            resid = rhs_field
        else:
            resid = rhs_field - apply_op(solution)
        solution, resid = chebyshev(solution, resid, apply_op, precond, True)
        restrict_coarse = jnp.einsum("av,abxyz->vbxyz", interp, inv_mult * resid, precision=highest)
        restrict_coarse = jnp.einsum("bu,vbxyz->vuxyz", interp, restrict_coarse, precision=highest)
        correction = coarse_solve(jnp.matmul(restrict_coarse, z_restrict, precision=highest))
        fine_field = jnp.einsum("av,vuxyz->auxyz", interp, correction, precision=highest)
        fine_field = jnp.einsum("bu,auxyz->abxyz", interp, fine_field, precision=highest)
        solution = solution + dirichlet * inv_mult * assembler(
            jnp.matmul(fine_field, z_prolong, precision=highest), z_sum
        )
        resid = rhs_field - apply_op(solution)
        solution, resid = chebyshev(solution, resid, apply_op, precond, False)
    return solution


def per_device(source, geometry, disc_mask, thrust, xxt_factor, col_count):
    setup_tables = build_setup(geometry)

    def coarse_solve(coarse):
        flattened = coarse.reshape(-1)
        partial_value = jnp.einsum("lkn,n->lk", xxt_factor, flattened, precision=highest)
        live_mask = (jnp.arange(xxt_factor.shape[1])[None, :] < col_count).astype(jnp.float32)
        partial_value = partial_value * live_mask
        bit_count = (lax.axis_size("gx") * lax.axis_size("gy")).bit_length() - 1
        for bit_index in range(bit_count):
            upper_levels = partial_value[bit_index + 1 :]
            partner = swapped(upper_levels, ("gx", "gy"), bit_index)
            partial_value = jnp.concatenate(
                [partial_value[: bit_index + 1], upper_levels + partner], axis=0
            )
        return jnp.einsum("lkn,lk->n", xxt_factor, partial_value, precision=highest).reshape(
            coarse.shape
        )

    return pressure_solve(source, disc_mask, thrust, setup_tables, assemble, coarse_solve)


VMEM = pltpu.VMEM
SMEM = pltpu.SMEM
f32 = jnp.float32
bf16 = jnp.bfloat16


@functools.lru_cache(maxsize=None)
def placement(gx_count, gy_count):
    layers = gy_count // 2
    a, b, c, d = (0, 0), (0, 1), (1, 1), (1, 0)
    chips = [(d, 0), (a, 0), (b, 0), (c, 0)]
    for z in range(1, layers - 1):
        chips += [(column, z) for column in ((c, b, a) if z % 2 else (a, b, c))]
    chips += [(column, layers - 1) for column in (c, b, a, d)]
    chips += [(d, z) for z in range(layers - 2, 0, -1)]
    count = len(chips)

    def moved(turn):
        return sum(abs(chips[(i + turn) % count][1] - i // gx_count) for i in range(count))

    turn = min(range(count), key=moved)
    chips = chips[turn:] + chips[:turn]
    spots = [(column, z, core) for column, z in chips for core in (0, 1)]
    ring = [(y * 2 + x) * gy_count + 2 * z + core for (y, x), z, core in spots]

    def hops(i, j, place):
        (y, x), z, _ = spots[place]
        return abs(i // 2 - y) + abs(i % 2 - x) + abs(j // 2 - z)

    orders = list(itertools.permutations(range(gx_count)))
    squares = [
        rows
        for rows in itertools.product(orders, repeat=gx_count)
        if all(len(set(column)) == gx_count for column in zip(*rows))
    ]
    send = np.zeros((gx_count * gy_count, gx_count), np.int32)
    part = np.zeros((gx_count * gy_count, gx_count), np.int32)
    group = np.zeros(gx_count * gy_count, np.int32)
    for j in range(gy_count):
        far = [[hops(i, j, gx_count * j + s) for s in range(gx_count)] for i in range(gx_count)]
        cost = lambda rows: [max(far[i][row[i]] for i in range(gx_count)) for row in rows]
        best = min(squares, key=lambda rows: (sum(cost(rows)), cost(rows)))
        for q, row in enumerate(best):
            for i in range(gx_count):
                send[i * gy_count + j, q] = row[i]
                part[ring[gx_count * j + row[i]], q] = i
        for s in range(gx_count):
            group[ring[gx_count * j + s]] = j
    codes = group.astype(np.int64) << 24
    for q in range(gx_count):
        codes |= (send[:, q] << 2 * q) | (part[:, q] << 8 + 2 * q)
        codes |= np.argsort(send, axis=1)[:, q] << 16 + 2 * q
    return ring, send, group, [int(c) for c in codes]


def field_of(code, at):
    return lax.shift_right_logical(code, jnp.int32(at)) & 3


def split_bf16(values):
    high = values.astype(np.float32).astype(bf16)
    low = (values - high.astype(np.float64)).astype(np.float32).astype(bf16)
    return high, low


def wide(matrix):
    high, low = split_bf16(matrix)
    return np.concatenate([high, high, low], axis=1)


@functools.lru_cache(maxsize=None)
def constant_tables(ez_count, lanes):
    weights, _, modes, values, interp = [
        np.asarray(t, np.float64) for t in gll_tables(NODES)
    ]
    half = NODES // 2
    root = np.sqrt(weights)
    basis = root[:, None] * modes
    parity = np.sign(np.sum(basis * basis[::-1], axis=0))
    basis = 0.5 * (basis + parity * basis[::-1])
    even = [i for i in range(NODES) if parity[i] > 0]
    odd = [i for i in range(NODES) if parity[i] < 0]
    blocks = []
    for picked in (even, odd):
        blocks.append(np.kron(basis[:half, picked].T, np.kron(basis.T, basis.T)))
    forward = np.stack([wide(m) for m in blocks])
    backward = np.stack([wide(m.T) for m in blocks])
    order_b = even + odd
    one = np.ones(NODES)
    lam_a = np.kron(one, np.kron(values, one))
    lam_b = np.kron(values[order_b], np.kron(one, one))
    lam_c = np.kron(one, np.kron(one, values))
    root3 = np.kron(root, np.kron(root, root))
    spectrum = np.stack([lam_a, lam_b, lam_c, root3, 1.0 / root3] + [0 * lam_a] * 3, axis=1)
    edge = np.where((np.arange(NODES) == 0) | (np.arange(NODES) == NODES - 1), 0.5, 1.0)
    jw = interp * root[:, None] * edge[:, None]
    first = np.zeros_like(jw)
    first[0] = jw[0]
    def rows_of(jc):
        return np.stack(
            [
                np.kron(jw[:, u], np.kron(jw[:, v], jc[:, t]))
                for t in (0, 1) for v in (0, 1) for u in (0, 1)
            ]
        )
    restrict = np.concatenate([rows_of(jw), rows_of(first)], axis=0)
    jp = interp * root[:, None]
    prolong = np.stack(
        [
            np.kron(jp[:, u], np.kron(jp[:, v], jp[:, t]))
            for t in (0, 1) for v in (0, 1) for u in (0, 1)
        ],
        axis=1,
    )
    swap = np.zeros((4 * ez_count, 4 * ez_count))
    for t in range(2):
        for ex in range(2):
            for ez in range(ez_count):
                swap[(t * 2 + ex) * ez_count + ez, ex * 2 * ez_count + 2 * ez + t] = 1.0
    span = 2 * ez_count * NODES
    deal = np.zeros((span, span))
    for ex in range(2):
        for ez in range(ez_count):
            for c in range(NODES):
                deal[(ex * ez_count + ez) * NODES + c, (c * 2 + ex) * ez_count + ez] = 1.0
    as32 = lambda t: np.asarray(t, np.float32)
    return dict(
        forward=forward,
        backward=backward,
        columns=as32(np.concatenate([spectrum, prolong], axis=1)),
        restrict=as32(restrict),
        swaps=as32(np.concatenate([swap, swap.T], axis=0)),
        deal=deal.astype(bf16),
        gather=deal.T.astype(bf16),
    )


def hp_dot(a, b):
    return jnp.dot(a, b, precision=highest, preferred_element_type=f32)


def move_lanes(field, table):
    rows = field.shape[0]
    high = field.astype(bf16)
    rest = field - high.astype(f32)
    middle = rest.astype(bf16)
    low = (rest - middle.astype(f32)).astype(bf16)
    moved = jnp.dot(
        jnp.concatenate([high, middle, low], axis=0), table, preferred_element_type=f32
    )
    return moved[:rows] + moved[rows : 2 * rows] + moved[2 * rows :]


def wide_dot(table, field):
    high = field.astype(bf16)
    low = (field - high.astype(f32)).astype(bf16)
    stacked = jnp.concatenate([high, low, high], axis=0)
    return jnp.dot(table, stacked, preferred_element_type=f32)


def spectral_apply(field, forward_ref, backward_ref, scale_ref):
    face = field.shape[0] // NODES
    half = field.shape[0] // 2
    top = field[:half]
    bottom = jnp.concatenate(
        [field[(NODES - 1 - b) * face : (NODES - b) * face] for b in range(NODES // 2)], axis=0
    )
    even = wide_dot(forward_ref[0], top + bottom) * scale_ref[:half]
    odd = wide_dot(forward_ref[1], top - bottom) * scale_ref[half:]
    even = wide_dot(backward_ref[0], even)
    odd = wide_dot(backward_ref[1], odd)
    low_half = even + odd
    diff = even - odd
    parts = [low_half] + [diff[b * face : (b + 1) * face] for b in reversed(range(NODES // 2))]
    return jnp.concatenate(parts, axis=0)


def lane_layer(shape, ez_count):
    return lax.rem(lax.broadcasted_iota(jnp.int32, shape, 1), ez_count)


def lane_halves(ref):
    rows = ref.shape[0] // 2
    return jnp.concatenate([ref[:rows], ref[rows:]], axis=1)


def store_halves(ref, field):
    rows = field.shape[0]
    ref[:rows] = field[:, :128]
    ref[rows:] = field[:, 128:]


def assemble_local(field, out_ref, low_ref, high_ref, ez_count, average):
    rows, lanes = field.shape
    face = rows // NODES
    tile = NODES
    f4 = field.reshape(NODES, NODES, tile, lanes)
    a_low = f4[:, 0].reshape(face, lanes)
    a_high = f4[:, NODES - 1].reshape(face, lanes)
    new_low = a_low + pltpu.roll(a_high, ez_count, 1)
    new_high = a_high + pltpu.roll(a_low, lanes - ez_count, 1)
    if average:
        new_low = 0.5 * new_low
        new_high = 0.5 * new_high
    store_halves(out_ref, field)
    layer = lane_layer((face, 128), ez_count)
    for side in range(2):
        base = side * rows
        span = slice(side * 128, (side + 1) * 128)
        for b in range(NODES):
            at = base + b * face
            out_ref[at : at + tile] = new_low[b * tile : (b + 1) * tile, span]
            out_ref[at + face - tile : at + face] = new_high[b * tile : (b + 1) * tile, span]
        c_low = out_ref[pl.ds(base, face, stride=NODES), :]
        c_high = out_ref[pl.ds(base + NODES - 1, face, stride=NODES), :]
        above = c_low + pltpu.roll(c_high, 1, 1)
        below = c_high + pltpu.roll(c_low, 127, 1)
        if average:
            above = 0.5 * above
            below = 0.5 * below
        out_ref[pl.ds(base, face, stride=NODES), :] = jnp.where(layer > 0, above, c_low)
        out_ref[pl.ds(base + NODES - 1, face, stride=NODES), :] = jnp.where(
            layer < ez_count - 1, below, 0.0
        )
        low = out_ref[base : base + face]
        high = out_ref[base + rows - face : base + rows]
        low_ref[:, span] = low
        high_ref[:, span] = high


def joined(w_ref, below_ref, above_ref, scale):
    face = below_ref.shape[0]
    rows = w_ref.shape[0] // 2
    field = lane_halves(w_ref)
    low = field[:face] + below_ref[...]
    high = field[rows - face :] + above_ref[...]
    if scale != 1.0:
        low = low * scale
        high = high * scale
    return jnp.concatenate([low, field[face : rows - face], high], axis=0)


def pack_kernel(cols, codes, *refs):
    (device_ref, count_ref, source_hbm, geometry_hbm, disc_hbm, thrust_hbm, factor_hbm,
     q0, q1, q2, q3, place_hbm,
     held, geometry_ref, disc_ref, thrust_ref, factor_ref, place_ref, sems, row_sems) = refs
    parts = 4
    _, nodes, elem_x, _, lanes = source_hbm.shape
    face = nodes * nodes
    nodes_rows = elem_x * face
    copies = [
        pltpu.make_async_copy(hbm, ref, sems.at[i])
        for i, (hbm, ref) in enumerate(
            (
                (geometry_hbm, geometry_ref),
                (disc_hbm, disc_ref),
                (thrust_hbm, thrust_ref),
                (factor_hbm, factor_ref),
            )
        )
    ]
    for copy in copies:
        copy.start()
    row_copies = []
    for ey in range(parts):
        for ex in range(elem_x):
            for b in range(nodes):
                row = ex * face + b * nodes
                row_copies.append(
                    pltpu.make_async_copy(
                        source_hbm.at[:, b, ex, ey, :],
                        held.at[ey, row : row + nodes, :],
                        row_sems.at[len(row_copies)],
                    )
                )
    for copy in row_copies:
        copy.start()
    code = jnp.int32(codes[0])
    for d in range(1, len(codes)):
        code = jnp.where(device_ref[0] == d, jnp.int32(codes[d]), code)
    place_ref[...] = jnp.full(place_ref.shape, code, jnp.int32)
    levels = count_ref.shape[0]
    lane = lax.broadcasted_iota(jnp.int32, (1, lanes), 1)
    limit = jnp.zeros((1, lanes), jnp.int32)
    for l in range(levels):
        limit = jnp.where(lane // cols == l, count_ref[l], limit)
    live = jnp.where(lax.rem(lane, cols) < limit, 1.0, 0.0).astype(f32)
    for copy in copies:
        copy.wait()
    push = disc_ref[...].astype(f32) * thrust_ref[...]
    ez_count = push.shape[2]
    blank = jnp.zeros((1, lanes - 2 * ez_count), f32)
    count = factor_ref.shape[0]
    span = factor_ref.shape[1] // (8 * parts)
    for ey in range(parts):
        pieces = [
            jnp.concatenate([geometry_ref[c, ex, ey : ey + 1] for ex in range(2)] + [blank], 1)
            for c in range(3)
        ]
        pieces.append(jnp.concatenate([push[ex, ey : ey + 1] for ex in range(2)] + [blank], 1))
        pieces.append(live)
        pieces.append(jnp.zeros((3, lanes), f32))
        held[ey, nodes_rows : nodes_rows + 8] = jnp.concatenate(pieces, axis=0)
        for pair in range(4):
            at = [(2 * pair + k) * parts * span + ey * span for k in range(2)]
            base = nodes_rows + 8 + (pair // 2) * count
            column = (pair % 2) * 2 * span
            held[ey, base : base + count, column : column + 2 * span] = jnp.concatenate(
                [factor_ref[:, start : start + span] for start in at], axis=1
            )
    for copy in row_copies:
        copy.wait()
    outs = [
        pltpu.make_async_copy(held.at[field_of(code, 2 * q)], ref, sems.at[4 + q])
        for q, ref in enumerate((q0, q1, q2, q3))
    ]
    outs.append(pltpu.make_async_copy(place_ref, place_hbm, sems.at[8]))
    for copy in outs:
        copy.start()
    for copy in outs:
        copy.wait()


def message_part(base_ref, q):
    return field_of(base_ref[0, 0], 8 + 2 * q)


def factor_block(ref, count, vu):
    base = ref.shape[0] - 2 * count + (vu // 2) * count
    return ref[base : base + count, (vu % 2) * 128 : (vu % 2) * 128 + 128]


def entry_kernel(ez_count, *refs):
    (place_ref, q0, q1, q2, q3, columns_ref, deal_ref,
     w_ref, low_ref, high_ref, inv_ref, den_ref, live_ref, held) = refs
    rows = w_ref.shape[0] // 2
    face = rows // NODES
    lanes = 2 * w_ref.shape[1]
    parts = 4
    width = lanes // parts
    for q, ref in enumerate((q0, q1, q2, q3)):
        held[message_part(place_ref, q)] = ref[: 2 * face + 8]
    sizes = jnp.concatenate(
        [held[i, 2 * face : 2 * face + 8, :width] for i in range(parts)], axis=1
    )
    len_x, len_y, len_z, push = sizes[0:1], sizes[1:2], sizes[2:3], sizes[3:4]
    metric_x = len_y * len_z / (2.0 * len_x)
    metric_y = len_x * len_z / (2.0 * len_y)
    metric_z = len_x * len_y / (2.0 * len_z)
    volume = len_x * len_y * len_z / 8.0
    metrics = jnp.concatenate(
        [metric_x, metric_y, metric_z, jnp.zeros((5, lanes), f32)], axis=0
    )
    stiff = hp_dot(columns_ref[:, :8], metrics)
    den_ref[...] = stiff
    inv_ref[...] = 1.0 / (stiff + shift_ratio * (metric_x + metric_y + metric_z))
    for i in range(parts):
        live_ref[2 * i : 2 * i + 1] = held[i, 2 * face + 4 : 2 * face + 5, :128]
        live_ref[2 * i + 1 : 2 * i + 2] = held[i, 2 * face + 4 : 2 * face + 5, 128:256]
    raw = jnp.concatenate(
        [
            jnp.concatenate([held[i, :face], held[i, face : 2 * face]], axis=1)
            for i in range(parts)
        ],
        axis=0,
    )
    dealt = move_lanes(raw, deal_ref[...])
    for c in range(NODES):
        for side in range(2):
            w_ref[pl.ds(side * rows + c, face, stride=NODES), :] = jnp.concatenate(
                [
                    dealt[i * face : (i + 1) * face, c * width : (c + 1) * width]
                    for i in (2 * side, 2 * side + 1)
                ],
                axis=1,
            )
    forcing = (lane_halves(w_ref) + push) * (columns_ref[:, 3:4] * volume)
    assemble_local(forcing, w_ref, low_ref, high_ref, ez_count, False)


def precond_kernel(ez_count, first, *refs):
    if first:
        (w_ref, below_ref, above_ref, fwd_ref, bwd_ref, inv_ref,
         r_ref, u_ref, low_ref, high_ref) = refs
        resid = joined(w_ref, below_ref, above_ref, 1.0)
    else:
        (w_ref, below_ref, above_ref, r_in_ref, fwd_ref, bwd_ref, inv_ref,
         r_ref, u_ref, low_ref, high_ref) = refs
        resid = r_in_ref[...] - joined(w_ref, below_ref, above_ref, 1.0)
    r_ref[...] = resid
    field = spectral_apply(resid, fwd_ref, bwd_ref, inv_ref)
    assemble_local(field, u_ref, low_ref, high_ref, ez_count, True)


def apply_kernel(ez_count, keep, gain, start, keep_d, *refs):
    refs = list(refs)
    w_ref, below_ref, above_ref = refs[:3]
    refs = refs[3:]
    step = joined(w_ref, below_ref, above_ref, 0.5)
    if gain != 1.0:
        step = step * gain
    if keep != 0.0:
        step = step + keep * refs.pop(0)[...]
    total = step if start else refs.pop(0)[...] + step
    fwd_ref, bwd_ref, den_ref = refs[:3]
    refs = refs[3:]
    x_ref, k_ref, low_ref, high_ref = refs[:4]
    x_ref[...] = total
    if keep_d:
        refs[4][...] = step
    field = spectral_apply(step, fwd_ref, bwd_ref, den_ref)
    assemble_local(field, k_ref, low_ref, high_ref, ez_count, False)


def restrict_kernel(ez_count, count, *refs):
    (place_ref, w_ref, below_ref, above_ref, r_in_ref, restrict_ref, swaps_ref, x0, x1, x2, x3,
     r_ref, part_ref, coarse, sums) = refs
    lanes = 2 * w_ref.shape[1]
    parts = 4
    width = lanes // parts
    resid = r_in_ref[...] - joined(w_ref, below_ref, above_ref, 1.0)
    r_ref[...] = resid
    rows = hp_dot(restrict_ref[...], resid)
    b = rows[:8] + jnp.where(lane_layer((8, lanes), ez_count) == 0, rows[8:], 0.0)
    for i in range(parts):
        pair = jnp.concatenate(
            [b[:4, i * width : (i + 1) * width], b[4:, i * width : (i + 1) * width]], axis=1
        )
        coarse[i] = hp_dot(jnp.concatenate([pair, pair], axis=0), swaps_ref[: 2 * width])
    sums[...] = jnp.zeros_like(sums)
    block = 2 * width
    for q, ref in enumerate((x0, x1, x2, x3)):
        i = message_part(place_ref, q)
        mine = coarse[i]
        acc = factor_block(ref, count, 0) * mine[0:1]
        for vu in range(1, 4):
            acc = acc + factor_block(ref, count, vu) * mine[vu : vu + 1]
        sums[i, :count] = acc
    flat = sums[...].reshape(parts * sums.shape[1], block)
    ones = jnp.ones((8, block), f32)
    row = lax.dot_general(
        ones, flat, (((1,), (1,)), ((), ())), precision=highest, preferred_element_type=f32
    )
    tile = jnp.concatenate(
        [row[0:1, i * 128 : (i + 1) * 128] for i in range(2 * parts)], axis=0
    )
    part_ref[...] = jnp.broadcast_to(tile[None], part_ref.shape)


def prolong_kernel(ez_count, count, inner_levels, cols, groups, *refs):
    (place_ref, all_ref, live_ref, swaps_ref, columns_ref, x0, x1, x2, x3,
     w_ref, low_ref, high_ref, table, coarse) = refs
    lanes = 2 * w_ref.shape[1]
    parts = 4
    width = lanes // parts
    block = 2 * width
    row_id = lax.broadcasted_iota(jnp.int32, all_ref.shape[1:], 0)
    lane_id = lax.broadcasted_iota(jnp.int32, all_ref.shape[1:], 1)
    level = (lax.rem(row_id, 2) * 128 + lane_id) // cols
    mine = lax.shift_right_logical(jnp.full_like(level, lax.shift_right_logical(place_ref[0, 0], 24)), level)
    base = jnp.zeros(all_ref.shape[1:], f32)
    for source in range(all_ref.shape[0]):
        theirs = lax.shift_right_logical(jnp.full_like(level, groups[source]), level)
        base = base + jnp.where(theirs == mine, all_ref[source], 0.0)
    total = base
    step = 2
    for bit in range(2):
        flip = jnp.where(
            lax.rem(row_id // step, 2) == 0,
            pltpu.roll(total, 8 - step, 0),
            pltpu.roll(total, step, 0),
        )
        total = jnp.where(level > inner_levels + bit, total + flip, total)
        step *= 2
    total = total * live_ref[...]
    turned = jnp.transpose(total)
    for i in range(parts):
        table[i, :128] = jnp.broadcast_to(turned[:, 2 * i : 2 * i + 1], (128, block))
        table[i, 128:] = jnp.broadcast_to(turned[:, 2 * i + 1 : 2 * i + 2], (128, block))
    for q, ref in enumerate((x0, x1, x2, x3)):
        i = message_part(place_ref, q)
        y = table[i, :count]
        for vu in range(4):
            coarse[i, vu : vu + 1] = jnp.sum(
                factor_block(ref, count, vu) * y, axis=0, keepdims=True
            )
    lows, highs = [], []
    for i in range(parts):
        pair = hp_dot(coarse[i], swaps_ref[2 * width :])
        lows.append(pair[:4, :width])
        highs.append(pair[:4, width:])
    e = jnp.concatenate([jnp.concatenate(lows, axis=1), jnp.concatenate(highs, axis=1)], axis=0)
    field = hp_dot(columns_ref[...], jnp.concatenate([jnp.zeros_like(e), e], axis=0))
    assemble_local(field, w_ref, low_ref, high_ref, ez_count, True)


def exit_kernel(keep, gain, *refs):
    (place_ref, w_ref, below_ref, above_ref, d_ref, x_ref, columns_ref, gather_ref,
     q0, q1, q2, q3, field, held) = refs
    lanes = 2 * w_ref.shape[1]
    parts = 4
    width = lanes // parts
    face = below_ref.shape[0]
    rows = x_ref.shape[0]
    step = joined(w_ref, below_ref, above_ref, 0.5) * gain + keep * d_ref[...]
    store_halves(field, (x_ref[...] + step) * columns_ref[:, 4:5])
    blocks = []
    for side in range(2):
        layers = [field[pl.ds(side * rows + c, face, stride=NODES), :] for c in range(NODES)]
        for i in range(2):
            blocks.append(
                jnp.concatenate([t[:, i * width : (i + 1) * width] for t in layers], axis=1)
            )
    dealt = move_lanes(jnp.concatenate(blocks, axis=0), gather_ref[...])
    half = dealt.shape[1] // 2
    for i in range(parts):
        held[i, 0] = dealt[i * face : (i + 1) * face, :half]
        held[i, 1] = dealt[i * face : (i + 1) * face, half:]
    for q, ref in enumerate((q0, q1, q2, q3)):
        ref[...] = held[message_part(place_ref, q)]


def call(kernel, name, out_shapes, args, scratch=()):
    return pl.pallas_call(
        kernel,
        name=name,
        out_shape=[jax.ShapeDtypeStruct(s, f32) for s in out_shapes],
        in_specs=[pl.BlockSpec(memory_space=VMEM)] * len(args),
        out_specs=[pl.BlockSpec(memory_space=VMEM)] * len(out_shapes),
        scratch_shapes=list(scratch),
        compiler_params=pltpu.CompilerParams(vmem_limit_bytes=12 * 1024 * 1024),
    )(*args)


def fast_device(source, geometry, disc_mask, thrust, xxt_factor, col_count):
    gx_count, gy_count = lax.axis_size("gx"), lax.axis_size("gy")
    axes = ("gx", "gy")
    nodes, _, elem_x, elem_y, z_count = source.shape
    ez_count = geometry.shape[3]
    levels, cols, _ = xxt_factor.shape
    parts = gx_count
    lanes = parts * elem_x * ez_count
    width = elem_x * ez_count
    rows = nodes**3
    face = nodes * nodes
    devices = gx_count * gy_count
    tables = {k: jnp.asarray(v) for k, v in constant_tables(ez_count, lanes).items()}
    ring, send, group, codes = placement(gx_count, gy_count)
    groups = [int(g) for g in group]
    device = lax.axis_index("gx") * gy_count + lax.axis_index("gy")
    up = [(ring[i], ring[(i + 1) % devices]) for i in range(devices)]
    down = [(target, origin) for origin, target in up]

    def spread(q):
        return [
            (i * gy_count + j, ring[parts * j + int(send[i * gy_count + j, q])])
            for i in range(gx_count)
            for j in range(gy_count)
        ]

    def halo(low, high):
        return lax.ppermute(high, axes, up), lax.ppermute(low, axes, down)

    count = levels * cols
    message = (elem_x * face + 8 + 2 * count, z_count)
    spec = lambda space: pl.BlockSpec(memory_space=space)
    *packed, place = pl.pallas_call(
        functools.partial(pack_kernel, cols, codes),
        name="pack",
        out_shape=[jax.ShapeDtypeStruct(message, f32)] * parts
        + [jax.ShapeDtypeStruct((8, 128), jnp.int32)],
        in_specs=[spec(SMEM)] * 2 + [spec(pl.ANY)] * 5,
        out_specs=[spec(pl.ANY)] * (parts + 1),
        scratch_shapes=[
            VMEM((parts,) + message, f32),
            VMEM(geometry.shape, f32),
            VMEM(disc_mask.shape, jnp.int32),
            VMEM(thrust.shape, f32),
            VMEM((count, xxt_factor.shape[2]), f32),
            VMEM((8, 128), jnp.int32),
            pltpu.SemaphoreType.DMA((2 * parts + 1,)),
            pltpu.SemaphoreType.DMA((elem_y * elem_x * nodes,)),
        ],
        compiler_params=pltpu.CompilerParams(vmem_limit_bytes=67043328),
    )(
        jnp.reshape(device, (1,)), col_count.reshape(levels), source, geometry, disc_mask, thrust,
        xxt_factor.reshape(count, -1),
    )
    received = [lax.ppermute(packed[q], axes, spread(q)) for q in range(parts)]
    inner_levels = gy_count.bit_length() - 1

    fshape = (rows, lanes)
    sshape = (2 * rows, lanes // 2)
    hshape = (face, lanes)
    w, low, high, inv, den, live_tile = call(
        functools.partial(entry_kernel, ez_count), "entry",
        [sshape, hshape, hshape, fshape, fshape, (2 * parts, 128)],
        [place, *received, tables["columns"], tables["deal"]],
        [VMEM((parts, 2 * face + 8, z_count), f32)],
    )
    fwd, bwd = tables["forward"], tables["backward"]

    def precond(w, low, high, resid):
        prev, nxt = halo(low, high)
        args = [w, prev, nxt] + ([] if resid is None else [resid]) + [fwd, bwd, inv]
        return call(
            functools.partial(precond_kernel, ez_count, resid is None), "precond",
            [fshape, sshape, hshape, hshape], args,
        )

    def advance(w, low, high, d, x, keep, gain, keep_d):
        prev, nxt = halo(low, high)
        args = [w, prev, nxt] + ([] if keep == 0.0 else [d]) + ([] if x is None else [x])
        out = call(
            functools.partial(apply_kernel, ez_count, keep, gain, x is None, keep_d), "apply",
            [fshape, sshape, hshape, hshape] + ([fshape] if keep_d else []),
            args + [fwd, bwd, den],
        )
        return out[0], out[1], out[2], out[3], (out[4] if keep_d else None)

    center = 0.5 * (bound_high + bound_low)
    radius = 0.5 * (bound_high - bound_low)
    ratio = center / radius
    rho_old = 1.0 / ratio
    rho_new = 1.0 / (2.0 * ratio - rho_old)
    first_gain = 1.0 / center
    keep = rho_new * rho_old
    gain = 2.0 * rho_new / radius

    x = None
    resid = None
    for cycle in range(CYCLES):
        resid, u, low, high = precond(w, low, high, resid)
        x, k, low, high, d = advance(u, low, high, None, x, 0.0, first_gain, True)
        resid, u, low, high = precond(k, low, high, resid)
        x, k, low, high, _ = advance(u, low, high, d, x, keep, gain, False)
        prev, nxt = halo(low, high)
        resid, partial = call(
            functools.partial(restrict_kernel, ez_count, count), "restrict",
            [fshape, (devices, 2 * parts, 128)],
            [place, k, prev, nxt, resid, tables["restrict"], tables["swaps"], *received],
            [VMEM((parts, 8, 2 * width), f32), VMEM((parts, 256, 2 * width), f32)],
        )
        everyone = lax.all_to_all(partial, axes, 0, 0)
        f, low, high = call(
            functools.partial(prolong_kernel, ez_count, count, inner_levels, cols, groups), "prolong",
            [sshape, hshape, hshape],
            [place, everyone, live_tile, tables["swaps"], tables["columns"],
             *received],
            [VMEM((parts, 256, 2 * width), f32), VMEM((parts, 8, 2 * width), f32)],
        )
        x, k, low, high, _ = advance(f, low, high, None, x, 0.0, 1.0, False)
        resid, u, low, high = precond(k, low, high, resid)
        x, k, low, high, d = advance(u, low, high, None, x, 0.0, first_gain, True)
        resid, u, low, high = precond(k, low, high, resid)
        if cycle < CYCLES - 1:
            x, w, low, high, _ = advance(u, low, high, d, x, keep, gain, False)
    prev, nxt = halo(low, high)
    chunks = call(
        functools.partial(exit_kernel, keep, gain), "exit",
        [(2, face, z_count)] * parts,
        [place, u, prev, nxt, d, x, tables["columns"], tables["gather"]],
        [VMEM(sshape, f32), VMEM((parts, 2, face, z_count), f32)],
    )
    back = [
        lax.ppermute(chunks[q], axes, [(t, s) for s, t in spread(q)]) for q in range(parts)
    ]
    stacked = jnp.stack(back)
    by_ey = jnp.stack(
        [
            lax.dynamic_index_in_dim(stacked, field_of(place[0, 0], 16 + 2 * ey), 0, keepdims=False)
            for ey in range(parts)
        ]
    )
    by_ey = by_ey.reshape(elem_y, elem_x, nodes, nodes, z_count)
    return by_ey.transpose(3, 2, 1, 0, 4)


def is_fast(mesh, source, geometry, xxt_factor):
    gx_count, gy_count = mesh.shape["gx"], mesh.shape["gy"]
    nodes, _, elem_x, elem_y, z_count = source.shape
    ez_count = geometry.shape[3]
    levels, cols, _ = xxt_factor.shape
    return (
        gx_count == 4 and elem_y == gx_count and gy_count % 4 == 0 and gy_count >= 8
        and gy_count & (gy_count - 1) == 0 and elem_x == 2 and nodes == NODES and z_count == 256
        and 2 * elem_x * ez_count == 128 and levels * cols <= 256
        and 4 * elem_x * ez_count == 256 and levels == (gx_count * gy_count).bit_length() and (levels * cols) % 8 == 0
    )


def solution(mesh):
    def body(source, geometry, disc_mask, thrust, xxt_factor, col_count):
        run = fast_device if is_fast(mesh, source, geometry, xxt_factor) else per_device
        return run(source, geometry, disc_mask, thrust, xxt_factor, col_count)

    return jax.shard_map(
        body,
        mesh=mesh,
        in_specs=(
            P(None, None, "gx", "gy", None),
            P(None, "gx", "gy", None),
            P("gx", "gy", None),
            P("gx", "gy", None),
            P(None, None, ("gx", "gy")),
            P(None, ("gx", "gy")),
        ),
        out_specs=P(None, None, "gx", "gy", None),
        check_vma=False,
    )
```

```python
import functools
import itertools
import math

import jax
import jax.numpy as jnp
import numpy as np
from jax import lax
from jax.experimental import pallas as pl
from jax.experimental.pallas import tpu as pltpu
from jax.sharding import PartitionSpec as P

NODES = 8
CYCLES = 2
CHEB_DEGREE = 2


highest = lax.Precision.HIGHEST
bound_low = 0.3
bound_high = 3.0
shift_ratio = 0.25


def padded(block, sides, width):
    for axis, dim in sides:
        count = lax.axis_size(axis)
        forward = [(i, i + 1) for i in range(count - 1)]
        forward.append((count - 1, 0))
        backward = [(target, source) for source, target in forward]
        low = lax.ppermute(
            lax.slice_in_dim(block, block.shape[dim] - width, None, axis=dim), axis, forward
        )
        high = lax.ppermute(lax.slice_in_dim(block, 0, width, axis=dim), axis, backward)
        block = jnp.concatenate([low, block, high], axis=dim)
    return block


def swapped(x, axis, bit):
    return lax.ppermute(x, axis, [(i, i ^ 1 << bit) for i in range(lax.axis_size(axis))])


def legendre_table(points, poly_order):
    table = [points * 0.0 + 1.0, points]
    for degree in range(2, poly_order + 1):
        table.append(
            ((2.0 * degree - 1.0) * points * table[-1] - (degree - 1.0) * table[-2]) / degree
        )
    return table


def jacobi_eigen(matrix):
    size_n = matrix.shape[0]
    current = matrix.copy()
    vectors = np.eye(size_n)
    for sweep_index in range(30):
        for first in range(size_n - 1):
            for second in range(first + 1, size_n):
                angle = 0.5 * math.atan2(
                    2.0 * float(current[first, second]),
                    float(current[second, second] - current[first, first]),
                )
                rotation = np.eye(size_n)
                rotation[first, first] = math.cos(angle)
                rotation[second, second] = math.cos(angle)
                rotation[first, second] = math.sin(angle)
                rotation[second, first] = -math.sin(angle)
                current = rotation.T @ current @ rotation
                vectors = vectors @ rotation
    values = np.array([current[index, index] for index in range(size_n)])
    order = np.argsort(values)
    return (values[order], vectors[:, order])


def gll_tables(node_count):
    poly_order = node_count - 1
    points = np.cos(np.pi * np.arange(node_count) / poly_order)
    for newton_index in range(200):
        table = legendre_table(points, poly_order)
        points = points - (points * table[poly_order] - table[poly_order - 1]) / (
            node_count * table[poly_order]
        )
    points = points[::-1].copy()
    legendre = legendre_table(points, poly_order)[poly_order]
    weights = 2.0 / (poly_order * (poly_order + 1) * legendre**2)
    identity = np.eye(node_count)
    gap_matrix = points[:, None] - points[None, :] + identity
    off_diagonal = legendre[:, None] / (legendre[None, :] * gap_matrix) * (1.0 - identity)
    end_value = poly_order * (poly_order + 1) / 4.0
    end_terms = np.concatenate([[-end_value], np.zeros(node_count - 2), [end_value]])
    derivative = off_diagonal + identity * end_terms[None, :]
    stiffness = derivative.T @ (weights[:, None] * derivative)
    root_inverse = 1.0 / np.sqrt(weights)
    symmetric = root_inverse[:, None] * stiffness * root_inverse[None, :]
    symmetric = 0.5 * (symmetric + symmetric.T)
    eigen_values, eigen_vectors = jacobi_eigen(symmetric)
    eigen_modes = root_inverse[:, None] * eigen_vectors
    vertex_interp = np.stack([(1.0 - points) / 2.0, (1.0 + points) / 2.0], axis=1)
    return (
        weights.astype(np.float32),
        stiffness.astype(np.float32),
        eigen_modes.astype(np.float32),
        eigen_values.astype(np.float32),
        vertex_interp.astype(np.float32),
    )


def build_setup(geometry):
    weights, stiffness, eigen_modes, eigen_values, vertex_interp = gll_tables(NODES)
    elem_z = geometry.shape[3]
    z_count = elem_z * NODES
    lengths = jnp.repeat(geometry, NODES, axis=3)
    len_x = lengths[0][None, None]
    len_y = lengths[1][None, None]
    len_z = lengths[2][None, None]
    metric_x = len_y * len_z / (2.0 * len_x)
    metric_y = len_x * len_z / (2.0 * len_y)
    metric_z = len_x * len_y / (2.0 * len_z)
    node_weight = jnp.asarray(weights)
    weight_a = node_weight[:, None, None, None, None]
    weight_b = node_weight[None, :, None, None, None]
    weight_c = jnp.tile(node_weight, elem_z)
    coef_x = metric_x * weight_b * weight_c
    coef_y = metric_y * weight_a * weight_c
    coef_z = metric_z * weight_a * weight_b
    mass_diag = len_x * len_y * len_z / 8.0 * weight_a * weight_b * weight_c
    spectrum = jnp.asarray(eigen_values)
    denominator = (
        metric_x * spectrum[:, None, None, None, None]
        + metric_y * spectrum[None, :, None, None, None]
        + metric_z * jnp.tile(spectrum, elem_z)
        + shift_ratio * (metric_x + metric_y + metric_z)
    )
    inv_denom = 1.0 / denominator
    z_index = jnp.arange(z_count)
    z_node = z_index % NODES
    dirichlet = (z_index < z_count - 1).astype(jnp.float32)
    node_index = jnp.arange(NODES)
    edge_node = ((node_index == 0) | (node_index == NODES - 1)).astype(jnp.float32) + 1.0
    z_shared = (
        1.0
        + ((z_node == 0) & (z_index > 0)).astype(jnp.float32)
        + ((z_node == NODES - 1) & (z_index < z_count - 1)).astype(jnp.float32)
    )
    inv_mult = 1.0 / (
        edge_node[:, None, None, None, None] * edge_node[None, :, None, None, None] * z_shared
    )
    eye_z = jnp.eye(elem_z, dtype=jnp.float32)
    stiff_matrix = jnp.asarray(stiffness)
    mode_matrix = jnp.asarray(eigen_modes)
    interp = jnp.asarray(vertex_interp)
    z_stiff = jnp.kron(eye_z, stiff_matrix.T)
    z_modes = jnp.kron(eye_z, mode_matrix)
    z_modes_t = jnp.kron(eye_z, mode_matrix.T)
    z_restrict = jnp.kron(eye_z, interp)
    z_prolong = jnp.kron(eye_z, interp.T)
    link_up = (z_index[None, :] == z_index[:, None] + 1) & (z_node[:, None] == NODES - 1)
    link_down = (z_index[None, :] == z_index[:, None] - 1) & (z_node[:, None] == 0)
    z_sum = ((z_index[:, None] == z_index[None, :]) | link_up | link_down).astype(jnp.float32)
    return (
        coef_x,
        coef_y,
        coef_z,
        mass_diag,
        inv_denom,
        dirichlet,
        inv_mult,
        stiff_matrix,
        mode_matrix,
        z_stiff,
        z_modes,
        z_modes_t,
        z_restrict,
        z_prolong,
        z_sum,
        interp,
    )


def pair_sum_x(data_field, prev_high, next_low):
    low_face = data_field[0]
    high_face = data_field[-1]
    before_faces = jnp.concatenate([prev_high[:, None], high_face[:, :-1]], axis=1)
    after_faces = jnp.concatenate([low_face[:, 1:], next_low[:, None]], axis=1)
    return jnp.concatenate(
        [(low_face + before_faces)[None], data_field[1:-1], (high_face + after_faces)[None]], axis=0
    )


def pair_sum_y(data_field, prev_high, next_low):
    low_face = data_field[:, 0]
    high_face = data_field[:, -1]
    before_faces = jnp.concatenate([prev_high[:, :, None], high_face[:, :, :-1]], axis=2)
    after_faces = jnp.concatenate([low_face[:, :, 1:], next_low[:, :, None]], axis=2)
    return jnp.concatenate(
        [
            (low_face + before_faces)[:, None],
            data_field[:, 1:-1],
            (high_face + after_faces)[:, None],
        ],
        axis=1,
    )


def corner_slot(line_values, node_count):
    padding = jnp.zeros((node_count - 1, line_values.shape[0]), jnp.float32)
    return jnp.concatenate([line_values[None], padding], axis=0)


def summed_neighbour_face(raw_face, prev_line, next_line):
    node_count, elem_x, z_count = raw_face.shape
    shaped = raw_face.reshape(node_count, 1, elem_x, 1, z_count)
    summed = pair_sum_x(shaped, prev_line[None, None], next_line[None, None])
    return summed.reshape(node_count, elem_x, z_count)


def assemble(data_field, z_sum):
    node_count = data_field.shape[0]
    elem_x = data_field.shape[2]
    elem_y = data_field.shape[3]
    z_count = data_field.shape[4]
    frame = jnp.zeros((elem_x + 2, elem_y + 2, node_count, z_count), jnp.float32)
    frame = frame.at[0, 1 : elem_y + 1].set(jnp.transpose(data_field[0][:, 0], (1, 0, 2)))
    frame = frame.at[elem_x + 1, 1 : elem_y + 1].set(
        jnp.transpose(data_field[-1][:, -1], (1, 0, 2))
    )
    frame = frame.at[1 : elem_x + 1, 0].set(jnp.transpose(data_field[:, 0][:, :, 0], (1, 0, 2)))
    frame = frame.at[1 : elem_x + 1, elem_y + 1].set(
        jnp.transpose(data_field[:, -1][:, :, -1], (1, 0, 2))
    )
    frame = frame.at[0, 0].set(corner_slot(data_field[0, 0, 0, 0], node_count))
    frame = frame.at[0, elem_y + 1].set(corner_slot(data_field[0, -1, 0, -1], node_count))
    frame = frame.at[elem_x + 1, 0].set(corner_slot(data_field[-1, 0, -1, 0], node_count))
    frame = frame.at[elem_x + 1, elem_y + 1].set(
        corner_slot(data_field[-1, -1, -1, -1], node_count)
    )
    bordered = padded(frame, (("gx", 0), ("gy", 1)), 1)
    last_x = elem_x + 3
    last_y = elem_y + 3
    left_high = jnp.transpose(bordered[0, 2 : elem_y + 2], (1, 0, 2))
    right_low = jnp.transpose(bordered[last_x, 2 : elem_y + 2], (1, 0, 2))
    down_raw = jnp.transpose(bordered[2 : elem_x + 2, 0], (1, 0, 2))
    up_raw = jnp.transpose(bordered[2 : elem_x + 2, last_y], (1, 0, 2))
    down_high = summed_neighbour_face(down_raw, bordered[0, 0][0], bordered[last_x, 0][0])
    up_low = summed_neighbour_face(up_raw, bordered[0, last_y][0], bordered[last_x, last_y][0])
    data_field = pair_sum_x(data_field, left_high, right_low)
    data_field = pair_sum_y(data_field, down_high, up_low)
    return jnp.matmul(data_field, z_sum, precision=highest)


def chebyshev(solution, resid, apply_op, precond, keep_resid):
    center = 0.5 * (bound_high + bound_low)
    radius = 0.5 * (bound_high - bound_low)
    center_ratio = center / radius
    rho_old = 1.0 / center_ratio
    direction = precond(resid) / center
    for step_index in range(CHEB_DEGREE):
        solution = solution + direction
        if step_index < CHEB_DEGREE - 1 or keep_resid:
            resid = resid - apply_op(direction)
        if step_index < CHEB_DEGREE - 1:
            rho_new = 1.0 / (2.0 * center_ratio - rho_old)
            direction = rho_new * rho_old * direction + 2.0 * rho_new / radius * precond(resid)
            rho_old = rho_new
    return (solution, resid)


def pressure_solve(source, disc_mask, thrust, setup_tables, assembler, coarse_solve):
    (
        coef_x,
        coef_y,
        coef_z,
        mass_diag,
        inv_denom,
        dirichlet,
        inv_mult,
        stiff_matrix,
        mode_matrix,
        z_stiff,
        z_modes,
        z_modes_t,
        z_restrict,
        z_prolong,
        z_sum,
        interp,
    ) = setup_tables

    def apply_op(data_field):
        along_x = jnp.einsum("ac,cbxyz->abxyz", stiff_matrix, data_field, precision=highest)
        along_y = jnp.einsum("bc,acxyz->abxyz", stiff_matrix, data_field, precision=highest)
        along_z = jnp.matmul(data_field, z_stiff, precision=highest)
        return dirichlet * assembler(coef_x * along_x + coef_y * along_y + coef_z * along_z, z_sum)

    def precond(resid):
        spectral = jnp.einsum("ai,abxyz->ibxyz", mode_matrix, resid, precision=highest)
        spectral = jnp.einsum("bj,abxyz->ajxyz", mode_matrix, spectral, precision=highest)
        spectral = jnp.matmul(spectral, z_modes, precision=highest) * inv_denom
        spectral = jnp.einsum("ai,ibxyz->abxyz", mode_matrix, spectral, precision=highest)
        spectral = jnp.einsum("bj,ajxyz->abxyz", mode_matrix, spectral, precision=highest)
        return (
            dirichlet
            * inv_mult
            * assembler(jnp.matmul(spectral, z_modes_t, precision=highest), z_sum)
        )

    forcing = source + jnp.repeat(disc_mask.astype(jnp.float32) * thrust, NODES, axis=2)[None, None]
    rhs_field = dirichlet * assembler(mass_diag * forcing, z_sum)
    solution = jnp.zeros_like(rhs_field)
    for sweep_index in range(CYCLES):
        if sweep_index == 0:
            resid = rhs_field
        else:
            resid = rhs_field - apply_op(solution)
        solution, resid = chebyshev(solution, resid, apply_op, precond, True)
        restrict_coarse = jnp.einsum("av,abxyz->vbxyz", interp, inv_mult * resid, precision=highest)
        restrict_coarse = jnp.einsum("bu,vbxyz->vuxyz", interp, restrict_coarse, precision=highest)
        correction = coarse_solve(jnp.matmul(restrict_coarse, z_restrict, precision=highest))
        fine_field = jnp.einsum("av,vuxyz->auxyz", interp, correction, precision=highest)
        fine_field = jnp.einsum("bu,auxyz->abxyz", interp, fine_field, precision=highest)
        solution = solution + dirichlet * inv_mult * assembler(
            jnp.matmul(fine_field, z_prolong, precision=highest), z_sum
        )
        resid = rhs_field - apply_op(solution)
        solution, resid = chebyshev(solution, resid, apply_op, precond, False)
    return solution


def per_device(source, geometry, disc_mask, thrust, xxt_factor, col_count):
    setup_tables = build_setup(geometry)

    def coarse_solve(coarse):
        flattened = coarse.reshape(-1)
        partial_value = jnp.einsum("lkn,n->lk", xxt_factor, flattened, precision=highest)
        live_mask = (jnp.arange(xxt_factor.shape[1])[None, :] < col_count).astype(jnp.float32)
        partial_value = partial_value * live_mask
        bit_count = (lax.axis_size("gx") * lax.axis_size("gy")).bit_length() - 1
        for bit_index in range(bit_count):
            upper_levels = partial_value[bit_index + 1 :]
            partner = swapped(upper_levels, ("gx", "gy"), bit_index)
            partial_value = jnp.concatenate(
                [partial_value[: bit_index + 1], upper_levels + partner], axis=0
            )
        return jnp.einsum("lkn,lk->n", xxt_factor, partial_value, precision=highest).reshape(
            coarse.shape
        )

    return pressure_solve(source, disc_mask, thrust, setup_tables, assemble, coarse_solve)


VMEM = pltpu.VMEM
SMEM = pltpu.SMEM
f32 = jnp.float32
bf16 = jnp.bfloat16


@functools.lru_cache(maxsize=None)
def placement(gx_count, gy_count):
    layers = gy_count // 2
    a, b, c, d = (0, 0), (0, 1), (1, 1), (1, 0)
    chips = [(d, 0), (a, 0), (b, 0), (c, 0)]
    for z in range(1, layers - 1):
        chips += [(column, z) for column in ((c, b, a) if z % 2 else (a, b, c))]
    chips += [(column, layers - 1) for column in (c, b, a, d)]
    chips += [(d, z) for z in range(layers - 2, 0, -1)]
    count = len(chips)

    def moved(turn):
        return sum(abs(chips[(i + turn) % count][1] - i // gx_count) for i in range(count))

    turn = min(range(count), key=moved)
    chips = chips[turn:] + chips[:turn]
    spots = [(column, z, core) for column, z in chips for core in (0, 1)]
    ring = [(y * 2 + x) * gy_count + 2 * z + core for (y, x), z, core in spots]

    def hops(i, j, place):
        (y, x), z, _ = spots[place]
        return abs(i // 2 - y) + abs(i % 2 - x) + abs(j // 2 - z)

    orders = list(itertools.permutations(range(gx_count)))
    squares = [
        rows
        for rows in itertools.product(orders, repeat=gx_count)
        if all(len(set(column)) == gx_count for column in zip(*rows))
    ]
    send = np.zeros((gx_count * gy_count, gx_count), np.int32)
    part = np.zeros((gx_count * gy_count, gx_count), np.int32)
    group = np.zeros(gx_count * gy_count, np.int32)
    for j in range(gy_count):
        far = [[hops(i, j, gx_count * j + s) for s in range(gx_count)] for i in range(gx_count)]
        cost = lambda rows: [max(far[i][row[i]] for i in range(gx_count)) for row in rows]
        best = min(squares, key=lambda rows: (sum(cost(rows)), cost(rows)))
        for q, row in enumerate(best):
            for i in range(gx_count):
                send[i * gy_count + j, q] = row[i]
                part[ring[gx_count * j + row[i]], q] = i
        for s in range(gx_count):
            group[ring[gx_count * j + s]] = j
    codes = group.astype(np.int64) << 24
    for q in range(gx_count):
        codes |= (send[:, q] << 2 * q) | (part[:, q] << 8 + 2 * q)
        codes |= np.argsort(send, axis=1)[:, q] << 16 + 2 * q
    return ring, send, group, [int(c) for c in codes]


def field_of(code, at):
    return lax.shift_right_logical(code, jnp.int32(at)) & 3


def split_bf16(values):
    high = values.astype(np.float32).astype(bf16)
    low = (values - high.astype(np.float64)).astype(np.float32).astype(bf16)
    return high, low


def wide(matrix):
    high, low = split_bf16(matrix)
    return np.concatenate([high, high, low], axis=1)


@functools.lru_cache(maxsize=None)
def constant_tables(ez_count, lanes):
    weights, _, modes, values, interp = [
        np.asarray(t, np.float64) for t in gll_tables(NODES)
    ]
    half = NODES // 2
    root = np.sqrt(weights)
    basis = root[:, None] * modes
    parity = np.sign(np.sum(basis * basis[::-1], axis=0))
    basis = 0.5 * (basis + parity * basis[::-1])
    even = [i for i in range(NODES) if parity[i] > 0]
    odd = [i for i in range(NODES) if parity[i] < 0]
    blocks = []
    for picked in (even, odd):
        blocks.append(np.kron(basis[:half, picked].T, np.kron(basis.T, basis.T)))
    forward = np.stack([wide(m) for m in blocks])
    backward = np.stack([wide(m.T) for m in blocks])
    face = NODES * NODES
    forward_face = np.stack([wide(m[:, :face]) for m in blocks])
    order_b = even + odd
    one = np.ones(NODES)
    lam_a = np.kron(one, np.kron(values, one))
    lam_b = np.kron(values[order_b], np.kron(one, one))
    lam_c = np.kron(one, np.kron(one, values))
    root3 = np.kron(root, np.kron(root, root))
    spectrum = np.stack([lam_a, lam_b, lam_c, root3] + [0 * lam_a] * 4, axis=1)
    edge = np.where((np.arange(NODES) == 0) | (np.arange(NODES) == NODES - 1), 0.5, 1.0)
    jw = interp * root[:, None] * edge[:, None]
    first = np.zeros_like(jw)
    first[0] = jw[0]
    def rows_of(jc):
        return np.stack(
            [
                np.kron(jw[:, u], np.kron(jw[:, v], jc[:, t]))
                for t in (0, 1) for v in (0, 1) for u in (0, 1)
            ]
        )
    restrict = np.concatenate([rows_of(jw), rows_of(first)], axis=0)
    jp = interp * root[:, None]
    prolong = np.stack(
        [
            np.kron(jp[:, u], np.kron(jp[:, v], jp[:, t]))
            for t in (0, 1) for v in (0, 1) for u in (0, 1)
        ],
        axis=1,
    )
    swap = np.zeros((4 * ez_count, 4 * ez_count))
    for t in range(2):
        for ex in range(2):
            for ez in range(ez_count):
                swap[(t * 2 + ex) * ez_count + ez, ex * 2 * ez_count + 2 * ez + t] = 1.0
    span = 2 * ez_count * NODES
    deal = np.zeros((span, span))
    for ex in range(2):
        for ez in range(ez_count):
            for c in range(NODES):
                deal[(ex * ez_count + ez) * NODES + c, (c * 2 + ex) * ez_count + ez] = 1.0
    as32 = lambda t: np.asarray(t, np.float32)
    return dict(
        forward=forward,
        forward_face=forward_face,
        backward=backward,
        columns=wide(np.concatenate([spectrum, prolong], axis=1)),
        inv_root=as32(1.0 / root3[:, None]),
        restrict=wide(restrict),
        swaps=np.concatenate([swap, swap.T], axis=0).astype(bf16),
        gather=deal.T.astype(bf16),
    )


def hp_dot(a, b):
    return jnp.dot(a, b, precision=highest, preferred_element_type=f32)


def move_lanes(field, table):
    rows = field.shape[0]
    high = field.astype(bf16)
    rest = field - high.astype(f32)
    middle = rest.astype(bf16)
    low = (rest - middle.astype(f32)).astype(bf16)
    moved = jnp.dot(
        jnp.concatenate([high, middle, low], axis=0), table, preferred_element_type=f32
    )
    return moved[:rows] + moved[rows : 2 * rows] + moved[2 * rows :]


def wide_dot(table, field):
    high = field.astype(bf16)
    low = (field - high.astype(f32)).astype(bf16)
    stacked = jnp.concatenate([high, low, high], axis=0)
    return jnp.dot(table, stacked, preferred_element_type=f32)


def to_modes(field, forward_ref, scale_ref):
    face = field.shape[0] // NODES
    half = field.shape[0] // 2
    top = field[:half]
    bottom = jnp.concatenate(
        [field[(NODES - 1 - b) * face : (NODES - b) * face] for b in range(NODES // 2)], axis=0
    )
    even = wide_dot(forward_ref[0], top + bottom) * scale_ref[:half]
    odd = wide_dot(forward_ref[1], top - bottom) * scale_ref[half:]
    return jnp.concatenate([even, odd], axis=0)


def from_modes(modes, backward_ref):
    half = modes.shape[0] // 2
    face = modes.shape[0] // NODES
    even = wide_dot(backward_ref[0], modes[:half])
    odd = wide_dot(backward_ref[1], modes[half:])
    diff = even - odd
    parts = [diff[b * face : (b + 1) * face] for b in reversed(range(NODES // 2))]
    return jnp.concatenate([even + odd] + parts, axis=0)


def faces_to_modes(low, high, forward_face_ref, scale_ref):
    half = scale_ref.shape[0] // 2
    even = wide_dot(forward_face_ref[0], low + high) * scale_ref[:half]
    odd = wide_dot(forward_face_ref[1], low - high) * scale_ref[half:]
    return jnp.concatenate([even, odd], axis=0)


def modes_to_faces(modes, backward_ref):
    half = modes.shape[0] // 2
    face = modes.shape[0] // NODES
    even = wide_dot(backward_ref[0, :face], modes[:half])
    odd = wide_dot(backward_ref[1, :face], modes[half:])
    return even + odd, even - odd


def lane_layer(shape, ez_count):
    return lax.rem(lax.broadcasted_iota(jnp.int32, shape, 1), ez_count)


def lane_halves(ref):
    rows = ref.shape[0] // 2
    return jnp.concatenate([ref[:rows], ref[rows:]], axis=1)


def store_halves(ref, field):
    rows = field.shape[0]
    ref[:rows] = field[:, :128]
    ref[rows:] = field[:, 128:]


def sum_pairs(field, work_ref, ez_count, average):
    rows, lanes = field.shape
    face = NODES * NODES
    tile = NODES
    count = rows // face
    f4 = field.reshape(count, NODES, tile, lanes)
    a_low = f4[:, 0].reshape(count * tile, lanes)
    a_high = f4[:, NODES - 1].reshape(count * tile, lanes)
    new_low = a_low + pltpu.roll(a_high, ez_count, 1)
    new_high = a_high + pltpu.roll(a_low, lanes - ez_count, 1)
    if average:
        new_low = 0.5 * new_low
        new_high = 0.5 * new_high
    store_halves(work_ref, field)
    spots = rows // NODES
    layer = lane_layer((spots, 128), ez_count)
    for side in range(2):
        base = side * rows
        span = slice(side * 128, (side + 1) * 128)
        for b in range(count):
            at = base + b * face
            work_ref[at : at + tile] = new_low[b * tile : (b + 1) * tile, span]
            work_ref[at + face - tile : at + face] = new_high[b * tile : (b + 1) * tile, span]
        c_low = work_ref[pl.ds(base, spots, stride=NODES), :]
        c_high = work_ref[pl.ds(base + NODES - 1, spots, stride=NODES), :]
        above = c_low + pltpu.roll(c_high, 1, 1)
        below = c_high + pltpu.roll(c_low, 127, 1)
        if average:
            above = 0.5 * above
            below = 0.5 * below
        work_ref[pl.ds(base, spots, stride=NODES), :] = jnp.where(layer > 0, above, c_low)
        work_ref[pl.ds(base + NODES - 1, spots, stride=NODES), :] = jnp.where(
            layer < ez_count - 1, below, 0.0
        )


def store_faces(work_ref, low_ref, high_ref):
    face = low_ref.shape[0]
    rows = work_ref.shape[0] // 2
    for side in range(2):
        span = slice(side * 128, (side + 1) * 128)
        low_ref[:, span] = work_ref[side * rows : side * rows + face]
        high_ref[:, span] = work_ref[(side + 1) * rows - face : (side + 1) * rows]


def assemble_local(field, out_ref, low_ref, high_ref, ez_count, average):
    sum_pairs(field, out_ref, ez_count, average)
    store_faces(out_ref, low_ref, high_ref)


def with_faces(field, below_ref, above_ref, scale):
    face = below_ref.shape[0]
    rows = field.shape[0]
    return jnp.concatenate(
        [
            field[:face] + scale * below_ref[...],
            field[face : rows - face],
            field[rows - face :] + scale * above_ref[...],
        ],
        axis=0,
    )


def half_faces(field):
    face = NODES * NODES
    rows = field.shape[0]
    return jnp.concatenate(
        [0.5 * field[:face], field[face : rows - face], 0.5 * field[rows - face :]], axis=0
    )


def pack_kernel(cols, gy_count, codes, *refs):
    (device_ref, count_ref, source_hbm, geometry_hbm, disc_hbm, thrust_hbm, factor_hbm,
     q0, q1, q2, q3,
     held, geometry_ref, disc_ref, thrust_ref, factor_ref, sems, row_sems) = refs
    parts = 4
    _, nodes, elem_x, _, lanes = source_hbm.shape
    face = nodes * nodes
    nodes_rows = elem_x * face
    copies = [
        pltpu.make_async_copy(hbm, ref, sems.at[i])
        for i, (hbm, ref) in enumerate(
            (
                (geometry_hbm, geometry_ref),
                (disc_hbm, disc_ref),
                (thrust_hbm, thrust_ref),
                (factor_hbm, factor_ref),
            )
        )
    ]
    for copy in copies:
        copy.start()
    row_copies = []
    for ey in range(parts):
        for ex in range(elem_x):
            for b in range(nodes):
                row = ex * face + b * nodes
                row_copies.append(
                    pltpu.make_async_copy(
                        source_hbm.at[:, b, ex, ey, :],
                        held.at[ey, row : row + nodes, :],
                        row_sems.at[len(row_copies)],
                    )
                )
    for copy in row_copies:
        copy.start()
    code = jnp.int32(codes[0])
    for d in range(1, len(codes)):
        code = jnp.where(device_ref[0] == d, jnp.int32(codes[d]), code)
    levels = count_ref.shape[0]
    lane = lax.broadcasted_iota(jnp.int32, (1, lanes), 1)
    limit = jnp.zeros((1, lanes), jnp.int32)
    for l in range(levels):
        limit = jnp.where(lane // cols == l, count_ref[l], limit)
    live = jnp.where(lax.rem(lane, cols) < limit, 1.0, 0.0).astype(f32)
    for copy in copies:
        copy.wait()
    own_gx = jnp.full((1, lanes), device_ref[0] // gy_count, jnp.int32).astype(f32)
    own_gy = jnp.full((1, lanes), lax.rem(device_ref[0], gy_count), jnp.int32).astype(f32)
    blank_row = jnp.zeros((1, lanes), f32)
    push = disc_ref[...].astype(f32) * thrust_ref[...]
    ez_count = push.shape[2]
    blank = jnp.zeros((1, lanes - 2 * ez_count), f32)
    count = factor_ref.shape[0]
    span = factor_ref.shape[1] // (8 * parts)
    for ey in range(parts):
        pieces = [
            jnp.concatenate([geometry_ref[c, ex, ey : ey + 1] for ex in range(2)] + [blank], 1)
            for c in range(3)
        ]
        pieces.append(jnp.concatenate([push[ex, ey : ey + 1] for ex in range(2)] + [blank], 1))
        pieces += [live, own_gx, own_gy, blank_row]
        held[ey, nodes_rows : nodes_rows + 8] = jnp.concatenate(pieces, axis=0)
        for pair in range(4):
            at = [(2 * pair + k) * parts * span + ey * span for k in range(2)]
            base = nodes_rows + 8 + (pair // 2) * count
            column = (pair % 2) * 2 * span
            held[ey, base : base + count, column : column + 2 * span] = jnp.concatenate(
                [factor_ref[:, start : start + span] for start in at], axis=1
            )
    for copy in row_copies:
        copy.wait()
    outs = [
        pltpu.make_async_copy(held.at[field_of(code, 2 * q)], ref, sems.at[4 + q])
        for q, ref in enumerate((q0, q1, q2, q3))
    ]
    for copy in outs:
        copy.start()
    for copy in outs:
        copy.wait()


def sender_of(ref, count, row):
    at = ref.shape[0] - 2 * count - 8 + row
    return ref[at, 0].astype(jnp.int32)


def factor_block(ref, count, vu):
    base = ref.shape[0] - 2 * count + (vu // 2) * count
    return ref[base : base + count, (vu % 2) * 128 : (vu % 2) * 128 + 128]


def entry_kernel(ez_count, count, *refs):
    (q0, q1, q2, q3, columns_ref,
     w_ref, low_ref, high_ref, inv_ref, den_ref, live_ref, held) = refs
    rows = w_ref.shape[0] // 2
    face = rows // NODES
    lanes = 2 * w_ref.shape[1]
    parts = 4
    width = lanes // parts
    for q, ref in enumerate((q0, q1, q2, q3)):
        part = sender_of(ref, count, 5)
        held[part] = ref[: 2 * face + 8]
        live_ref[8 + q : 9 + q] = jnp.full((1, 128), part, jnp.int32).astype(f32)
    sizes = jnp.concatenate(
        [held[i, 2 * face : 2 * face + 8, :width] for i in range(parts)], axis=1
    )
    len_x, len_y, len_z, push = sizes[0:1], sizes[1:2], sizes[2:3], sizes[3:4]
    metric_x = len_y * len_z / (2.0 * len_x)
    metric_y = len_x * len_z / (2.0 * len_y)
    metric_z = len_x * len_y / (2.0 * len_z)
    volume = len_x * len_y * len_z / 8.0
    metrics = jnp.concatenate(
        [metric_x, metric_y, metric_z, jnp.zeros((13, lanes), f32)], axis=0
    )
    stiff = wide_dot(columns_ref[...], metrics)
    volumes = jnp.concatenate(
        [jnp.zeros((3, lanes), f32), volume, jnp.zeros((12, lanes), f32)], axis=0
    )
    mass = wide_dot(columns_ref[...], volumes)
    span = 2 * ez_count * NODES
    target = lax.broadcasted_iota(jnp.int32, (span, span), 1)
    origin = lax.rem(target, 2 * ez_count) * NODES + target // (2 * ez_count)
    deal = jnp.where(
        lax.broadcasted_iota(jnp.int32, (span, span), 0) == origin, 1.0, 0.0
    ).astype(bf16)
    den_ref[...] = stiff
    inv_ref[...] = 1.0 / (stiff + shift_ratio * (metric_x + metric_y + metric_z))
    for i in range(parts):
        live_ref[2 * i : 2 * i + 1] = held[i, 2 * face + 4 : 2 * face + 5, :128]
        live_ref[2 * i + 1 : 2 * i + 2] = held[i, 2 * face + 4 : 2 * face + 5, 128:256]
    raw = jnp.concatenate(
        [
            jnp.concatenate([held[i, :face], held[i, face : 2 * face]], axis=1)
            for i in range(parts)
        ],
        axis=0,
    )
    dealt = move_lanes(raw, deal)
    for c in range(NODES):
        for side in range(2):
            w_ref[pl.ds(side * rows + c, face, stride=NODES), :] = jnp.concatenate(
                [
                    dealt[i * face : (i + 1) * face, c * width : (c + 1) * width]
                    for i in (2 * side, 2 * side + 1)
                ],
                axis=1,
            )
    forcing = (lane_halves(w_ref) + push) * mass
    assemble_local(forcing, w_ref, low_ref, high_ref, ez_count, False)


def face_kernel(ez_count, average, scale, *refs):
    (below_ref, above_ref, own_low_ref, own_high_ref, scale_ref, forward_face_ref, backward_ref,
     low_ref, high_ref, modes_ref, work) = refs
    modes = faces_to_modes(
        scale * below_ref[...], scale * above_ref[...], forward_face_ref, scale_ref
    )
    modes_ref[...] = modes
    low, high = modes_to_faces(modes, backward_ref)
    field = jnp.concatenate([own_low_ref[...] + low, own_high_ref[...] + high], axis=0)
    sum_pairs(field, work, ez_count, average)
    store_faces(work, low_ref, high_ref)


def open_kernel(halve, *refs):
    (w_ref, forward_ref, backward_ref, scale_ref,
     base_ref, modes_ref, low_ref, high_ref) = refs
    base = lane_halves(w_ref)
    if halve:
        base = half_faces(base)
    base_ref[...] = base
    modes = to_modes(base, forward_ref, scale_ref)
    modes_ref[...] = modes
    low_ref[...], high_ref[...] = modes_to_faces(modes, backward_ref)


def rest_precond_kernel(ez_count, sign, keep, gain, *refs):
    refs = list(refs)
    below_ref, above_ref, base_ref, own_ref, more_ref = refs[:5]
    refs = refs[5:]
    old_ref = refs.pop(0) if keep != 0.0 else None
    (forward_ref, backward_ref, scale_ref,
     r_ref, step_ref, modes_ref, low_ref, high_ref, work) = refs
    r_ref[...] = with_faces(base_ref[...], below_ref, above_ref, sign)
    sum_pairs(from_modes(own_ref[...] + more_ref[...], backward_ref), work, ez_count, True)
    step = half_faces(lane_halves(work)) * gain
    if keep != 0.0:
        step = step + keep * old_ref[...]
    step_ref[...] = step
    modes = to_modes(step, forward_ref, scale_ref)
    modes_ref[...] = modes
    low_ref[...], high_ref[...] = modes_to_faces(modes, backward_ref)


def close_kernel(ez_count, keep, gain, *refs):
    own_ref, more_ref, old_ref, x_ref, backward_ref, total_ref, work = refs
    sum_pairs(from_modes(own_ref[...] + more_ref[...], backward_ref), work, ez_count, True)
    step = half_faces(lane_halves(work)) * gain + keep * old_ref[...]
    total_ref[...] = x_ref[...] + step


def rest_apply_kernel(ez_count, scale, start, keep_d, go_on, *refs):
    refs = list(refs)
    below_ref, above_ref, step_ref, own_ref, more_ref, r_ref = refs[:6]
    refs = refs[6:]
    x_in_ref = None if start else refs.pop(0)
    backward_ref = refs.pop(0)
    if go_on:
        forward_ref, scale_ref = refs[:2]
        refs = refs[2:]
    x_ref, base_ref = refs[:2]
    refs = refs[2:]
    step = with_faces(step_ref[...], below_ref, above_ref, scale)
    x_ref[...] = step if start else x_in_ref[...] + step
    if keep_d:
        refs.pop(0)[...] = step
    work = refs[-1]
    sum_pairs(from_modes(own_ref[...] + more_ref[...], backward_ref), work, ez_count, False)
    base = r_ref[...] - lane_halves(work)
    base_ref[...] = base
    if go_on:
        modes = to_modes(base, forward_ref, scale_ref)
        refs[0][...] = modes
        refs[1][...], refs[2][...] = modes_to_faces(modes, backward_ref)


def restrict_kernel(ez_count, count, *refs):
    (below_ref, above_ref, base_ref, restrict_ref, swaps_ref, x0, x1, x2, x3,
     r_ref, part_ref, coarse, sums) = refs
    lanes = base_ref.shape[1]
    parts = 4
    width = lanes // parts
    resid = with_faces(base_ref[...], below_ref, above_ref, -1.0)
    r_ref[...] = resid
    rows = wide_dot(restrict_ref[...], resid)
    b = rows[:8] + jnp.where(lane_layer((8, lanes), ez_count) == 0, rows[8:], 0.0)
    pairs = []
    for i in range(parts):
        pair = jnp.concatenate(
            [b[:4, i * width : (i + 1) * width], b[4:, i * width : (i + 1) * width]], axis=1
        )
        pairs += [pair, pair]
    swapped_rows = move_lanes(jnp.concatenate(pairs, axis=0), swaps_ref[: 2 * width])
    for i in range(parts):
        coarse[i] = swapped_rows[8 * i : 8 * (i + 1)]
    sums[...] = jnp.zeros_like(sums)
    block = 2 * width
    for q, ref in enumerate((x0, x1, x2, x3)):
        i = sender_of(ref, count, 5)
        mine = coarse[i]
        acc = factor_block(ref, count, 0) * mine[0:1]
        for vu in range(1, 4):
            acc = acc + factor_block(ref, count, vu) * mine[vu : vu + 1]
        sums[i, :count] = acc
    flat = sums[...].reshape(parts * sums.shape[1], block)
    ones = jnp.ones((8, block), bf16)
    high = flat.astype(bf16)
    low = (flat - high.astype(f32)).astype(bf16)
    across = lambda t: lax.dot_general(
        ones, t, (((1,), (1,)), ((), ())), preferred_element_type=f32
    )
    row = across(high) + across(low)
    tile = jnp.concatenate(
        [row[0:1, i * 128 : (i + 1) * 128] for i in range(2 * parts)], axis=0
    )
    part_ref[...] = jnp.broadcast_to(tile[None], part_ref.shape)


def prolong_kernel(ez_count, count, inner_levels, cols, groups, *refs):
    (all_ref, live_ref, swaps_ref, columns_ref, x0, x1, x2, x3,
     w_ref, low_ref, high_ref, table, coarse) = refs
    lanes = 2 * w_ref.shape[1]
    parts = 4
    width = lanes // parts
    block = 2 * width
    row_id = lax.broadcasted_iota(jnp.int32, all_ref.shape[1:], 0)
    lane_id = lax.broadcasted_iota(jnp.int32, all_ref.shape[1:], 1)
    level = (lax.rem(row_id, 2) * 128 + lane_id) // cols
    mine = lax.shift_right_logical(jnp.full_like(level, sender_of(x0, count, 6)), level)
    base = jnp.zeros(all_ref.shape[1:], f32)
    for source in range(all_ref.shape[0]):
        theirs = lax.shift_right_logical(jnp.full_like(level, groups[source]), level)
        base = base + jnp.where(theirs == mine, all_ref[source], 0.0)
    total = base
    step = 2
    for bit in range(2):
        flip = jnp.where(
            lax.rem(row_id // step, 2) == 0,
            pltpu.roll(total, 8 - step, 0),
            pltpu.roll(total, step, 0),
        )
        total = jnp.where(level > inner_levels + bit, total + flip, total)
        step *= 2
    total = total * live_ref[:8]
    turned = jnp.transpose(total)
    for i in range(parts):
        table[i, :128] = jnp.broadcast_to(turned[:, 2 * i : 2 * i + 1], (128, block))
        table[i, 128:] = jnp.broadcast_to(turned[:, 2 * i + 1 : 2 * i + 2], (128, block))
    for q, ref in enumerate((x0, x1, x2, x3)):
        i = sender_of(ref, count, 5)
        y = table[i, :count]
        for vu in range(4):
            coarse[i, vu : vu + 1] = jnp.sum(
                factor_block(ref, count, vu) * y, axis=0, keepdims=True
            )
    unswapped = move_lanes(coarse[...].reshape(parts * 8, block), swaps_ref[2 * width :])
    lows, highs = [], []
    for i in range(parts):
        pair = unswapped[8 * i : 8 * (i + 1)]
        lows.append(pair[:4, :width])
        highs.append(pair[:4, width:])
    e = jnp.concatenate([jnp.concatenate(lows, axis=1), jnp.concatenate(highs, axis=1)], axis=0)
    field = wide_dot(columns_ref[...], jnp.concatenate([jnp.zeros_like(e), e], axis=0))
    assemble_local(field, w_ref, low_ref, high_ref, ez_count, True)


def exit_kernel(scale, *refs):
    (place_ref, below_ref, above_ref, x_ref, inv_root_ref, gather_ref,
     q0, q1, q2, q3, field, held) = refs
    lanes = x_ref.shape[1]
    parts = 4
    width = lanes // parts
    face = below_ref.shape[0]
    rows = x_ref.shape[0]
    final = with_faces(x_ref[...], below_ref, above_ref, scale)
    store_halves(field, final * inv_root_ref[...])
    blocks = []
    for side in range(2):
        layers = [field[pl.ds(side * rows + c, face, stride=NODES), :] for c in range(NODES)]
        for i in range(2):
            blocks.append(
                jnp.concatenate([t[:, i * width : (i + 1) * width] for t in layers], axis=1)
            )
    dealt = move_lanes(jnp.concatenate(blocks, axis=0), gather_ref[...])
    half = dealt.shape[1] // 2
    for i in range(parts):
        held[i, 0] = dealt[i * face : (i + 1) * face, :half]
        held[i, 1] = dealt[i * face : (i + 1) * face, half:]
    for q, ref in enumerate((q0, q1, q2, q3)):
        ref[...] = held[place_ref[8 + q, 0].astype(jnp.int32)]


def call(kernel, name, out_shapes, args, scratch=()):
    return pl.pallas_call(
        kernel,
        name=name,
        out_shape=[jax.ShapeDtypeStruct(s, f32) for s in out_shapes],
        in_specs=[pl.BlockSpec(memory_space=VMEM)] * len(args),
        out_specs=[pl.BlockSpec(memory_space=VMEM)] * len(out_shapes),
        scratch_shapes=list(scratch),
        compiler_params=pltpu.CompilerParams(vmem_limit_bytes=12 * 1024 * 1024),
    )(*args)


def fast_device(source, geometry, disc_mask, thrust, xxt_factor, col_count):
    gx_count, gy_count = lax.axis_size("gx"), lax.axis_size("gy")
    axes = ("gx", "gy")
    nodes, _, elem_x, elem_y, z_count = source.shape
    ez_count = geometry.shape[3]
    levels, cols, _ = xxt_factor.shape
    parts = gx_count
    lanes = parts * elem_x * ez_count
    width = elem_x * ez_count
    rows = nodes**3
    face = nodes * nodes
    devices = gx_count * gy_count
    tables = {k: jnp.asarray(v) for k, v in constant_tables(ez_count, lanes).items()}
    ring, send, group, codes = placement(gx_count, gy_count)
    groups = [int(g) for g in group]
    device = lax.axis_index("gx") * gy_count + lax.axis_index("gy")
    up = [(ring[i], ring[(i + 1) % devices]) for i in range(devices)]
    down = [(target, origin) for origin, target in up]

    def spread(q):
        return [
            (i * gy_count + j, ring[parts * j + int(send[i * gy_count + j, q])])
            for i in range(gx_count)
            for j in range(gy_count)
        ]

    def halo(low, high):
        return lax.ppermute(high, axes, up), lax.ppermute(low, axes, down)

    count = levels * cols
    message = (elem_x * face + 8 + 2 * count, z_count)
    spec = lambda space: pl.BlockSpec(memory_space=space)
    packed = pl.pallas_call(
        functools.partial(pack_kernel, cols, gy_count, codes),
        name="pack",
        out_shape=[jax.ShapeDtypeStruct(message, f32)] * parts,
        in_specs=[spec(SMEM)] * 2 + [spec(pl.ANY)] * 5,
        out_specs=[spec(pl.ANY)] * parts,
        scratch_shapes=[
            VMEM((parts,) + message, f32),
            VMEM(geometry.shape, f32),
            VMEM(disc_mask.shape, jnp.int32),
            VMEM(thrust.shape, f32),
            VMEM((count, xxt_factor.shape[2]), f32),
            pltpu.SemaphoreType.DMA((2 * parts,)),
            pltpu.SemaphoreType.DMA((elem_y * elem_x * nodes,)),
        ],
        compiler_params=pltpu.CompilerParams(vmem_limit_bytes=67043328),
    )(
        jnp.reshape(device, (1,)), col_count.reshape(levels), source, geometry, disc_mask, thrust,
        xxt_factor.reshape(count, -1),
    )
    received = [lax.ppermute(packed[q], axes, spread(q)) for q in range(parts)]
    inner_levels = gy_count.bit_length() - 1

    fshape = (rows, lanes)
    sshape = (2 * rows, lanes // 2)
    hshape = (face, lanes)
    w, low, high, inv, den, live_tile = call(
        functools.partial(entry_kernel, ez_count, count), "entry",
        [sshape, hshape, hshape, fshape, fshape, (4 * parts, 128)],
        [*received, tables["columns"]],
        [VMEM((parts, 2 * face + 8, z_count), f32)],
    )
    fwd, bwd = tables["forward"], tables["backward"]
    fwd_face = tables["forward_face"]
    work = [VMEM(sshape, f32)]

    def faces(halos, own, average, scale, spectrum):
        low, high, modes = call(
            functools.partial(face_kernel, ez_count, average, scale), "face",
            [hshape, hshape, fshape], [*halos, *own, spectrum, fwd_face, bwd],
            [VMEM((4 * face, lanes // 2), f32)],
        )
        return halo(low, high), modes

    def opened(field, halve, spectrum):
        base, modes, *own = call(
            functools.partial(open_kernel, halve), "open", [fshape, fshape, hshape, hshape],
            [field, fwd, bwd, spectrum],
        )
        return base, modes, own

    def rest_precond(halos, base, modes, more, d, sign, keep, gain):
        resid, step, modes, *own = call(
            functools.partial(rest_precond_kernel, ez_count, sign, keep, gain), "rest_precond",
            [fshape, fshape, fshape, hshape, hshape],
            [*halos, base, modes, more] + ([] if keep == 0.0 else [d]) + [fwd, bwd, den], work,
        )
        return resid, step, modes, own

    def rest_apply(halos, step, modes, more, resid, x, scale, keep_d, go_on):
        out = call(
            functools.partial(rest_apply_kernel, ez_count, scale, x is None, keep_d, go_on),
            "rest_apply",
            [fshape] * (2 + keep_d + go_on) + [hshape] * (2 * go_on),
            [*halos, step, modes, more, resid] + ([] if x is None else [x]) + [bwd]
            + ([fwd, inv] if go_on else []),
            work,
        )
        x, base = out[:2]
        d = out[2] if keep_d else None
        modes, own = (out[2 + keep_d], out[3 + keep_d :]) if go_on else (None, None)
        return x, base, d, modes, own

    center = 0.5 * (bound_high + bound_low)
    radius = 0.5 * (bound_high - bound_low)
    ratio = center / radius
    rho_old = 1.0 / ratio
    rho_new = 1.0 / (2.0 * ratio - rho_old)
    first_gain = 1.0 / center
    keep = rho_new * rho_old
    gain = 2.0 * rho_new / radius

    x = None
    sign = 1.0
    halos = halo(low, high)
    base, modes, own = opened(w, False, inv)
    for cycle in range(CYCLES):
        for post in (False, True):
            ahead, more = faces(halos, own, True, sign, inv)
            resid, step, modes, own = rest_precond(
                halos, base, modes, more, None, sign, 0.0, first_gain
            )
            halos, more = faces(ahead, own, False, 0.5 * first_gain, den)
            x, base, d, modes, own = rest_apply(
                ahead, step, modes, more, resid, x, 0.5 * first_gain, True, True
            )
            sign = -1.0
            ahead, more = faces(halos, own, True, sign, inv)
            if post and cycle == CYCLES - 1:
                total = call(
                    functools.partial(close_kernel, ez_count, keep, gain), "close", [fshape],
                    [modes, more, d, x, bwd], work,
                )[0]
                halos = ahead
                break
            resid, step, modes, own = rest_precond(
                halos, base, modes, more, d, sign, keep, gain
            )
            halos, more = faces(ahead, own, False, 0.5 * gain, den)
            x, base, _, modes, own = rest_apply(
                ahead, step, modes, more, resid, x, 0.5 * gain, False, post
            )
            if post:
                break
            resid, partial = call(
                functools.partial(restrict_kernel, ez_count, count), "restrict",
                [fshape, (devices, 2 * parts, 128)],
                [*halos, base, tables["restrict"], tables["swaps"], *received],
                [VMEM((parts, 8, 2 * width), f32), VMEM((parts, 256, 2 * width), f32)],
            )
            everyone = lax.all_to_all(partial, axes, 0, 0)
            f, low, high = call(
                functools.partial(prolong_kernel, ez_count, count, inner_levels, cols, groups),
                "prolong", [sshape, hshape, hshape],
                [everyone, live_tile, tables["swaps"], tables["columns"], *received],
                [VMEM((parts, 256, 2 * width), f32), VMEM((parts, 8, 2 * width), f32)],
            )
            ahead = halo(low, high)
            step, modes, own = opened(f, True, den)
            halos, more = faces(ahead, own, False, 0.5, den)
            x, base, _, modes, own = rest_apply(
                ahead, step, modes, more, resid, x, 0.5, False, True
            )
    chunks = call(
        functools.partial(exit_kernel, 0.5 * gain), "exit",
        [(2, face, z_count)] * parts,
        [live_tile, *halos, total, tables["inv_root"], tables["gather"]],
        [VMEM(sshape, f32), VMEM((parts, 2, face, z_count), f32)],
    )
    back = [
        lax.ppermute(chunks[q], axes, [(t, s) for s, t in spread(q)]) for q in range(parts)
    ]
    code = jnp.int32(codes[0])
    for d in range(1, devices):
        code = jnp.where(device == d, jnp.int32(codes[d]), code)
    stacked = jnp.stack(back)
    by_ey = jnp.stack(
        [
            lax.dynamic_index_in_dim(stacked, field_of(code, 16 + 2 * ey), 0, keepdims=False)
            for ey in range(parts)
        ]
    )
    by_ey = by_ey.reshape(elem_y, elem_x, nodes, nodes, z_count)
    return by_ey.transpose(3, 2, 1, 0, 4)


def is_fast(mesh, source, geometry, xxt_factor):
    gx_count, gy_count = mesh.shape["gx"], mesh.shape["gy"]
    nodes, _, elem_x, elem_y, z_count = source.shape
    ez_count = geometry.shape[3]
    levels, cols, _ = xxt_factor.shape
    return (
        gx_count == 4 and elem_y == gx_count and gy_count % 4 == 0 and gy_count >= 8
        and gy_count & (gy_count - 1) == 0 and elem_x == 2 and nodes == NODES and z_count == 256
        and 2 * elem_x * ez_count == 128 and levels * cols <= 256
        and 4 * elem_x * ez_count == 256 and levels == (gx_count * gy_count).bit_length() and (levels * cols) % 8 == 0
    )


def solution(mesh):
    def body(source, geometry, disc_mask, thrust, xxt_factor, col_count):
        run = fast_device if is_fast(mesh, source, geometry, xxt_factor) else per_device
        return run(source, geometry, disc_mask, thrust, xxt_factor, col_count)

    return jax.shard_map(
        body,
        mesh=mesh,
        in_specs=(
            P(None, None, "gx", "gy", None),
            P(None, "gx", "gy", None),
            P("gx", "gy", None),
            P("gx", "gy", None),
            P(None, None, ("gx", "gy")),
            P(None, ("gx", "gy")),
        ),
        out_specs=P(None, None, "gx", "gy", None),
        check_vma=False,
    )
```

```python
import functools
import itertools
import math

import jax
import jax.numpy as jnp
import numpy as np
from jax import lax
from jax.experimental import pallas as pl
from jax.experimental.pallas import tpu as pltpu
from jax.sharding import PartitionSpec as P

NODES = 8
CYCLES = 2
CHEB_DEGREE = 2


highest = lax.Precision.HIGHEST
bound_low = 0.3
bound_high = 3.0
shift_ratio = 0.25


def padded(block, sides, width):
    for axis, dim in sides:
        count = lax.axis_size(axis)
        forward = [(i, i + 1) for i in range(count - 1)]
        forward.append((count - 1, 0))
        backward = [(target, source) for source, target in forward]
        low = lax.ppermute(
            lax.slice_in_dim(block, block.shape[dim] - width, None, axis=dim), axis, forward
        )
        high = lax.ppermute(lax.slice_in_dim(block, 0, width, axis=dim), axis, backward)
        block = jnp.concatenate([low, block, high], axis=dim)
    return block


def swapped(x, axis, bit):
    return lax.ppermute(x, axis, [(i, i ^ 1 << bit) for i in range(lax.axis_size(axis))])


def legendre_table(points, poly_order):
    table = [points * 0.0 + 1.0, points]
    for degree in range(2, poly_order + 1):
        table.append(
            ((2.0 * degree - 1.0) * points * table[-1] - (degree - 1.0) * table[-2]) / degree
        )
    return table


def jacobi_eigen(matrix):
    size_n = matrix.shape[0]
    current = matrix.copy()
    vectors = np.eye(size_n)
    for sweep_index in range(30):
        for first in range(size_n - 1):
            for second in range(first + 1, size_n):
                angle = 0.5 * math.atan2(
                    2.0 * float(current[first, second]),
                    float(current[second, second] - current[first, first]),
                )
                rotation = np.eye(size_n)
                rotation[first, first] = math.cos(angle)
                rotation[second, second] = math.cos(angle)
                rotation[first, second] = math.sin(angle)
                rotation[second, first] = -math.sin(angle)
                current = rotation.T @ current @ rotation
                vectors = vectors @ rotation
    values = np.array([current[index, index] for index in range(size_n)])
    order = np.argsort(values)
    return (values[order], vectors[:, order])


def gll_tables(node_count):
    poly_order = node_count - 1
    points = np.cos(np.pi * np.arange(node_count) / poly_order)
    for newton_index in range(200):
        table = legendre_table(points, poly_order)
        points = points - (points * table[poly_order] - table[poly_order - 1]) / (
            node_count * table[poly_order]
        )
    points = points[::-1].copy()
    legendre = legendre_table(points, poly_order)[poly_order]
    weights = 2.0 / (poly_order * (poly_order + 1) * legendre**2)
    identity = np.eye(node_count)
    gap_matrix = points[:, None] - points[None, :] + identity
    off_diagonal = legendre[:, None] / (legendre[None, :] * gap_matrix) * (1.0 - identity)
    end_value = poly_order * (poly_order + 1) / 4.0
    end_terms = np.concatenate([[-end_value], np.zeros(node_count - 2), [end_value]])
    derivative = off_diagonal + identity * end_terms[None, :]
    stiffness = derivative.T @ (weights[:, None] * derivative)
    root_inverse = 1.0 / np.sqrt(weights)
    symmetric = root_inverse[:, None] * stiffness * root_inverse[None, :]
    symmetric = 0.5 * (symmetric + symmetric.T)
    eigen_values, eigen_vectors = jacobi_eigen(symmetric)
    eigen_modes = root_inverse[:, None] * eigen_vectors
    vertex_interp = np.stack([(1.0 - points) / 2.0, (1.0 + points) / 2.0], axis=1)
    return (
        weights.astype(np.float32),
        stiffness.astype(np.float32),
        eigen_modes.astype(np.float32),
        eigen_values.astype(np.float32),
        vertex_interp.astype(np.float32),
    )


def build_setup(geometry):
    weights, stiffness, eigen_modes, eigen_values, vertex_interp = gll_tables(NODES)
    elem_z = geometry.shape[3]
    z_count = elem_z * NODES
    lengths = jnp.repeat(geometry, NODES, axis=3)
    len_x = lengths[0][None, None]
    len_y = lengths[1][None, None]
    len_z = lengths[2][None, None]
    metric_x = len_y * len_z / (2.0 * len_x)
    metric_y = len_x * len_z / (2.0 * len_y)
    metric_z = len_x * len_y / (2.0 * len_z)
    node_weight = jnp.asarray(weights)
    weight_a = node_weight[:, None, None, None, None]
    weight_b = node_weight[None, :, None, None, None]
    weight_c = jnp.tile(node_weight, elem_z)
    coef_x = metric_x * weight_b * weight_c
    coef_y = metric_y * weight_a * weight_c
    coef_z = metric_z * weight_a * weight_b
    mass_diag = len_x * len_y * len_z / 8.0 * weight_a * weight_b * weight_c
    spectrum = jnp.asarray(eigen_values)
    denominator = (
        metric_x * spectrum[:, None, None, None, None]
        + metric_y * spectrum[None, :, None, None, None]
        + metric_z * jnp.tile(spectrum, elem_z)
        + shift_ratio * (metric_x + metric_y + metric_z)
    )
    inv_denom = 1.0 / denominator
    z_index = jnp.arange(z_count)
    z_node = z_index % NODES
    dirichlet = (z_index < z_count - 1).astype(jnp.float32)
    node_index = jnp.arange(NODES)
    edge_node = ((node_index == 0) | (node_index == NODES - 1)).astype(jnp.float32) + 1.0
    z_shared = (
        1.0
        + ((z_node == 0) & (z_index > 0)).astype(jnp.float32)
        + ((z_node == NODES - 1) & (z_index < z_count - 1)).astype(jnp.float32)
    )
    inv_mult = 1.0 / (
        edge_node[:, None, None, None, None] * edge_node[None, :, None, None, None] * z_shared
    )
    eye_z = jnp.eye(elem_z, dtype=jnp.float32)
    stiff_matrix = jnp.asarray(stiffness)
    mode_matrix = jnp.asarray(eigen_modes)
    interp = jnp.asarray(vertex_interp)
    z_stiff = jnp.kron(eye_z, stiff_matrix.T)
    z_modes = jnp.kron(eye_z, mode_matrix)
    z_modes_t = jnp.kron(eye_z, mode_matrix.T)
    z_restrict = jnp.kron(eye_z, interp)
    z_prolong = jnp.kron(eye_z, interp.T)
    link_up = (z_index[None, :] == z_index[:, None] + 1) & (z_node[:, None] == NODES - 1)
    link_down = (z_index[None, :] == z_index[:, None] - 1) & (z_node[:, None] == 0)
    z_sum = ((z_index[:, None] == z_index[None, :]) | link_up | link_down).astype(jnp.float32)
    return (
        coef_x,
        coef_y,
        coef_z,
        mass_diag,
        inv_denom,
        dirichlet,
        inv_mult,
        stiff_matrix,
        mode_matrix,
        z_stiff,
        z_modes,
        z_modes_t,
        z_restrict,
        z_prolong,
        z_sum,
        interp,
    )


def pair_sum_x(data_field, prev_high, next_low):
    low_face = data_field[0]
    high_face = data_field[-1]
    before_faces = jnp.concatenate([prev_high[:, None], high_face[:, :-1]], axis=1)
    after_faces = jnp.concatenate([low_face[:, 1:], next_low[:, None]], axis=1)
    return jnp.concatenate(
        [(low_face + before_faces)[None], data_field[1:-1], (high_face + after_faces)[None]], axis=0
    )


def pair_sum_y(data_field, prev_high, next_low):
    low_face = data_field[:, 0]
    high_face = data_field[:, -1]
    before_faces = jnp.concatenate([prev_high[:, :, None], high_face[:, :, :-1]], axis=2)
    after_faces = jnp.concatenate([low_face[:, :, 1:], next_low[:, :, None]], axis=2)
    return jnp.concatenate(
        [
            (low_face + before_faces)[:, None],
            data_field[:, 1:-1],
            (high_face + after_faces)[:, None],
        ],
        axis=1,
    )


def corner_slot(line_values, node_count):
    padding = jnp.zeros((node_count - 1, line_values.shape[0]), jnp.float32)
    return jnp.concatenate([line_values[None], padding], axis=0)


def summed_neighbour_face(raw_face, prev_line, next_line):
    node_count, elem_x, z_count = raw_face.shape
    shaped = raw_face.reshape(node_count, 1, elem_x, 1, z_count)
    summed = pair_sum_x(shaped, prev_line[None, None], next_line[None, None])
    return summed.reshape(node_count, elem_x, z_count)


def assemble(data_field, z_sum):
    node_count = data_field.shape[0]
    elem_x = data_field.shape[2]
    elem_y = data_field.shape[3]
    z_count = data_field.shape[4]
    frame = jnp.zeros((elem_x + 2, elem_y + 2, node_count, z_count), jnp.float32)
    frame = frame.at[0, 1 : elem_y + 1].set(jnp.transpose(data_field[0][:, 0], (1, 0, 2)))
    frame = frame.at[elem_x + 1, 1 : elem_y + 1].set(
        jnp.transpose(data_field[-1][:, -1], (1, 0, 2))
    )
    frame = frame.at[1 : elem_x + 1, 0].set(jnp.transpose(data_field[:, 0][:, :, 0], (1, 0, 2)))
    frame = frame.at[1 : elem_x + 1, elem_y + 1].set(
        jnp.transpose(data_field[:, -1][:, :, -1], (1, 0, 2))
    )
    frame = frame.at[0, 0].set(corner_slot(data_field[0, 0, 0, 0], node_count))
    frame = frame.at[0, elem_y + 1].set(corner_slot(data_field[0, -1, 0, -1], node_count))
    frame = frame.at[elem_x + 1, 0].set(corner_slot(data_field[-1, 0, -1, 0], node_count))
    frame = frame.at[elem_x + 1, elem_y + 1].set(
        corner_slot(data_field[-1, -1, -1, -1], node_count)
    )
    bordered = padded(frame, (("gx", 0), ("gy", 1)), 1)
    last_x = elem_x + 3
    last_y = elem_y + 3
    left_high = jnp.transpose(bordered[0, 2 : elem_y + 2], (1, 0, 2))
    right_low = jnp.transpose(bordered[last_x, 2 : elem_y + 2], (1, 0, 2))
    down_raw = jnp.transpose(bordered[2 : elem_x + 2, 0], (1, 0, 2))
    up_raw = jnp.transpose(bordered[2 : elem_x + 2, last_y], (1, 0, 2))
    down_high = summed_neighbour_face(down_raw, bordered[0, 0][0], bordered[last_x, 0][0])
    up_low = summed_neighbour_face(up_raw, bordered[0, last_y][0], bordered[last_x, last_y][0])
    data_field = pair_sum_x(data_field, left_high, right_low)
    data_field = pair_sum_y(data_field, down_high, up_low)
    return jnp.matmul(data_field, z_sum, precision=highest)


def chebyshev(solution, resid, apply_op, precond, keep_resid):
    center = 0.5 * (bound_high + bound_low)
    radius = 0.5 * (bound_high - bound_low)
    center_ratio = center / radius
    rho_old = 1.0 / center_ratio
    direction = precond(resid) / center
    for step_index in range(CHEB_DEGREE):
        solution = solution + direction
        if step_index < CHEB_DEGREE - 1 or keep_resid:
            resid = resid - apply_op(direction)
        if step_index < CHEB_DEGREE - 1:
            rho_new = 1.0 / (2.0 * center_ratio - rho_old)
            direction = rho_new * rho_old * direction + 2.0 * rho_new / radius * precond(resid)
            rho_old = rho_new
    return (solution, resid)


def pressure_solve(source, disc_mask, thrust, setup_tables, assembler, coarse_solve):
    (
        coef_x,
        coef_y,
        coef_z,
        mass_diag,
        inv_denom,
        dirichlet,
        inv_mult,
        stiff_matrix,
        mode_matrix,
        z_stiff,
        z_modes,
        z_modes_t,
        z_restrict,
        z_prolong,
        z_sum,
        interp,
    ) = setup_tables

    def apply_op(data_field):
        along_x = jnp.einsum("ac,cbxyz->abxyz", stiff_matrix, data_field, precision=highest)
        along_y = jnp.einsum("bc,acxyz->abxyz", stiff_matrix, data_field, precision=highest)
        along_z = jnp.matmul(data_field, z_stiff, precision=highest)
        return dirichlet * assembler(coef_x * along_x + coef_y * along_y + coef_z * along_z, z_sum)

    def precond(resid):
        spectral = jnp.einsum("ai,abxyz->ibxyz", mode_matrix, resid, precision=highest)
        spectral = jnp.einsum("bj,abxyz->ajxyz", mode_matrix, spectral, precision=highest)
        spectral = jnp.matmul(spectral, z_modes, precision=highest) * inv_denom
        spectral = jnp.einsum("ai,ibxyz->abxyz", mode_matrix, spectral, precision=highest)
        spectral = jnp.einsum("bj,ajxyz->abxyz", mode_matrix, spectral, precision=highest)
        return (
            dirichlet
            * inv_mult
            * assembler(jnp.matmul(spectral, z_modes_t, precision=highest), z_sum)
        )

    forcing = source + jnp.repeat(disc_mask.astype(jnp.float32) * thrust, NODES, axis=2)[None, None]
    rhs_field = dirichlet * assembler(mass_diag * forcing, z_sum)
    solution = jnp.zeros_like(rhs_field)
    for sweep_index in range(CYCLES):
        if sweep_index == 0:
            resid = rhs_field
        else:
            resid = rhs_field - apply_op(solution)
        solution, resid = chebyshev(solution, resid, apply_op, precond, True)
        restrict_coarse = jnp.einsum("av,abxyz->vbxyz", interp, inv_mult * resid, precision=highest)
        restrict_coarse = jnp.einsum("bu,vbxyz->vuxyz", interp, restrict_coarse, precision=highest)
        correction = coarse_solve(jnp.matmul(restrict_coarse, z_restrict, precision=highest))
        fine_field = jnp.einsum("av,vuxyz->auxyz", interp, correction, precision=highest)
        fine_field = jnp.einsum("bu,auxyz->abxyz", interp, fine_field, precision=highest)
        solution = solution + dirichlet * inv_mult * assembler(
            jnp.matmul(fine_field, z_prolong, precision=highest), z_sum
        )
        resid = rhs_field - apply_op(solution)
        solution, resid = chebyshev(solution, resid, apply_op, precond, False)
    return solution


def per_device(source, geometry, disc_mask, thrust, xxt_factor, col_count):
    setup_tables = build_setup(geometry)

    def coarse_solve(coarse):
        flattened = coarse.reshape(-1)
        partial_value = jnp.einsum("lkn,n->lk", xxt_factor, flattened, precision=highest)
        live_mask = (jnp.arange(xxt_factor.shape[1])[None, :] < col_count).astype(jnp.float32)
        partial_value = partial_value * live_mask
        bit_count = (lax.axis_size("gx") * lax.axis_size("gy")).bit_length() - 1
        for bit_index in range(bit_count):
            upper_levels = partial_value[bit_index + 1 :]
            partner = swapped(upper_levels, ("gx", "gy"), bit_index)
            partial_value = jnp.concatenate(
                [partial_value[: bit_index + 1], upper_levels + partner], axis=0
            )
        return jnp.einsum("lkn,lk->n", xxt_factor, partial_value, precision=highest).reshape(
            coarse.shape
        )

    return pressure_solve(source, disc_mask, thrust, setup_tables, assemble, coarse_solve)


VMEM = pltpu.VMEM
SMEM = pltpu.SMEM
f32 = jnp.float32
bf16 = jnp.bfloat16


@functools.lru_cache(maxsize=None)
def placement(gx_count, gy_count):
    layers = gy_count // 2
    a, b, c, d = (0, 0), (0, 1), (1, 1), (1, 0)
    chips = [(d, 0), (a, 0), (b, 0), (c, 0)]
    for z in range(1, layers - 1):
        chips += [(column, z) for column in ((c, b, a) if z % 2 else (a, b, c))]
    chips += [(column, layers - 1) for column in (c, b, a, d)]
    chips += [(d, z) for z in range(layers - 2, 0, -1)]
    count = len(chips)

    def moved(turn):
        return sum(abs(chips[(i + turn) % count][1] - i // gx_count) for i in range(count))

    turn = min(range(count), key=moved)
    chips = chips[turn:] + chips[:turn]
    spots = [(column, z, core) for column, z in chips for core in (0, 1)]
    ring = [(y * 2 + x) * gy_count + 2 * z + core for (y, x), z, core in spots]

    def hops(i, j, place):
        (y, x), z, _ = spots[place]
        return abs(i // 2 - y) + abs(i % 2 - x) + abs(j // 2 - z)

    orders = list(itertools.permutations(range(gx_count)))
    squares = [
        rows
        for rows in itertools.product(orders, repeat=gx_count)
        if all(len(set(column)) == gx_count for column in zip(*rows))
    ]
    send = np.zeros((gx_count * gy_count, gx_count), np.int32)
    part = np.zeros((gx_count * gy_count, gx_count), np.int32)
    group = np.zeros(gx_count * gy_count, np.int32)
    for j in range(gy_count):
        far = [[hops(i, j, gx_count * j + s) for s in range(gx_count)] for i in range(gx_count)]
        cost = lambda rows: [max(far[i][row[i]] for i in range(gx_count)) for row in rows]
        best = min(squares, key=lambda rows: (sum(cost(rows)), cost(rows)[::-1]))
        for q, row in enumerate(best):
            for i in range(gx_count):
                send[i * gy_count + j, q] = row[i]
                part[ring[gx_count * j + row[i]], q] = i
        for s in range(gx_count):
            group[ring[gx_count * j + s]] = j
    codes = group.astype(np.int64) << 24
    for q in range(gx_count):
        codes |= (send[:, q] << 2 * q) | (part[:, q] << 8 + 2 * q)
        codes |= np.argsort(send, axis=1)[:, q] << 16 + 2 * q
    return ring, send, group, [int(c) for c in codes]


def field_of(code, at):
    return lax.shift_right_logical(code, jnp.int32(at)) & 3


def split_bf16(values):
    high = values.astype(np.float32).astype(bf16)
    low = (values - high.astype(np.float64)).astype(np.float32).astype(bf16)
    return high, low


def wide(matrix):
    high, low = split_bf16(matrix)
    return np.concatenate([high, high, low], axis=1)


@functools.lru_cache(maxsize=None)
def constant_tables(ez_count, lanes):
    weights, _, modes, values, interp = [
        np.asarray(t, np.float64) for t in gll_tables(NODES)
    ]
    half = NODES // 2
    root = np.sqrt(weights)
    basis = root[:, None] * modes
    parity = np.sign(np.sum(basis * basis[::-1], axis=0))
    basis = 0.5 * (basis + parity * basis[::-1])
    even = [i for i in range(NODES) if parity[i] > 0]
    odd = [i for i in range(NODES) if parity[i] < 0]
    blocks = []
    for picked in (even, odd):
        blocks.append(np.kron(basis[:half, picked].T, np.kron(basis.T, basis.T)))
    forward = np.stack([wide(m) for m in blocks])
    backward = np.stack([wide(m.T) for m in blocks])
    face = NODES * NODES
    forward_face = np.stack([wide(m[:, :face]) for m in blocks])
    order_b = even + odd
    one = np.ones(NODES)
    lam_a = np.kron(one, np.kron(values, one))
    lam_b = np.kron(values[order_b], np.kron(one, one))
    lam_c = np.kron(one, np.kron(one, values))
    root3 = np.kron(root, np.kron(root, root))
    spectrum = np.stack([lam_a, lam_b, lam_c, root3] + [0 * lam_a] * 4, axis=1)
    edge = np.where((np.arange(NODES) == 0) | (np.arange(NODES) == NODES - 1), 0.5, 1.0)
    jw = interp * root[:, None] * edge[:, None]
    first = np.zeros_like(jw)
    first[0] = jw[0]
    def rows_of(jc):
        return np.stack(
            [
                np.kron(jw[:, u], np.kron(jw[:, v], jc[:, t]))
                for t in (0, 1) for v in (0, 1) for u in (0, 1)
            ]
        )
    restrict = np.concatenate([rows_of(jw), rows_of(first)], axis=0)
    jp = interp * root[:, None]
    prolong = np.stack(
        [
            np.kron(jp[:, u], np.kron(jp[:, v], jp[:, t]))
            for t in (0, 1) for v in (0, 1) for u in (0, 1)
        ],
        axis=1,
    )
    swap = np.zeros((4 * ez_count, 4 * ez_count))
    for t in range(2):
        for ex in range(2):
            for ez in range(ez_count):
                swap[(t * 2 + ex) * ez_count + ez, ex * 2 * ez_count + 2 * ez + t] = 1.0
    span = 2 * ez_count * NODES
    deal = np.zeros((span, span))
    for ex in range(2):
        for ez in range(ez_count):
            for c in range(NODES):
                deal[(ex * ez_count + ez) * NODES + c, (c * 2 + ex) * ez_count + ez] = 1.0
    as32 = lambda t: np.asarray(t, np.float32)
    return dict(
        forward=forward,
        forward_face=forward_face,
        backward=backward,
        columns=wide(np.concatenate([spectrum, prolong], axis=1)),
        inv_root=as32(1.0 / root3[:, None]),
        restrict=wide(restrict),
        swaps=np.concatenate([swap, swap.T], axis=0).astype(bf16),
        gather=deal.T.astype(bf16),
    )


def hp_dot(a, b):
    return jnp.dot(a, b, precision=highest, preferred_element_type=f32)


def move_lanes(field, table):
    rows = field.shape[0]
    high = field.astype(bf16)
    rest = field - high.astype(f32)
    middle = rest.astype(bf16)
    low = (rest - middle.astype(f32)).astype(bf16)
    moved = jnp.dot(
        jnp.concatenate([high, middle, low], axis=0), table, preferred_element_type=f32
    )
    return moved[:rows] + moved[rows : 2 * rows] + moved[2 * rows :]


def wide_dot(table, field):
    high = field.astype(bf16)
    low = (field - high.astype(f32)).astype(bf16)
    stacked = jnp.concatenate([high, low, high], axis=0)
    return jnp.dot(table, stacked, preferred_element_type=f32)


def to_modes(field, forward_ref, scale_ref):
    face = field.shape[0] // NODES
    half = field.shape[0] // 2
    top = field[:half]
    bottom = jnp.concatenate(
        [field[(NODES - 1 - b) * face : (NODES - b) * face] for b in range(NODES // 2)], axis=0
    )
    even = wide_dot(forward_ref[0], top + bottom) * scale_ref[:half]
    odd = wide_dot(forward_ref[1], top - bottom) * scale_ref[half:]
    return jnp.concatenate([even, odd], axis=0)


def from_modes(modes, backward_ref):
    half = modes.shape[0] // 2
    face = modes.shape[0] // NODES
    even = wide_dot(backward_ref[0], modes[:half])
    odd = wide_dot(backward_ref[1], modes[half:])
    diff = even - odd
    parts = [diff[b * face : (b + 1) * face] for b in reversed(range(NODES // 2))]
    return jnp.concatenate([even + odd] + parts, axis=0)


def faces_to_modes(low, high, forward_face_ref, scale_ref):
    half = scale_ref.shape[0] // 2
    even = wide_dot(forward_face_ref[0], low + high) * scale_ref[:half]
    odd = wide_dot(forward_face_ref[1], low - high) * scale_ref[half:]
    return jnp.concatenate([even, odd], axis=0)


def modes_to_faces(modes, backward_ref):
    half = modes.shape[0] // 2
    face = modes.shape[0] // NODES
    even = wide_dot(backward_ref[0, :face], modes[:half])
    odd = wide_dot(backward_ref[1, :face], modes[half:])
    return even + odd, even - odd


def lane_layer(shape, ez_count):
    return lax.rem(lax.broadcasted_iota(jnp.int32, shape, 1), ez_count)


def lane_halves(ref):
    rows = ref.shape[0] // 2
    return jnp.concatenate([ref[:rows], ref[rows:]], axis=1)


def store_halves(ref, field):
    rows = field.shape[0]
    ref[:rows] = field[:, :128]
    ref[rows:] = field[:, 128:]


def sum_pairs(field, work_ref, ez_count, average):
    rows, lanes = field.shape
    face = NODES * NODES
    tile = NODES
    count = rows // face
    f4 = field.reshape(count, NODES, tile, lanes)
    a_low = f4[:, 0].reshape(count * tile, lanes)
    a_high = f4[:, NODES - 1].reshape(count * tile, lanes)
    new_low = a_low + pltpu.roll(a_high, ez_count, 1)
    new_high = a_high + pltpu.roll(a_low, lanes - ez_count, 1)
    if average:
        new_low = 0.5 * new_low
        new_high = 0.5 * new_high
    store_halves(work_ref, field)
    spots = rows // NODES
    layer = lane_layer((spots, 128), ez_count)
    for side in range(2):
        base = side * rows
        span = slice(side * 128, (side + 1) * 128)
        for b in range(count):
            at = base + b * face
            work_ref[at : at + tile] = new_low[b * tile : (b + 1) * tile, span]
            work_ref[at + face - tile : at + face] = new_high[b * tile : (b + 1) * tile, span]
        c_low = work_ref[pl.ds(base, spots, stride=NODES), :]
        c_high = work_ref[pl.ds(base + NODES - 1, spots, stride=NODES), :]
        above = c_low + pltpu.roll(c_high, 1, 1)
        below = c_high + pltpu.roll(c_low, 127, 1)
        if average:
            above = 0.5 * above
            below = 0.5 * below
        work_ref[pl.ds(base, spots, stride=NODES), :] = jnp.where(layer > 0, above, c_low)
        work_ref[pl.ds(base + NODES - 1, spots, stride=NODES), :] = jnp.where(
            layer < ez_count - 1, below, 0.0
        )


def store_faces(work_ref, low_ref, high_ref):
    face = low_ref.shape[0]
    rows = work_ref.shape[0] // 2
    for side in range(2):
        span = slice(side * 128, (side + 1) * 128)
        low_ref[:, span] = work_ref[side * rows : side * rows + face]
        high_ref[:, span] = work_ref[(side + 1) * rows - face : (side + 1) * rows]


def assemble_local(field, out_ref, low_ref, high_ref, ez_count, average):
    sum_pairs(field, out_ref, ez_count, average)
    store_faces(out_ref, low_ref, high_ref)


def with_faces(field, below_ref, above_ref, scale):
    face = below_ref.shape[0]
    rows = field.shape[0]
    return jnp.concatenate(
        [
            field[:face] + scale * below_ref[...],
            field[face : rows - face],
            field[rows - face :] + scale * above_ref[...],
        ],
        axis=0,
    )


def half_faces(field):
    face = NODES * NODES
    rows = field.shape[0]
    return jnp.concatenate(
        [0.5 * field[:face], field[face : rows - face], 0.5 * field[rows - face :]], axis=0
    )


def pack_kernel(cols, gy_count, codes, *refs):
    (device_ref, count_ref, source_hbm, geometry_hbm, disc_hbm, thrust_hbm, factor_hbm,
     q0, q1, q2, q3,
     held, geometry_ref, disc_ref, thrust_ref, factor_ref, sems, row_sems) = refs
    parts = 4
    _, nodes, elem_x, _, lanes = source_hbm.shape
    face = nodes * nodes
    nodes_rows = elem_x * face
    copies = [
        pltpu.make_async_copy(hbm, ref, sems.at[i])
        for i, (hbm, ref) in enumerate(
            (
                (geometry_hbm, geometry_ref),
                (disc_hbm, disc_ref),
                (thrust_hbm, thrust_ref),
                (factor_hbm, factor_ref),
            )
        )
    ]
    for copy in copies:
        copy.start()
    row_copies = []
    for ey in range(parts):
        for ex in range(elem_x):
            for b in range(nodes):
                row = ex * face + b * nodes
                row_copies.append(
                    pltpu.make_async_copy(
                        source_hbm.at[:, b, ex, ey, :],
                        held.at[ey, row : row + nodes, :],
                        row_sems.at[len(row_copies)],
                    )
                )
    for copy in row_copies:
        copy.start()
    code = jnp.int32(codes[0])
    for d in range(1, len(codes)):
        code = jnp.where(device_ref[0] == d, jnp.int32(codes[d]), code)
    levels = count_ref.shape[0]
    lane = lax.broadcasted_iota(jnp.int32, (1, lanes), 1)
    limit = jnp.zeros((1, lanes), jnp.int32)
    for l in range(levels):
        limit = jnp.where(lane // cols == l, count_ref[l], limit)
    live = jnp.where(lax.rem(lane, cols) < limit, 1.0, 0.0).astype(f32)
    for copy in copies:
        copy.wait()
    own_gx = jnp.full((1, lanes), device_ref[0] // gy_count, jnp.int32).astype(f32)
    own_gy = jnp.full((1, lanes), lax.rem(device_ref[0], gy_count), jnp.int32).astype(f32)
    blank_row = jnp.zeros((1, lanes), f32)
    push = disc_ref[...].astype(f32) * thrust_ref[...]
    ez_count = push.shape[2]
    blank = jnp.zeros((1, lanes - 2 * ez_count), f32)
    count = factor_ref.shape[0]
    span = factor_ref.shape[1] // (8 * parts)
    for ey in range(parts):
        pieces = [
            jnp.concatenate([geometry_ref[c, ex, ey : ey + 1] for ex in range(2)] + [blank], 1)
            for c in range(3)
        ]
        pieces.append(jnp.concatenate([push[ex, ey : ey + 1] for ex in range(2)] + [blank], 1))
        pieces += [live, own_gx, own_gy, blank_row]
        held[ey, nodes_rows : nodes_rows + 8] = jnp.concatenate(pieces, axis=0)
        for pair in range(4):
            at = [(2 * pair + k) * parts * span + ey * span for k in range(2)]
            base = nodes_rows + 8 + (pair // 2) * count
            column = (pair % 2) * 2 * span
            held[ey, base : base + count, column : column + 2 * span] = jnp.concatenate(
                [factor_ref[:, start : start + span] for start in at], axis=1
            )
    for copy in row_copies:
        copy.wait()
    outs = [
        pltpu.make_async_copy(held.at[field_of(code, 2 * q)], ref, sems.at[4 + q])
        for q, ref in enumerate((q0, q1, q2, q3))
    ]
    for copy in outs:
        copy.start()
    for copy in outs:
        copy.wait()


def sender_of(ref, count, row):
    at = ref.shape[0] - 2 * count - 8 + row
    return ref[at, 0].astype(jnp.int32)


def factor_block(ref, count, vu):
    base = ref.shape[0] - 2 * count + (vu // 2) * count
    return ref[base : base + count, (vu % 2) * 128 : (vu % 2) * 128 + 128]


def entry_kernel(ez_count, count, *refs):
    (q0, q1, q2, q3, columns_ref,
     w_ref, low_ref, high_ref, inv_ref, den_ref, live_ref, held) = refs
    rows = w_ref.shape[0] // 2
    face = rows // NODES
    lanes = 2 * w_ref.shape[1]
    parts = 4
    width = lanes // parts
    for q, ref in enumerate((q0, q1, q2, q3)):
        part = sender_of(ref, count, 5)
        held[part] = ref[: 2 * face + 8]
        live_ref[8 + q : 9 + q] = jnp.full((1, 128), part, jnp.int32).astype(f32)
    sizes = jnp.concatenate(
        [held[i, 2 * face : 2 * face + 8, :width] for i in range(parts)], axis=1
    )
    len_x, len_y, len_z, push = sizes[0:1], sizes[1:2], sizes[2:3], sizes[3:4]
    metric_x = len_y * len_z / (2.0 * len_x)
    metric_y = len_x * len_z / (2.0 * len_y)
    metric_z = len_x * len_y / (2.0 * len_z)
    volume = len_x * len_y * len_z / 8.0
    metrics = jnp.concatenate(
        [metric_x, metric_y, metric_z, jnp.zeros((13, lanes), f32)], axis=0
    )
    stiff = wide_dot(columns_ref[...], metrics)
    volumes = jnp.concatenate(
        [jnp.zeros((3, lanes), f32), volume, jnp.zeros((12, lanes), f32)], axis=0
    )
    mass = wide_dot(columns_ref[...], volumes)
    span = 2 * ez_count * NODES
    target = lax.broadcasted_iota(jnp.int32, (span, span), 1)
    origin = lax.rem(target, 2 * ez_count) * NODES + target // (2 * ez_count)
    deal = jnp.where(
        lax.broadcasted_iota(jnp.int32, (span, span), 0) == origin, 1.0, 0.0
    ).astype(bf16)
    den_ref[...] = stiff
    inv_ref[...] = 1.0 / (stiff + shift_ratio * (metric_x + metric_y + metric_z))
    for i in range(parts):
        live_ref[2 * i : 2 * i + 1] = held[i, 2 * face + 4 : 2 * face + 5, :128]
        live_ref[2 * i + 1 : 2 * i + 2] = held[i, 2 * face + 4 : 2 * face + 5, 128:256]
    raw = jnp.concatenate(
        [
            jnp.concatenate([held[i, :face], held[i, face : 2 * face]], axis=1)
            for i in range(parts)
        ],
        axis=0,
    )
    dealt = move_lanes(raw, deal)
    for c in range(NODES):
        for side in range(2):
            w_ref[pl.ds(side * rows + c, face, stride=NODES), :] = jnp.concatenate(
                [
                    dealt[i * face : (i + 1) * face, c * width : (c + 1) * width]
                    for i in (2 * side, 2 * side + 1)
                ],
                axis=1,
            )
    forcing = (lane_halves(w_ref) + push) * mass
    assemble_local(forcing, w_ref, low_ref, high_ref, ez_count, False)


def face_kernel(ez_count, average, scale, *refs):
    (below_ref, above_ref, own_low_ref, own_high_ref, scale_ref, forward_face_ref, backward_ref,
     low_ref, high_ref, modes_ref, work) = refs
    modes = faces_to_modes(
        scale * below_ref[...], scale * above_ref[...], forward_face_ref, scale_ref
    )
    modes_ref[...] = modes
    low, high = modes_to_faces(modes, backward_ref)
    field = jnp.concatenate([own_low_ref[...] + low, own_high_ref[...] + high], axis=0)
    sum_pairs(field, work, ez_count, average)
    store_faces(work, low_ref, high_ref)


def open_kernel(halve, *refs):
    (w_ref, forward_ref, backward_ref, scale_ref,
     base_ref, modes_ref, low_ref, high_ref) = refs
    base = lane_halves(w_ref)
    if halve:
        base = half_faces(base)
    base_ref[...] = base
    modes = to_modes(base, forward_ref, scale_ref)
    modes_ref[...] = modes
    low_ref[...], high_ref[...] = modes_to_faces(modes, backward_ref)


def rest_precond_kernel(ez_count, sign, keep, gain, *refs):
    refs = list(refs)
    below_ref, above_ref, base_ref, own_ref, more_ref = refs[:5]
    refs = refs[5:]
    old_ref = refs.pop(0) if keep != 0.0 else None
    (forward_ref, backward_ref, scale_ref,
     r_ref, step_ref, modes_ref, low_ref, high_ref, work) = refs
    r_ref[...] = with_faces(base_ref[...], below_ref, above_ref, sign)
    sum_pairs(from_modes(own_ref[...] + more_ref[...], backward_ref), work, ez_count, True)
    step = half_faces(lane_halves(work)) * gain
    if keep != 0.0:
        step = step + keep * old_ref[...]
    step_ref[...] = step
    modes = to_modes(step, forward_ref, scale_ref)
    modes_ref[...] = modes
    low_ref[...], high_ref[...] = modes_to_faces(modes, backward_ref)


def close_kernel(ez_count, keep, gain, *refs):
    own_ref, more_ref, old_ref, x_ref, backward_ref, total_ref, work = refs
    sum_pairs(from_modes(own_ref[...] + more_ref[...], backward_ref), work, ez_count, True)
    step = half_faces(lane_halves(work)) * gain + keep * old_ref[...]
    total_ref[...] = x_ref[...] + step


def rest_apply_kernel(ez_count, scale, start, keep_d, go_on, *refs):
    refs = list(refs)
    below_ref, above_ref, step_ref, own_ref, more_ref, r_ref = refs[:6]
    refs = refs[6:]
    x_in_ref = None if start else refs.pop(0)
    backward_ref = refs.pop(0)
    if go_on:
        forward_ref, scale_ref = refs[:2]
        refs = refs[2:]
    x_ref, base_ref = refs[:2]
    refs = refs[2:]
    step = with_faces(step_ref[...], below_ref, above_ref, scale)
    x_ref[...] = step if start else x_in_ref[...] + step
    if keep_d:
        refs.pop(0)[...] = step
    work = refs[-1]
    sum_pairs(from_modes(own_ref[...] + more_ref[...], backward_ref), work, ez_count, False)
    base = r_ref[...] - lane_halves(work)
    base_ref[...] = base
    if go_on:
        modes = to_modes(base, forward_ref, scale_ref)
        refs[0][...] = modes
        refs[1][...], refs[2][...] = modes_to_faces(modes, backward_ref)


def restrict_kernel(ez_count, count, *refs):
    (below_ref, above_ref, base_ref, restrict_ref, swaps_ref, x0, x1, x2, x3,
     r_ref, part_ref, coarse, sums) = refs
    lanes = base_ref.shape[1]
    parts = 4
    width = lanes // parts
    resid = with_faces(base_ref[...], below_ref, above_ref, -1.0)
    r_ref[...] = resid
    rows = wide_dot(restrict_ref[...], resid)
    b = rows[:8] + jnp.where(lane_layer((8, lanes), ez_count) == 0, rows[8:], 0.0)
    pairs = []
    for i in range(parts):
        pair = jnp.concatenate(
            [b[:4, i * width : (i + 1) * width], b[4:, i * width : (i + 1) * width]], axis=1
        )
        pairs += [pair, pair]
    swapped_rows = move_lanes(jnp.concatenate(pairs, axis=0), swaps_ref[: 2 * width])
    for i in range(parts):
        coarse[i] = swapped_rows[8 * i : 8 * (i + 1)]
    sums[...] = jnp.zeros_like(sums)
    block = 2 * width
    for q, ref in enumerate((x0, x1, x2, x3)):
        i = sender_of(ref, count, 5)
        mine = coarse[i]
        acc = factor_block(ref, count, 0) * mine[0:1]
        for vu in range(1, 4):
            acc = acc + factor_block(ref, count, vu) * mine[vu : vu + 1]
        sums[i, :count] = acc
    flat = sums[...].reshape(parts * sums.shape[1], block)
    ones = jnp.ones((8, block), bf16)
    high = flat.astype(bf16)
    low = (flat - high.astype(f32)).astype(bf16)
    across = lambda t: lax.dot_general(
        ones, t, (((1,), (1,)), ((), ())), preferred_element_type=f32
    )
    row = across(high) + across(low)
    tile = jnp.concatenate(
        [row[0:1, i * 128 : (i + 1) * 128] for i in range(2 * parts)], axis=0
    )
    part_ref[...] = jnp.broadcast_to(tile[None], part_ref.shape)


def prolong_kernel(ez_count, count, inner_levels, cols, groups, *refs):
    (all_ref, live_ref, swaps_ref, columns_ref, x0, x1, x2, x3,
     w_ref, low_ref, high_ref, table, coarse) = refs
    lanes = 2 * w_ref.shape[1]
    parts = 4
    width = lanes // parts
    block = 2 * width
    row_id = lax.broadcasted_iota(jnp.int32, all_ref.shape[1:], 0)
    lane_id = lax.broadcasted_iota(jnp.int32, all_ref.shape[1:], 1)
    level = (lax.rem(row_id, 2) * 128 + lane_id) // cols
    mine = lax.shift_right_logical(jnp.full_like(level, sender_of(x0, count, 6)), level)
    base = jnp.zeros(all_ref.shape[1:], f32)
    for source in range(all_ref.shape[0]):
        theirs = lax.shift_right_logical(jnp.full_like(level, groups[source]), level)
        base = base + jnp.where(theirs == mine, all_ref[source], 0.0)
    total = base
    step = 2
    for bit in range(2):
        flip = jnp.where(
            lax.rem(row_id // step, 2) == 0,
            pltpu.roll(total, 8 - step, 0),
            pltpu.roll(total, step, 0),
        )
        total = jnp.where(level > inner_levels + bit, total + flip, total)
        step *= 2
    total = total * live_ref[:8]
    turned = jnp.transpose(total)
    for i in range(parts):
        table[i, :128] = jnp.broadcast_to(turned[:, 2 * i : 2 * i + 1], (128, block))
        table[i, 128:] = jnp.broadcast_to(turned[:, 2 * i + 1 : 2 * i + 2], (128, block))
    for q, ref in enumerate((x0, x1, x2, x3)):
        i = sender_of(ref, count, 5)
        y = table[i, :count]
        for vu in range(4):
            coarse[i, vu : vu + 1] = jnp.sum(
                factor_block(ref, count, vu) * y, axis=0, keepdims=True
            )
    unswapped = move_lanes(coarse[...].reshape(parts * 8, block), swaps_ref[2 * width :])
    lows, highs = [], []
    for i in range(parts):
        pair = unswapped[8 * i : 8 * (i + 1)]
        lows.append(pair[:4, :width])
        highs.append(pair[:4, width:])
    e = jnp.concatenate([jnp.concatenate(lows, axis=1), jnp.concatenate(highs, axis=1)], axis=0)
    field = wide_dot(columns_ref[...], jnp.concatenate([jnp.zeros_like(e), e], axis=0))
    assemble_local(field, w_ref, low_ref, high_ref, ez_count, True)


def exit_kernel(scale, *refs):
    (place_ref, below_ref, above_ref, x_ref, inv_root_ref, gather_ref,
     q0, q1, q2, q3, field, held) = refs
    lanes = x_ref.shape[1]
    parts = 4
    width = lanes // parts
    face = below_ref.shape[0]
    rows = x_ref.shape[0]
    final = with_faces(x_ref[...], below_ref, above_ref, scale)
    store_halves(field, final * inv_root_ref[...])
    blocks = []
    for side in range(2):
        layers = [field[pl.ds(side * rows + c, face, stride=NODES), :] for c in range(NODES)]
        for i in range(2):
            blocks.append(
                jnp.concatenate([t[:, i * width : (i + 1) * width] for t in layers], axis=1)
            )
    dealt = move_lanes(jnp.concatenate(blocks, axis=0), gather_ref[...])
    half = dealt.shape[1] // 2
    for i in range(parts):
        held[i, 0] = dealt[i * face : (i + 1) * face, :half]
        held[i, 1] = dealt[i * face : (i + 1) * face, half:]
    for q, ref in enumerate((q0, q1, q2, q3)):
        ref[...] = held[place_ref[8 + q, 0].astype(jnp.int32)]


def call(kernel, name, out_shapes, args, scratch=()):
    return pl.pallas_call(
        kernel,
        name=name,
        out_shape=[jax.ShapeDtypeStruct(s, f32) for s in out_shapes],
        in_specs=[pl.BlockSpec(memory_space=VMEM)] * len(args),
        out_specs=[pl.BlockSpec(memory_space=VMEM)] * len(out_shapes),
        scratch_shapes=list(scratch),
        compiler_params=pltpu.CompilerParams(vmem_limit_bytes=12 * 1024 * 1024),
    )(*args)


def fast_device(source, geometry, disc_mask, thrust, xxt_factor, col_count):
    gx_count, gy_count = lax.axis_size("gx"), lax.axis_size("gy")
    axes = ("gx", "gy")
    nodes, _, elem_x, elem_y, z_count = source.shape
    ez_count = geometry.shape[3]
    levels, cols, _ = xxt_factor.shape
    parts = gx_count
    lanes = parts * elem_x * ez_count
    width = elem_x * ez_count
    rows = nodes**3
    face = nodes * nodes
    devices = gx_count * gy_count
    tables = {k: jnp.asarray(v) for k, v in constant_tables(ez_count, lanes).items()}
    ring, send, group, codes = placement(gx_count, gy_count)
    groups = [int(g) for g in group]
    device = lax.axis_index("gx") * gy_count + lax.axis_index("gy")
    up = [(ring[i], ring[(i + 1) % devices]) for i in range(devices)]
    down = [(target, origin) for origin, target in up]

    def spread(q):
        return [
            (i * gy_count + j, ring[parts * j + int(send[i * gy_count + j, q])])
            for i in range(gx_count)
            for j in range(gy_count)
        ]

    def halo(low, high):
        return lax.ppermute(high, axes, up), lax.ppermute(low, axes, down)

    count = levels * cols
    message = (elem_x * face + 8 + 2 * count, z_count)
    spec = lambda space: pl.BlockSpec(memory_space=space)
    packed = pl.pallas_call(
        functools.partial(pack_kernel, cols, gy_count, codes),
        name="pack",
        out_shape=[jax.ShapeDtypeStruct(message, f32)] * parts,
        in_specs=[spec(SMEM)] * 2 + [spec(pl.ANY)] * 5,
        out_specs=[spec(pl.ANY)] * parts,
        scratch_shapes=[
            VMEM((parts,) + message, f32),
            VMEM(geometry.shape, f32),
            VMEM(disc_mask.shape, jnp.int32),
            VMEM(thrust.shape, f32),
            VMEM((count, xxt_factor.shape[2]), f32),
            pltpu.SemaphoreType.DMA((2 * parts,)),
            pltpu.SemaphoreType.DMA((elem_y * elem_x * nodes,)),
        ],
        compiler_params=pltpu.CompilerParams(vmem_limit_bytes=67043328),
    )(
        jnp.reshape(device, (1,)), col_count.reshape(levels), source, geometry, disc_mask, thrust,
        xxt_factor.reshape(count, -1),
    )
    received = [lax.ppermute(packed[q], axes, spread(q)) for q in range(parts)]
    inner_levels = gy_count.bit_length() - 1

    fshape = (rows, lanes)
    sshape = (2 * rows, lanes // 2)
    hshape = (face, lanes)
    w, low, high, inv, den, live_tile = call(
        functools.partial(entry_kernel, ez_count, count), "entry",
        [sshape, hshape, hshape, fshape, fshape, (4 * parts, 128)],
        [*received, tables["columns"]],
        [VMEM((parts, 2 * face + 8, z_count), f32)],
    )
    fwd, bwd = tables["forward"], tables["backward"]
    fwd_face = tables["forward_face"]
    work = [VMEM(sshape, f32)]

    def faces(halos, own, average, scale, spectrum):
        low, high, modes = call(
            functools.partial(face_kernel, ez_count, average, scale), "face",
            [hshape, hshape, fshape], [*halos, *own, spectrum, fwd_face, bwd],
            [VMEM((4 * face, lanes // 2), f32)],
        )
        return halo(low, high), modes

    def opened(field, halve, spectrum):
        base, modes, *own = call(
            functools.partial(open_kernel, halve), "open", [fshape, fshape, hshape, hshape],
            [field, fwd, bwd, spectrum],
        )
        return base, modes, own

    def rest_precond(halos, base, modes, more, d, sign, keep, gain):
        resid, step, modes, *own = call(
            functools.partial(rest_precond_kernel, ez_count, sign, keep, gain), "rest_precond",
            [fshape, fshape, fshape, hshape, hshape],
            [*halos, base, modes, more] + ([] if keep == 0.0 else [d]) + [fwd, bwd, den], work,
        )
        return resid, step, modes, own

    def rest_apply(halos, step, modes, more, resid, x, scale, keep_d, go_on):
        out = call(
            functools.partial(rest_apply_kernel, ez_count, scale, x is None, keep_d, go_on),
            "rest_apply",
            [fshape] * (2 + keep_d + go_on) + [hshape] * (2 * go_on),
            [*halos, step, modes, more, resid] + ([] if x is None else [x]) + [bwd]
            + ([fwd, inv] if go_on else []),
            work,
        )
        x, base = out[:2]
        d = out[2] if keep_d else None
        modes, own = (out[2 + keep_d], out[3 + keep_d :]) if go_on else (None, None)
        return x, base, d, modes, own

    center = 0.5 * (bound_high + bound_low)
    radius = 0.5 * (bound_high - bound_low)
    ratio = center / radius
    rho_old = 1.0 / ratio
    rho_new = 1.0 / (2.0 * ratio - rho_old)
    first_gain = 1.0 / center
    keep = rho_new * rho_old
    gain = 2.0 * rho_new / radius

    x = None
    sign = 1.0
    halos = halo(low, high)
    base, modes, own = opened(w, False, inv)
    for cycle in range(CYCLES):
        for post in (False, True):
            ahead, more = faces(halos, own, True, sign, inv)
            resid, step, modes, own = rest_precond(
                halos, base, modes, more, None, sign, 0.0, first_gain
            )
            halos, more = faces(ahead, own, False, 0.5 * first_gain, den)
            x, base, d, modes, own = rest_apply(
                ahead, step, modes, more, resid, x, 0.5 * first_gain, True, True
            )
            sign = -1.0
            ahead, more = faces(halos, own, True, sign, inv)
            if post and cycle == CYCLES - 1:
                total = call(
                    functools.partial(close_kernel, ez_count, keep, gain), "close", [fshape],
                    [modes, more, d, x, bwd], work,
                )[0]
                halos = ahead
                break
            resid, step, modes, own = rest_precond(
                halos, base, modes, more, d, sign, keep, gain
            )
            halos, more = faces(ahead, own, False, 0.5 * gain, den)
            x, base, _, modes, own = rest_apply(
                ahead, step, modes, more, resid, x, 0.5 * gain, False, post
            )
            if post:
                break
            resid, partial = call(
                functools.partial(restrict_kernel, ez_count, count), "restrict",
                [fshape, (devices, 2 * parts, 128)],
                [*halos, base, tables["restrict"], tables["swaps"], *received],
                [VMEM((parts, 8, 2 * width), f32), VMEM((parts, 256, 2 * width), f32)],
            )
            everyone = lax.all_to_all(partial, axes, 0, 0)
            f, low, high = call(
                functools.partial(prolong_kernel, ez_count, count, inner_levels, cols, groups),
                "prolong", [sshape, hshape, hshape],
                [everyone, live_tile, tables["swaps"], tables["columns"], *received],
                [VMEM((parts, 256, 2 * width), f32), VMEM((parts, 8, 2 * width), f32)],
            )
            ahead = halo(low, high)
            step, modes, own = opened(f, True, den)
            halos, more = faces(ahead, own, False, 0.5, den)
            x, base, _, modes, own = rest_apply(
                ahead, step, modes, more, resid, x, 0.5, False, True
            )
    chunks = call(
        functools.partial(exit_kernel, 0.5 * gain), "exit",
        [(2, face, z_count)] * parts,
        [live_tile, *halos, total, tables["inv_root"], tables["gather"]],
        [VMEM(sshape, f32), VMEM((parts, 2, face, z_count), f32)],
    )
    back = [
        lax.ppermute(chunks[q], axes, [(t, s) for s, t in spread(q)]) for q in range(parts)
    ]
    code = jnp.int32(codes[0])
    for d in range(1, devices):
        code = jnp.where(device == d, jnp.int32(codes[d]), code)
    stacked = jnp.stack(back)
    by_ey = jnp.stack(
        [
            lax.dynamic_index_in_dim(stacked, field_of(code, 16 + 2 * ey), 0, keepdims=False)
            for ey in range(parts)
        ]
    )
    by_ey = by_ey.reshape(elem_y, elem_x, nodes, nodes, z_count)
    return by_ey.transpose(3, 2, 1, 0, 4)


def is_fast(mesh, source, geometry, xxt_factor):
    gx_count, gy_count = mesh.shape["gx"], mesh.shape["gy"]
    nodes, _, elem_x, elem_y, z_count = source.shape
    ez_count = geometry.shape[3]
    levels, cols, _ = xxt_factor.shape
    return (
        gx_count == 4 and elem_y == gx_count and gy_count % 4 == 0 and gy_count >= 8
        and gy_count & (gy_count - 1) == 0 and elem_x == 2 and nodes == NODES and z_count == 256
        and 2 * elem_x * ez_count == 128 and levels * cols <= 256
        and 4 * elem_x * ez_count == 256 and levels == (gx_count * gy_count).bit_length() and (levels * cols) % 8 == 0
    )


def solution(mesh):
    def body(source, geometry, disc_mask, thrust, xxt_factor, col_count):
        run = fast_device if is_fast(mesh, source, geometry, xxt_factor) else per_device
        return run(source, geometry, disc_mask, thrust, xxt_factor, col_count)

    return jax.shard_map(
        body,
        mesh=mesh,
        in_specs=(
            P(None, None, "gx", "gy", None),
            P(None, "gx", "gy", None),
            P("gx", "gy", None),
            P("gx", "gy", None),
            P(None, None, ("gx", "gy")),
            P(None, ("gx", "gy")),
        ),
        out_specs=P(None, None, "gx", "gy", None),
        check_vma=False,
    )
```
